32 devices in a mesh: group: 2 (over y), batch: 4 (over z), mp: 2 (over x), section: 2 (over core).
Axes of the slice: x: 2, y: 2, z: 4, core: 2. Of those that a mesh axis runs over, the one named last changes fastest.
Arguments:
- queries: bfloat16 [2, 192, 8192], P('section', ('group', 'batch'), 'mp'), parts along dimension 1, may hold values from -6 to 6
- new_keys: bfloat16 [2, 192, 1024], P('section', ('group', 'batch'), 'mp'), parts along dimension 1, may hold values from -6 to 6
- new_values: bfloat16 [2, 192, 1024], P('section', ('group', 'batch'), 'mp'), parts along dimension 1, may hold values from -6 to 6
- key_pages: bfloat16 [2, 768, 16, 1024], P('section', ('group', 'batch'), None, 'mp'), parts along dimension 1, may hold values from -6 to 6
- value_pages: bfloat16 [2, 768, 16, 1024], P('section', ('group', 'batch'), None, 'mp'), parts along dimension 1, may hold values from -6 to 6
- page_table: int32 [192, 4], P(('group', 'batch')), parts along dimension 0, may hold values from 0 to 95, as said below
- ancestry: int32 [192], P('group'), parts along dimension 0, may hold values from 0 to 95, as said below
- lengths: int32 [192], P('group'), parts along dimension 0, may hold values from 1 to 64, as said below
- step_rows: bfloat16 [8192, 4096], P(('group', 'batch', 'section'), 'mp'), parts along dimension 0, may hold values from -6 to 6
- norm_gain: float32 [4096], replicated, may hold values from 0.1 to 1.9
- head_weight: bfloat16 [4096, 4096], P(('batch', 'section'), 'mp'), may hold values from -0.09375 to 0.09375
- head_bias: float32 [4096], P('mp'), may hold values from -5 to 5
- class_weight: bfloat16 [4096, 2], P('mp'), may hold values from -0.125 to 0.125
- class_bias: float32 [2], replicated, may hold values from -4 to 4
Outputs:
- attention: bfloat16 [2, 192, 8192], P('section', ('group', 'batch'), 'mp'), parts along dimension 1
- log_odds: float32 [8192], P(('group', 'batch', 'section')), parts along dimension 0
The draws below stay inside these ranges and needn't reach their ends.
There are 2 independent parts, one for each index of `group`. The reference program is written for one: setup_inputs(seed, part) draws one part's arguments, and reference() takes and returns one part's arrays. A program takes and returns all parts, laid end to end along the dimension named above; an argument that names none is the same for every part. Nothing has to cross between parts.
Inputs may be any that keep to these rules, and one draw needn't show every extreme that they name: The pages of the particles on one index of batch lie on that index; the page_table rows of those 24 particles name each of its 96 pages exactly once. Particle j belongs to problem j % 24, and ancestry[j] % 24 == j % 24. Particles j // 24 == d stand on index d of batch; the 24 slots on one index take at most 12 ancestors from any one index, and in every draw some index gives exactly 12 ancestors to the slots of every index. `lengths`: some particle has all 64 positions live in every draw.
All inputs are finite; a program needn't handle non-finite values.
Results may differ from the reference program's by a relative error of at most 0.0043.
Values may be sent and summed in bfloat16 or wider, within the bound.
A program may use at most 64 MiB of HBM per device.

```python
import jax
import jax.numpy as jnp
from jax import lax

QH = 64
KVH = 8
HD = 128
VD = 4096
PAGE = 16
CTX = 64
LAYERS = 2
P_DEV = 24
CAP = 12
PAGES = 4
PARTICLES = 96
POOL = 384
VROWS = 4096


def draw_queries(key, part):
    shape = (LAYERS, PARTICLES, QH, HD)
    base = jnp.clip(jax.random.normal(key, shape, jnp.float32), -6.0, 6.0)
    return base.reshape(LAYERS, PARTICLES, QH * HD).astype(jnp.bfloat16)


def draw_key_pages(key, part):
    shape = (LAYERS, POOL, PAGE, KVH, HD)
    base = jnp.clip(jax.random.normal(key, shape, jnp.float32), -6.0, 6.0)
    return base.reshape(LAYERS, POOL, PAGE, KVH * HD).astype(jnp.bfloat16)


def draw_page_table(key, part):
    device_count = PARTICLES // P_DEV
    per_device = P_DEV * PAGES
    priority = jax.random.randint(key, (device_count, per_device), 0, 65536) * per_device + jnp.arange(per_device)[None, :]
    ordering = jnp.argsort(priority, axis=1)
    return ordering.reshape(PARTICLES, PAGES).astype(jnp.int32)


def draw_ancestry(key, part):
    device_count = PARTICLES // P_DEV
    key_star = jax.random.fold_in(key, 11)
    key_bias = jax.random.fold_in(key, 12)
    noise_random_key = jax.random.fold_in(key, 13)
    key_shuffle = jax.random.fold_in(key, 14)
    star = jax.random.randint(key_star, (), 0, device_count)
    device_bias = jax.random.randint(key_bias, (device_count,), 0, 8)
    noise = jax.random.randint(noise_random_key, (device_count, device_count), 0, 65536)
    device_ids = jnp.arange(device_count)
    priority = (device_bias[None, :] * 65536 + noise) * device_count + device_ids[None, :]
    priority = priority + jnp.where(device_ids == star, 1 << 29, 0)[None, :]
    priority = priority + jnp.where(device_ids[None, :] == device_ids[:, None], 1 << 28, 0)
    ordering = jnp.argsort(-priority, axis=1)
    chosen = ordering[:, jnp.arange(P_DEV) // CAP]
    shuffle_scores = jax.random.randint(key_shuffle, (device_count, P_DEV), 0, 65536) * P_DEV + jnp.arange(P_DEV)[None, :]
    shuffle = jnp.argsort(shuffle_scores, axis=1)
    source = jnp.take_along_axis(chosen, shuffle, axis=1)
    home_position = jnp.argmax((source == device_ids[:, None]).astype(jnp.int32), axis=1)
    last_source = source[:, P_DEV - 1]
    source = source.at[device_ids, home_position].set(last_source)
    source = source.at[:, P_DEV - 1].set(device_ids)
    return (source * P_DEV + jnp.arange(P_DEV)[None, :]).reshape(PARTICLES).astype(jnp.int32)


def draw_lengths(key, part):
    key_values = jax.random.fold_in(key, 21)
    key_longest = jax.random.fold_in(key, 22)
    values = jax.random.randint(key_values, (PARTICLES,), 1, CTX + 1)
    longest = jax.random.randint(key_longest, (), 0, PARTICLES)
    return jnp.where(jnp.arange(PARTICLES) == longest, CTX, values).astype(jnp.int32)


def steps_of(key, shape, shards, least, top_value):
    def one(axis_at, shards_of):
        heights = jax.random.uniform(jax.random.fold_in(jax.random.fold_in(key, 6), axis_at), (shards_of,), jnp.float32, least / len(shards), top_value / len(shards))
        return jnp.repeat(jnp.exp(heights), shape[axis_at] // shards_of).reshape((-1,) + (1,) * (len(shape) - axis_at - 1))

    gain = one(*shards[0])
    for cut in shards[1:]:
        gain = gain * one(*cut)
    return gain


def gaussian(stream_key, extent, spread, limit, shards=(), held_as=jnp.bfloat16):
    values = spread * jax.random.normal(stream_key, extent, jnp.float32)
    if shards:
        values = values * steps_of(stream_key, extent, shards, -0.22, 0.18)
    return jnp.clip(values, -limit, limit).astype(held_as)


def setup_inputs(seed: int = 0, part: int = 0) -> dict:
    key_list = jax.random.split(jax.random.key(seed), 15)
    part_splits = jax.random.split(jax.random.fold_in(key_list[14], part), 15)
    queries = draw_queries(jax.random.fold_in(jax.random.fold_in(key_list[14], part), 71), part)
    new_keys = gaussian(part_splits[1], (LAYERS, PARTICLES, KVH * HD), 1.0, 6.0, ((0, 2), (1, 4), (2, 2)))
    new_values = gaussian(part_splits[2], (LAYERS, PARTICLES, KVH * HD), 1.0, 6.0, ((0, 2), (1, 4), (2, 2)))
    key_pages = draw_key_pages(jax.random.fold_in(jax.random.fold_in(key_list[14], part), 71), part)
    value_pages = gaussian(part_splits[4], (LAYERS, POOL, PAGE, KVH * HD), 1.0, 6.0, ((0, 2), (1, 4), (3, 2)))
    page_table = draw_page_table(jax.random.fold_in(jax.random.fold_in(key_list[14], part), 71), part)
    ancestry = draw_ancestry(jax.random.fold_in(jax.random.fold_in(key_list[14], part), 71), part)
    lengths = draw_lengths(jax.random.fold_in(jax.random.fold_in(key_list[14], part), 71), part)
    step_rows = gaussian(part_splits[8], (VROWS, VD), 1.0, 6.0, ((0, 8), (1, 2)))
    norm_gain = jnp.clip(1.0 + 0.18 * jax.random.normal(key_list[9], (VD,), jnp.float32), 0.1, 1.9)
    head_weight = gaussian(key_list[10], (VD, VD), VD ** -0.5, 0.09375, ((0, 8), (1, 2)))
    head_bias = gaussian(key_list[11], (VD,), 1.0, 5.0, ((0, 2),), jnp.float32)
    class_weight = gaussian(key_list[12], (VD, 2), (VD // 2) ** -0.5, 0.125, ((0, 2),))
    class_bias = gaussian(key_list[13], (2,), 1.0, 4.0, (), jnp.float32)
    return {"queries": queries, "new_keys": new_keys, "new_values": new_values, "key_pages": key_pages, "value_pages": value_pages, "page_table": page_table, "ancestry": ancestry, "lengths": lengths, "step_rows": step_rows, "norm_gain": norm_gain, "head_weight": head_weight, "head_bias": head_bias, "class_weight": class_weight, "class_bias": class_bias}


def reference(queries, new_keys, new_values, key_pages, value_pages, page_table, ancestry, lengths, step_rows, norm_gain, head_weight, head_bias, class_weight, class_bias):
    score_scale = 1.0 / HD ** 0.5
    group_size = QH // KVH
    owner = ancestry // P_DEV
    pool_pages = page_table[ancestry] + (owner * (P_DEV * PAGES))[:, None]
    live_mask = jnp.arange(CTX)[None, :] < lengths[ancestry][:, None]

    def one_layer(layer_args):
        query_per_layer, layer_keys, layer_values, layer_key_pages, layer_value_pages = layer_args
        query_head_count = query_per_layer.reshape(PARTICLES, KVH, group_size, HD).astype(jnp.float32)
        cached_key_rows = layer_key_pages[pool_pages].reshape(PARTICLES, CTX, KVH, HD).astype(jnp.float32)
        cache_values = layer_value_pages[pool_pages].reshape(PARTICLES, CTX, KVH, HD).astype(jnp.float32)
        attention_scores = jnp.einsum('pkgd,ptkd->pkgt', query_head_count, cached_key_rows) * score_scale
        attention_scores = jnp.where(live_mask[:, None, None, :], attention_scores, -1e+30)
        top_score = lax.optimization_barrier(jnp.max(attention_scores, axis=-1))
        weights = jnp.exp(attention_scores - top_score[..., None])
        rounded = lax.optimization_barrier(weights.astype(jnp.bfloat16)).astype(jnp.float32)
        numerator = jnp.einsum('pkgt,ptkd->pkgd', rounded, cache_values)
        particle_key_rows = layer_keys.reshape(PARTICLES, KVH, HD).astype(jnp.float32)
        own_values = layer_values.reshape(PARTICLES, KVH, HD).astype(jnp.float32)
        own_score = jnp.einsum('pkgd,pkd->pkg', query_head_count, particle_key_rows) * score_scale
        own_weight = jnp.exp(own_score - top_score)
        denominator = lax.optimization_barrier(jnp.sum(weights, axis=-1)) + own_weight
        result = (numerator + own_weight[..., None] * own_values[:, :, None, :]) / denominator[..., None]
        return result.reshape(PARTICLES, QH * HD).astype(jnp.bfloat16)
    attention = lax.map(one_layer, (queries, new_keys, new_values, key_pages, value_pages))
    row_values = step_rows.astype(jnp.float32)
    power = lax.optimization_barrier(jnp.mean(row_values * row_values, axis=1, keepdims=True))
    normed = (row_values * lax.rsqrt(power + 1e-06) * norm_gain).astype(jnp.bfloat16)
    hidden = jnp.maximum(jnp.dot(normed, head_weight, preferred_element_type=jnp.float32) + head_bias, 0.0).astype(jnp.bfloat16)
    logits = jnp.dot(hidden, class_weight, preferred_element_type=jnp.float32) + class_bias
    log_odds = logits[:, 1] - logits[:, 0]
    return (attention, log_odds)
```

```python
import functools

import jax
import jax.numpy as jnp
from jax import lax
from jax.experimental import pallas as pl
from jax.experimental.pallas import tpu as pltpu
from jax.sharding import PartitionSpec as P

HD = 128
MESH = pl.DeviceIdType.MESH


def fused_kernel(
    dims,
    ancestry_ref,
    lengths_ref,
    pages_ref,
    class_bias_ref,
    queries_hbm,
    new_keys_hbm,
    new_values_hbm,
    keys_hbm,
    values_hbm,
    rows_hbm,
    gain_hbm,
    weight_hbm,
    bias_hbm,
    class_ref,
    attention_ref,
    odds_ref,
    follow,
    chosen,
    letter_rows,
    key_rows_in,
    value_rows_in,
    gain_ref,
    bias_ref,
    picker,
    mail_out,
    mail_in,
    served_out,
    returned,
    keys,
    values,
    raw,
    normed,
    weights,
    total,
    partial,
    logits_in,
    local_sem,
    weight_sem,
    mail_send,
    mail_recv,
    back_send,
    back_recv,
    line_send,
    line_recv,
    twin_send,
    twin_recv,
    swap_send,
    swap_recv,
    row_send,
    row_recv,
    norm_send,
    norm_recv,
    sum_send,
    sum_recv,
):
    nb, mp, ns = dims["nb"], dims["mp"], dims["ns"]
    cap, page_count, kvl, group = dims["cap"], dims["page_count"], dims["kvl"], dims["group"]
    half, chunk, chunks, depth = dims["half"], dims["chunk"], dims["chunks"], dims["depth"]
    row_chunks, cuts, first = dims["row_chunks"], dims["cuts"], dims["first"]
    slots, wide_slots = dims["slots"], dims["wide_slots"]
    heads = kvl * group
    sub = depth // cuts
    parts = chunks * cuts
    z, y = lax.axis_index("batch"), lax.axis_index("group")
    x, c = lax.axis_index("mp"), lax.axis_index("section")
    other = 1 - c
    twin = 1 - y
    cross = lax.rem(c + y, 2)
    row_count, row_width = rows_hbm.shape
    per_chunk = row_count // row_chunks

    def remote(src, dst, send, recv, device):
        return pltpu.make_async_remote_copy(
            src_ref=src, dst_ref=dst, send_sem=send, recv_sem=recv, device_id=device, device_id_type=MESH
        )

    def columns(owner, n):
        return pl.ds(pl.multiple_of(owner * half + n * chunk, chunk), chunk)

    barrier = pltpu.get_barrier_semaphore()

    def greet(device):
        pl.semaphore_signal(barrier, inc=1, device_id=device, device_id_type=MESH)

    for d in range(1, nb):
        greet({"batch": lax.rem(z + d, nb)})

    @pl.when(z > 0)
    def _():
        greet({"batch": z - 1, "section": other})

    @pl.when(z < nb - 1)
    def _():
        greet({"batch": z + 1, "section": other})

    greet({"section": other})
    greet({"group": twin})
    for d in range(1, mp):
        peer = lax.rem(x + d, mp)
        greet({"mp": peer})
        greet({"mp": peer, "section": other})

    own_copies = [
        pltpu.make_async_copy(queries_hbm.at[0], letter_rows, local_sem.at[0]),
        pltpu.make_async_copy(new_keys_hbm.at[0], key_rows_in, local_sem.at[1]),
        pltpu.make_async_copy(new_values_hbm.at[0], value_rows_in, local_sem.at[2]),
        pltpu.make_async_copy(keys_hbm.at[0], keys, local_sem.at[3]),
        pltpu.make_async_copy(values_hbm.at[0], values, local_sem.at[4]),
        pltpu.make_async_copy(gain_hbm, gain_ref, local_sem.at[5]),
        pltpu.make_async_copy(bias_hbm, bias_ref, local_sem.at[6]),
        pltpu.make_async_copy(rows_hbm, raw.at[x], local_sem.at[7]),
    ]
    for copy in own_copies:
        copy.start()

    neighbours = jnp.where(z > 0, 1, 0) + jnp.where(z < nb - 1, 1, 0)
    pl.semaphore_wait(barrier, (nb - 1) + 2 + 2 * (mp - 1) + neighbours)

    def mail(d):
        target = lax.rem(z + d, nb)
        return remote(mail_out.at[target], mail_in.at[z], mail_send.at[d], mail_recv.at[d], {"batch": target})

    def back(d):
        target = lax.rem(z + d, nb)
        return remote(
            served_out.at[target], returned.at[z], back_send.at[d], back_recv.at[d], {"batch": target}
        )

    def row_copy(d, i):
        target = lax.rem(x + d, mp)
        part = pl.ds(i * per_chunk, per_chunk)
        return remote(
            rows_hbm.at[part], raw.at[x, part], row_send.at[d, i], row_recv.at[d, i], {"mp": target}
        )

    def swap(n):
        return remote(
            weight_hbm.at[:, columns(other, n)],
            weights.at[z, c, n],
            swap_send.at[n],
            swap_recv.at[n],
            {"section": other},
        )

    def piece_rows(m):
        return pl.ds(pl.multiple_of((m % cuts) * sub, sub), sub)

    def first_hop(direction, m):
        return remote(
            weight_hbm.at[piece_rows(m), columns(cross, m // cuts)],
            weights.at[z, c, m // cuts, piece_rows(m)],
            line_send.at[direction, 0, m],
            line_recv.at[direction, 0, m],
            {"batch": z + (1 if direction == 0 else -1), "section": cross},
        )

    def later_hop(direction, hop, m, piece):
        place = weights.at[piece, cross, m // cuts, piece_rows(m)]
        return remote(
            place,
            place,
            line_send.at[direction, hop, m],
            line_recv.at[direction, hop, m],
            {"batch": z + (1 if direction == 0 else -1)},
        )

    def twin_copy(piece, m, kind):
        place = weights.at[piece, kind, m // cuts, piece_rows(m)]
        return remote(place, place, twin_send.at[piece, m], twin_recv.at[piece, m], {"group": twin})

    def norm_copy(i):
        part = pl.ds(i * per_chunk, per_chunk)
        return remote(
            normed.at[c, :, part],
            normed.at[c, :, part],
            norm_send.at[i],
            norm_recv.at[i],
            {"section": other},
        )

    def sum_copy(d, e):
        peer, side = lax.rem(x + d, mp), lax.rem(c + e, 2)
        return remote(
            partial.at[side],
            logits_in.at[d * 2 + e],
            sum_send.at[d * 2 + e],
            sum_recv.at[d * 2 + e],
            {"mp": peer, "section": side},
        )

    own_weights = [
        pltpu.make_async_copy(weight_hbm.at[:, columns(c, n)], weights.at[z, c, n], weight_sem.at[n])
        for n in range(chunks)
    ]

    def send_first(m):
        @pl.when(z < nb - 1)
        def _():
            first_hop(0, m).start()

        @pl.when(z > 0)
        def _():
            first_hop(1, m).start()

    for m in range(first):
        send_first(m)
    for i in range(row_chunks):
        for d in range(1, mp):
            row_copy(d, i).start()

    lane = lax.broadcasted_iota(jnp.int32, (1, group * wide_slots), 1)
    slot_of_lane = lane % wide_slots
    ancestor = jnp.full((1, group * wide_slots), -1, jnp.int32)
    for p in range(slots):
        ancestor = jnp.where(slot_of_lane == p, ancestry_ref[z * slots + p], ancestor)
    source = jnp.zeros_like(ancestor)
    for d in range(1, nb):
        source = source + jnp.where(ancestor >= d * slots, 1, 0)
    source = jnp.where(ancestor >= 0, source, -1)
    spread = jnp.broadcast_to(source, (wide_slots, group * wide_slots))
    row_at = lax.broadcasted_iota(jnp.int32, spread.shape, 0)
    lane_at = lax.broadcasted_iota(jnp.int32, spread.shape, 1)
    source_column = jnp.sum(jnp.where(row_at == lane_at, spread, 0), axis=1, keepdims=True)
    before = (source_column == spread) & (row_at < lane_at % wide_slots)
    rank = jnp.sum(jnp.where(before, 1, 0), axis=0, keepdims=True)
    code = jnp.where(source >= 0, (source * cap + rank) * group + lane // wide_slots, -1)
    lines = nb * cap * group
    wanted = lax.broadcasted_iota(jnp.int32, (lines, group * wide_slots), 0) == code
    requests = jnp.where(wanted, 1.0, 0.0).astype(jnp.bfloat16)

    own_copies[0].wait()
    own_copies[1].wait()
    own_copies[2].wait()

    def stack(block):
        blocks_of = [block[:, g * HD : (g + 1) * HD] for g in range(block.shape[1] // HD)]
        while len(blocks_of) < group:
            blocks_of.append(jnp.zeros_like(blocks_of[0]))
        filler = jnp.zeros((wide_slots - slots, HD), jnp.float32)
        tall = [part for g in blocks_of for part in ((g, filler) if wide_slots > slots else (g,))]
        return jnp.concatenate(tall, axis=0).astype(jnp.bfloat16)

    for h in range(kvl + 1):
        if h < kvl:
            block = letter_rows[:, h * group * HD : (h + 1) * group * HD].astype(jnp.float32)
        else:
            block = jnp.concatenate(
                [key_rows_in[...].astype(jnp.float32), value_rows_in[...].astype(jnp.float32)], axis=1
            )
        packed = jnp.dot(requests, stack(block), preferred_element_type=jnp.float32).astype(jnp.bfloat16)
        for s in range(nb):
            mail_out[s, h] = packed[s * cap * group : (s + 1) * cap * group]
    for d in range(1, nb):
        mail(d).start()
    own_mail = pltpu.make_async_copy(mail_out.at[z], mail_in.at[z], local_sem.at[8])
    own_mail.start()
    for m in range(first, parts):
        send_first(m)
    for n in range(chunks):
        swap(n).start()
    for copy in own_weights:
        copy.start()

    squares = (group * wide_slots, group * wide_slots)
    diagonal = lax.broadcasted_iota(jnp.int32, squares, 0) == lax.broadcasted_iota(jnp.int32, squares, 1)
    code_column = jnp.sum(jnp.where(diagonal, jnp.broadcast_to(code, squares), 0), axis=1, keepdims=True)
    found = lax.broadcasted_iota(jnp.int32, (group * wide_slots, lines), 1) == code_column
    picker[...] = jnp.where(found, 1.0, 0.0).astype(jnp.bfloat16)

    low = z * slots

    def list_served(d, carry):
        upcoming = jnp.int32(slots)
        follow[slots] = upcoming
        for p in reversed(range(slots)):
            a = ancestry_ref[d * slots + p]
            upcoming = jnp.where((a >= low) & (a < low + slots), p, upcoming)
            follow[p] = upcoming
        at = follow[0]
        for r in range(cap):
            chosen[d * cap + r] = jnp.minimum(at, slots - 1)
            at = follow[jnp.minimum(at + 1, slots)]
        return carry

    lax.fori_loop(0, nb, list_served, 0)

    own_copies[3].wait()
    own_copies[4].wait()
    own_mail.wait()

    def line_step(k):
        r, m = k // parts + 1, k % parts

        @pl.when(z - r >= 0)
        def _():
            piece = z - r
            later_hop(0, r - 1, m, piece).wait_recv()

            @pl.when(z + 1 < nb)
            def _():
                later_hop(0, r, m, piece).start()

            twin_copy(piece, m, cross).start()

        @pl.when(z + r < nb)
        def _():
            piece = z + r
            later_hop(1, r - 1, m, piece).wait_recv()

            @pl.when(z > 0)
            def _():
                later_hop(1, r, m, piece).start()

            twin_copy(piece, m, cross).start()

    scale = 1.0 / HD**0.5
    context = page_count * keys.shape[1]
    step = 4 if cap % 4 == 0 else cap
    blocks = cap // step
    serve_turns = nb * blocks
    turns = serve_turns + row_chunks
    early = (nb - 2) * parts

    def steps_of_turn(i):
        if early % turns == 0:
            for u in range(early // turns):
                line_step(i * (early // turns) + u)
        else:

            def one(k, carry):
                line_step(k)
                return carry

            lax.fori_loop(i * early // turns, (i + 1) * early // turns, one, 0)

    position = lax.broadcasted_iota(jnp.int32, (heads, context), 1)

    def serve(d, r, letters, u):
        p = chosen[d * cap + r]
        pages = [pages_ref[i, p] for i in range(page_count)]
        length = lengths_ref[low + p]
        key_block = jnp.concatenate([keys[page] for page in pages], axis=0)
        value_block = jnp.concatenate([values[page] for page in pages], axis=0)
        mine = [letter[u * group : (u + 1) * group] for letter in letters]
        nothing = jnp.zeros((group, HD), jnp.float32)
        wide = jnp.concatenate(
            [
                jnp.concatenate([mine[h] if g == h else nothing for g in range(kvl)], axis=1)
                for h in range(kvl)
            ],
            axis=0,
        ).astype(jnp.bfloat16)
        scores = (
            lax.dot_general(
                wide, key_block, (((1,), (1,)), ((), ())), preferred_element_type=jnp.float32
            )
            * scale
        )
        scores = jnp.where(position < length, scores, -1e30)
        top = jnp.max(scores, axis=1, keepdims=True)
        w = jnp.exp(scores - top)
        den = jnp.sum(w, axis=1, keepdims=True)
        everything = jnp.dot(w.astype(jnp.bfloat16), value_block, preferred_element_type=jnp.float32)
        answers = []
        for h in range(kvl):
            rows = slice(h * group, (h + 1) * group)
            own_score = jnp.sum(mine[h] * mine[kvl][h : h + 1], axis=1, keepdims=True) * scale
            own = jnp.exp(own_score - top[rows])
            num = everything[rows, h * HD : (h + 1) * HD] + own * mine[kvl][kvl + h : kvl + h + 1]
            answers.append(num / (den[rows] + own))
        return answers

    def serve_block(i, carry):
        steps_of_turn(i)
        away = i // blocks
        d = lax.rem(z + away, nb)
        r0 = lax.rem(i, blocks) * step

        @pl.when((lax.rem(i, blocks) == 0) & (away > 0))
        def _():
            mail(nb - away).wait_recv()

        some = pl.ds(pl.multiple_of(r0 * group, step * group), step * group)
        letters = [mail_in[d, h, some].astype(jnp.float32) for h in range(kvl + 1)]
        results = [serve(d, r0 + u, letters, u) for u in range(step)]
        for h in range(kvl):
            served_out[d, h, some] = jnp.concatenate([answers[h] for answers in results], axis=0).astype(
                jnp.bfloat16
            )
        return carry

    lax.fori_loop(0, serve_turns, serve_block, 0)
    own_back = pltpu.make_async_copy(served_out.at[z], returned.at[z], local_sem.at[9])
    own_back.start()

    features = row_width * mp
    pieces_per_block = row_width // depth
    fine = min(16, per_chunk)

    def row_step(i):
        for d in range(1, mp):
            row_copy(d, i).wait_recv()

        def normalise(j, carry):
            start = pl.multiple_of(i * per_chunk + j * fine, fine)
            part = pl.ds(start, fine)
            power = jnp.zeros((fine, 1), jnp.float32)
            for b in range(mp):
                block = raw[b, part].astype(jnp.float32)
                power = power + jnp.sum(block * block, axis=1, keepdims=True)
            factor = lax.rsqrt(power / features + 1e-06)
            for b in range(mp):
                block = raw[b, part].astype(jnp.float32)
                gain = gain_ref[:, b * row_width : (b + 1) * row_width]
                result = (block * factor * gain).astype(jnp.bfloat16)
                for p in range(pieces_per_block):
                    normed[c, b * pieces_per_block + p, part] = result[:, p * depth : (p + 1) * depth]
            return carry

        lax.fori_loop(0, per_chunk // fine, normalise, 0)
        norm_copy(i).start()

    own_copies[5].wait()
    own_copies[7].wait()
    for i in range(row_chunks):
        steps_of_turn(serve_turns + i)
        row_step(i)
    for i in range(row_chunks):
        norm_copy(i).wait_recv()
    own_copies[6].wait()

    def multiply(piece, kind, n, fresh=False):
        here = slice(n * chunk, (n + 1) * chunk)
        for side in range(2):
            product = jnp.dot(
                normed[side, piece * ns + kind], weights[piece, kind, n], preferred_element_type=jnp.float32
            )
            if fresh:
                total[side, :, here] = bias_ref[:, columns(c, n)] + product
            else:
                total[side, :, here] += product

    def multiply_own(n):
        own_weights[n].wait()
        swap(n).wait_recv()
        multiply(z, 0, n, fresh=True)
        multiply(z, 1, n)

    def multiply_at(r, n):
        def both(piece):
            multiply(piece, cross, n)
            for j in range(cuts):
                twin_copy(piece, n * cuts + j, 1 - cross).wait_recv()
            multiply(piece, 1 - cross, n)

        def left():
            both(z - r)

        def right():
            both(z + r)

        pl.when(z - r >= 0)(left)
        pl.when(z + r < nb)(right)

    def near(n):
        multiply_own(n)

        def one(r, carry):
            multiply_at(r, n)
            return carry

        lax.fori_loop(1, nb - 1, one, 0)

    def last(n):
        multiply_at(nb - 1, n)
        class_part = class_ref[:, columns(c, n)]
        here = slice(n * chunk, (n + 1) * chunk)
        for side in range(2):
            hidden = jnp.maximum(total[side, :, here], 0.0).astype(jnp.bfloat16)
            sums = lax.dot_general(
                class_part, hidden, (((1,), (1,)), ((), ())), preferred_element_type=jnp.float32
            )
            if n == 0:
                partial[side, 0:2] = sums
            else:
                partial[side, 0:2] += sums

    partial[...] = jnp.zeros_like(partial)
    plan = [[] for _ in range(parts + 1)]
    for n in range(chunks):
        plan[n * (parts // 2) // chunks].append(functools.partial(near, n))
    for n in range(chunks):
        when = (n + 1) * cuts + cuts
        plan[when if parts // 2 <= when < parts else parts].append(functools.partial(last, n))
    for m in range(parts):
        line_step(early + m)
        for unit in plan[m]:
            unit()
        if m == parts - dims["late"]:
            for d in range(1, nb):
                back(d).start()
    for unit in plan[parts]:
        unit()

    pairs = [(d, e) for d in range(mp) for e in range(2) if d or e]
    for d, e in pairs:
        sum_copy(d, e).start()

    own_back.wait()
    for d in range(1, nb):
        back(d).wait_recv()
    for h in range(kvl):
        answers = returned[:, h].reshape(lines, HD)
        mine = jnp.dot(picker[...], answers, preferred_element_type=jnp.float32).astype(jnp.bfloat16)
        for g in range(group):
            at = (h * group + g) * HD
            attention_ref[:, at : at + HD] = mine[g * wide_slots : g * wide_slots + slots]

    logits = partial[c]
    for d, e in pairs:
        sum_copy(d, e).wait_recv()
        logits = logits + logits_in[d * 2 + e]
    odds_ref[...] = (logits[1:2] + class_bias_ref[1]) - (logits[0:1] + class_bias_ref[0])

    for d in range(1, nb):
        mail(d).wait_send()
        back(d).wait_send()
    for i in range(row_chunks):
        for d in range(1, mp):
            row_copy(d, i).wait_send()
        norm_copy(i).wait_send()
    for d, e in pairs:
        sum_copy(d, e).wait_send()
    for n in range(chunks):
        swap(n).wait_send()

    def drain_first(m, carry):
        @pl.when(z < nb - 1)
        def _():
            first_hop(0, m).wait_send()

        @pl.when(z > 0)
        def _():
            first_hop(1, m).wait_send()

        return carry

    lax.fori_loop(0, parts, drain_first, 0)

    def drain(k, carry):
        r, m = k // parts + 1, k % parts

        @pl.when(z - r >= 0)
        def _():
            @pl.when(z + 1 < nb)
            def _():
                later_hop(0, r, m, z - r).wait_send()

            twin_copy(z - r, m, cross).wait_send()

        @pl.when(z + r < nb)
        def _():
            @pl.when(z > 0)
            def _():
                later_hop(1, r, m, z + r).wait_send()

            twin_copy(z + r, m, cross).wait_send()

        return carry

    lax.fori_loop(0, (nb - 1) * parts, drain, 0)


def per_device(
    queries,
    new_keys,
    new_values,
    key_pages,
    value_pages,
    page_table,
    ancestry,
    lengths,
    step_rows,
    norm_gain,
    head_weight,
    head_bias,
    class_weight,
    class_bias,
):
    slot_count, page_count = page_table.shape
    kv_width = key_pages.shape[3]
    kvl = kv_width // HD
    group = queries.shape[2] // kv_width
    nb, ng = lax.axis_size("batch"), lax.axis_size("group")
    mp, ns = lax.axis_size("mp"), lax.axis_size("section")
    assert ng == 2 and ns == 2 and queries.shape[0] == 1 and 2 * kvl <= group
    cap = max(2, (2 * slot_count + nb - 1) // nb)
    wide_slots = (slot_count + 15) // 16 * 16

    row_count, row_width = step_rows.shape
    depth, width = head_weight.shape
    half = width // ns
    chunk = min(256, half)
    chunks = half // chunk
    cuts = 2
    parts = chunks * cuts
    row_chunks = 4
    dims = dict(
        nb=nb, mp=mp, ns=ns, cap=cap, page_count=page_count, kvl=kvl, group=group, slots=slot_count,
        wide_slots=wide_slots, half=half, chunk=chunk, chunks=chunks, depth=depth, row_chunks=row_chunks,
        cuts=cuts, first=2, late=1,
    )
    smem = pl.BlockSpec(memory_space=pltpu.SMEM)
    vmem = pl.BlockSpec(memory_space=pltpu.VMEM)
    anywhere = pl.BlockSpec(memory_space=pl.ANY)
    bf16, f32, i32 = jnp.bfloat16, jnp.float32, jnp.int32
    sems = pltpu.SemaphoreType.DMA
    letters = (nb, kvl + 1, cap * group, HD)
    answers = (nb, kvl, cap * group, HD)
    attention, odds = pl.pallas_call(
        functools.partial(fused_kernel, dims),
        out_shape=(
            jax.ShapeDtypeStruct((slot_count, kvl * group * HD), bf16),
            jax.ShapeDtypeStruct((1, row_count), f32),
        ),
        in_specs=[smem] * 4 + [anywhere] * 9 + [vmem],
        out_specs=(vmem, vmem),
        scratch_shapes=[
            pltpu.SMEM((slot_count + 1,), i32),
            pltpu.SMEM((nb * cap,), i32),
            pltpu.VMEM(queries.shape[1:], bf16),
            pltpu.VMEM(new_keys.shape[1:], bf16),
            pltpu.VMEM(new_values.shape[1:], bf16),
            pltpu.VMEM((1, row_width * mp), f32),
            pltpu.VMEM((1, width), f32),
            pltpu.VMEM((group * wide_slots, nb * cap * group), bf16),
            pltpu.VMEM(letters, bf16),
            pltpu.VMEM(letters, bf16),
            pltpu.VMEM(answers, bf16),
            pltpu.VMEM(answers, bf16),
            pltpu.VMEM(key_pages.shape[1:], bf16),
            pltpu.VMEM(key_pages.shape[1:], bf16),
            pltpu.VMEM((mp, row_count, row_width), bf16),
            pltpu.VMEM((2, nb * ns, row_count, depth), bf16),
            pltpu.VMEM((nb, ns, chunks, depth, chunk), bf16),
            pltpu.VMEM((2, row_count, half), f32),
            pltpu.VMEM((2, 8, row_count), f32),
            pltpu.VMEM((2 * mp, 8, row_count), f32),
            sems((10,)),
            sems((chunks,)),
            sems((nb,)),
            sems((nb,)),
            sems((nb,)),
            sems((nb,)),
            sems((2, nb, parts)),
            sems((2, nb, parts)),
            sems((nb, parts)),
            sems((nb, parts)),
            sems((chunks,)),
            sems((chunks,)),
            sems((mp, row_chunks)),
            sems((mp, row_chunks)),
            sems((row_chunks,)),
            sems((row_chunks,)),
            sems((2 * mp,)),
            sems((2 * mp,)),
        ],
        compiler_params=pltpu.CompilerParams(
            collective_id=0, has_side_effects=True, vmem_limit_bytes=60 * 1024 * 1024
        ),
        name="filter_round",
    )(
        ancestry,
        lengths,
        page_table.T,
        class_bias,
        queries,
        new_keys,
        new_values,
        key_pages,
        value_pages,
        step_rows,
        norm_gain.reshape(1, -1),
        head_weight,
        head_bias.reshape(1, -1),
        class_weight.T,
    )
    return attention.reshape(1, slot_count, -1), odds.reshape(-1)


def solution(mesh):
    placed = (
        P("section", ("group", "batch"), "mp"),
        P("section", ("group", "batch"), "mp"),
        P("section", ("group", "batch"), "mp"),
        P("section", ("group", "batch"), None, "mp"),
        P("section", ("group", "batch"), None, "mp"),
        P(("group", "batch"), None),
        P("group"),
        P("group"),
        P(("group", "batch", "section"), "mp"),
        P(),
        P(("batch", "section"), "mp"),
        P("mp"),
        P("mp", None),
        P(),
    )
    return jax.shard_map(
        per_device,
        mesh=mesh,
        in_specs=placed,
        out_specs=(P("section", ("group", "batch"), "mp"), P(("group", "batch", "section"))),
        check_vma=False,
    )
```

```python
import functools

import jax
import jax.numpy as jnp
from jax import lax
from jax.experimental import pallas as pl
from jax.experimental.pallas import tpu as pltpu
from jax.sharding import PartitionSpec as P

HD = 128
MESH = pl.DeviceIdType.MESH


def fused_kernel(
    dims,
    ancestry_hbm,
    lengths_hbm,
    pages_hbm,
    class_bias_hbm,
    queries_hbm,
    new_keys_hbm,
    new_values_hbm,
    keys_hbm,
    values_hbm,
    rows_hbm,
    gain_hbm,
    weight_hbm,
    bias_hbm,
    class_hbm,
    attention_hbm,
    odds_hbm,
    ancestry_ref,
    lengths_ref,
    pages_ref,
    class_bias_ref,
    class_ref,
    attention_ref,
    odds_ref,
    follow,
    chosen,
    letter_rows,
    key_rows_in,
    value_rows_in,
    gain_ref,
    bias_ref,
    picker,
    mail_out,
    mail_in,
    served_out,
    returned,
    keys,
    values,
    raw,
    normed,
    weights,
    total,
    partial,
    logits_in,
    relay,
    small_sem,
    local_sem,
    weight_sem,
    mail_send,
    mail_recv,
    back_send,
    back_recv,
    line_send,
    line_recv,
    twin_send,
    twin_recv,
    swap_send,
    swap_recv,
    row_send,
    row_recv,
    norm_send,
    norm_recv,
    sum_send,
    sum_recv,
):
    nb, mp, ns = dims["nb"], dims["mp"], dims["ns"]
    cap, page_count, kvl, group = dims["cap"], dims["page_count"], dims["kvl"], dims["group"]
    half, chunk, chunks, depth = dims["half"], dims["chunk"], dims["chunks"], dims["depth"]
    row_chunks, cuts, first = dims["row_chunks"], dims["cuts"], dims["first"]
    slots, wide_slots = dims["slots"], dims["wide_slots"]
    heads = kvl * group
    sub = depth // cuts
    parts = chunks * cuts
    z, y = lax.axis_index("batch"), lax.axis_index("group")
    x, c = lax.axis_index("mp"), lax.axis_index("section")
    other = 1 - c
    twin = 1 - y
    cross = lax.rem(c + y, 2)
    row_count, row_width = rows_hbm.shape
    per_chunk = row_count // row_chunks

    def remote(src, dst, send, recv, device):
        return pltpu.make_async_remote_copy(
            src_ref=src, dst_ref=dst, send_sem=send, recv_sem=recv, device_id=device, device_id_type=MESH
        )

    def columns(owner, n):
        return pl.ds(pl.multiple_of(owner * half + n * chunk, chunk), chunk)

    barrier = pltpu.get_barrier_semaphore()

    def greet(device):
        pl.semaphore_signal(barrier, inc=1, device_id=device, device_id_type=MESH)

    @pl.when(z > 0)
    def _():
        greet({"batch": z - 1})
        greet({"batch": z - 1, "section": other})

    @pl.when(z < nb - 1)
    def _():
        greet({"batch": z + 1})
        greet({"batch": z + 1, "section": other})

    greet({"section": other})
    greet({"group": twin})
    for d in range(1, mp):
        peer = lax.rem(x + d, mp)
        greet({"mp": peer})
        greet({"mp": peer, "section": other})

    own_copies = [
        pltpu.make_async_copy(queries_hbm.at[0], letter_rows, local_sem.at[0]),
        pltpu.make_async_copy(new_keys_hbm.at[0], key_rows_in, local_sem.at[1]),
        pltpu.make_async_copy(new_values_hbm.at[0], value_rows_in, local_sem.at[2]),
        pltpu.make_async_copy(keys_hbm.at[0], keys, local_sem.at[3]),
        pltpu.make_async_copy(values_hbm.at[0], values, local_sem.at[4]),
        pltpu.make_async_copy(gain_hbm, gain_ref, local_sem.at[5]),
        pltpu.make_async_copy(bias_hbm, bias_ref, local_sem.at[6]),
        pltpu.make_async_copy(rows_hbm, raw.at[x], local_sem.at[7]),
    ]
    small_copies = [
        pltpu.make_async_copy(src, dst, small_sem.at[i])
        for i, (src, dst) in enumerate(
            [
                (ancestry_hbm, ancestry_ref),
                (lengths_hbm, lengths_ref),
                (pages_hbm, pages_ref),
                (class_bias_hbm, class_bias_ref),
                (class_hbm, class_ref),
            ]
        )
    ]
    for copy in small_copies + own_copies:
        copy.start()

    neighbours = jnp.where(z > 0, 1, 0) + jnp.where(z < nb - 1, 1, 0)
    pl.semaphore_wait(barrier, 2 + 2 * (mp - 1) + 2 * neighbours)

    def mail(d):
        target = lax.rem(z + d, nb)
        return remote(mail_out.at[target], mail_in.at[z], mail_send.at[d], mail_recv.at[d], {"batch": target})

    def back(d):
        target = lax.rem(z + d, nb)
        return remote(
            served_out.at[target], returned.at[z], back_send.at[d], back_recv.at[d], {"batch": target}
        )

    def row_copy(d, i):
        target = lax.rem(x + d, mp)
        part = pl.ds(i * per_chunk, per_chunk)
        return remote(
            rows_hbm.at[part], raw.at[x, part], row_send.at[d, i], row_recv.at[d, i], {"mp": target}
        )

    def swap(n):
        return remote(
            weight_hbm.at[:, columns(other, n)],
            weights.at[z, c, n],
            swap_send.at[n],
            swap_recv.at[n],
            {"section": other},
        )

    def piece_rows(m):
        return pl.ds(pl.multiple_of((m % cuts) * sub, sub), sub)

    def first_hop(direction, m):
        return remote(
            weight_hbm.at[piece_rows(m), columns(cross, m // cuts)],
            weights.at[z, c, m // cuts, piece_rows(m)],
            line_send.at[direction, 0, m],
            line_recv.at[direction, 0, m],
            {"batch": z + (1 if direction == 0 else -1), "section": cross},
        )

    def later_hop(direction, hop, m, piece):
        place = weights.at[piece, cross, m // cuts, piece_rows(m)]
        return remote(
            place,
            place,
            line_send.at[direction, hop, m],
            line_recv.at[direction, hop, m],
            {"batch": z + (1 if direction == 0 else -1)},
        )

    def twin_copy(piece, m, kind):
        place = weights.at[piece, kind, m // cuts, piece_rows(m)]
        return remote(place, place, twin_send.at[piece, m], twin_recv.at[piece, m], {"group": twin})

    def norm_copy(i):
        part = pl.ds(i * per_chunk, per_chunk)
        return remote(
            normed.at[c, :, part],
            normed.at[c, :, part],
            norm_send.at[i],
            norm_recv.at[i],
            {"section": other},
        )

    def sum_copy(d, e):
        peer, side = lax.rem(x + d, mp), lax.rem(c + e, 2)
        return remote(
            partial.at[side],
            logits_in.at[d * 2 + e],
            sum_send.at[d * 2 + e],
            sum_recv.at[d * 2 + e],
            {"mp": peer, "section": side},
        )

    own_weights = [
        pltpu.make_async_copy(weight_hbm.at[:, columns(c, n)], weights.at[z, c, n], weight_sem.at[n])
        for n in range(chunks)
    ]

    def send_first(m):
        @pl.when(z < nb - 1)
        def _():
            first_hop(0, m).start()

        @pl.when(z > 0)
        def _():
            first_hop(1, m).start()

    for m in range(first):
        send_first(m)
    for i in range(row_chunks):
        for d in range(1, mp):
            row_copy(d, i).start()

    def pass_on(side, has_before, has_after, after):
        @pl.when(has_before)
        def _():
            pl.semaphore_wait(relay.at[side], 1)

        @pl.when(has_after)
        def _():
            pl.semaphore_signal(
                relay.at[side], inc=1, device_id={"batch": after}, device_id_type=MESH
            )

    def pass_right():
        pass_on(0, z > 0, z < nb - 1, z + 1)

    def pass_left():
        pass_on(1, z < nb - 1, z > 0, z - 1)

    @pl.when(z < nb // 2)
    def _():
        pass_right()
        pass_left()

    @pl.when(z >= nb // 2)
    def _():
        pass_left()
        pass_right()

    for copy in small_copies:
        copy.wait()
    lane = lax.broadcasted_iota(jnp.int32, (1, group * wide_slots), 1)
    slot_of_lane = lane % wide_slots
    ancestor = jnp.full((1, group * wide_slots), -1, jnp.int32)
    for p in range(slots):
        ancestor = jnp.where(slot_of_lane == p, ancestry_ref[z * slots + p], ancestor)
    source = jnp.zeros_like(ancestor)
    for d in range(1, nb):
        source = source + jnp.where(ancestor >= d * slots, 1, 0)
    source = jnp.where(ancestor >= 0, source, -1)
    spread = jnp.broadcast_to(source, (wide_slots, group * wide_slots))
    row_at = lax.broadcasted_iota(jnp.int32, spread.shape, 0)
    lane_at = lax.broadcasted_iota(jnp.int32, spread.shape, 1)
    source_column = jnp.sum(jnp.where(row_at == lane_at, spread, 0), axis=1, keepdims=True)
    before = (source_column == spread) & (row_at < lane_at % wide_slots)
    rank = jnp.sum(jnp.where(before, 1, 0), axis=0, keepdims=True)
    code = jnp.where(source >= 0, (source * cap + rank) * group + lane // wide_slots, -1)
    lines = nb * cap * group
    wanted = lax.broadcasted_iota(jnp.int32, (lines, group * wide_slots), 0) == code
    requests = jnp.where(wanted, 1.0, 0.0).astype(jnp.bfloat16)

    own_copies[0].wait()
    own_copies[1].wait()
    own_copies[2].wait()

    def stack(block):
        blocks_of = [block[:, g * HD : (g + 1) * HD] for g in range(block.shape[1] // HD)]
        while len(blocks_of) < group:
            blocks_of.append(jnp.zeros_like(blocks_of[0]))
        filler = jnp.zeros((wide_slots - slots, HD), jnp.float32)
        tall = [part for g in blocks_of for part in ((g, filler) if wide_slots > slots else (g,))]
        return jnp.concatenate(tall, axis=0).astype(jnp.bfloat16)

    for h in range(kvl + 1):
        if h < kvl:
            block = letter_rows[:, h * group * HD : (h + 1) * group * HD].astype(jnp.float32)
        else:
            block = jnp.concatenate(
                [key_rows_in[...].astype(jnp.float32), value_rows_in[...].astype(jnp.float32)], axis=1
            )
        packed = jnp.dot(requests, stack(block), preferred_element_type=jnp.float32).astype(jnp.bfloat16)
        for s in range(nb):
            mail_out[s, h] = packed[s * cap * group : (s + 1) * cap * group]
    for d in range(1, nb):
        mail(d).start()
    own_mail = pltpu.make_async_copy(mail_out.at[z], mail_in.at[z], local_sem.at[8])
    own_mail.start()
    for m in range(first, parts):
        send_first(m)
    for n in range(chunks):
        swap(n).start()
    for copy in own_weights:
        copy.start()

    squares = (group * wide_slots, group * wide_slots)
    diagonal = lax.broadcasted_iota(jnp.int32, squares, 0) == lax.broadcasted_iota(jnp.int32, squares, 1)
    code_column = jnp.sum(jnp.where(diagonal, jnp.broadcast_to(code, squares), 0), axis=1, keepdims=True)
    found = lax.broadcasted_iota(jnp.int32, (group * wide_slots, lines), 1) == code_column
    picker[...] = jnp.where(found, 1.0, 0.0).astype(jnp.bfloat16)

    low = z * slots

    def list_served(d, carry):
        upcoming = jnp.int32(slots)
        follow[slots] = upcoming
        for p in reversed(range(slots)):
            a = ancestry_ref[d * slots + p]
            upcoming = jnp.where((a >= low) & (a < low + slots), p, upcoming)
            follow[p] = upcoming
        at = follow[0]
        for r in range(cap):
            chosen[d * cap + r] = jnp.minimum(at, slots - 1)
            at = follow[jnp.minimum(at + 1, slots)]
        return carry

    lax.fori_loop(0, nb, list_served, 0)

    own_copies[3].wait()
    own_copies[4].wait()
    own_mail.wait()

    def line_step(k):
        r, m = k // parts + 1, k % parts

        @pl.when(z - r >= 0)
        def _():
            piece = z - r
            later_hop(0, r - 1, m, piece).wait_recv()

            @pl.when(z + 1 < nb)
            def _():
                later_hop(0, r, m, piece).start()

            twin_copy(piece, m, cross).start()

        @pl.when(z + r < nb)
        def _():
            piece = z + r
            later_hop(1, r - 1, m, piece).wait_recv()

            @pl.when(z > 0)
            def _():
                later_hop(1, r, m, piece).start()

            twin_copy(piece, m, cross).start()

    scale = 1.0 / HD**0.5
    context = page_count * keys.shape[1]
    step = 4 if cap % 4 == 0 else cap
    blocks = cap // step
    serve_turns = nb * blocks
    turns = serve_turns + row_chunks
    early = (nb - 2) * parts

    def steps_of_turn(i):
        if early % turns == 0:
            for u in range(early // turns):
                line_step(i * (early // turns) + u)
        else:

            def one(k, carry):
                line_step(k)
                return carry

            lax.fori_loop(i * early // turns, (i + 1) * early // turns, one, 0)

    position = lax.broadcasted_iota(jnp.int32, (heads, context), 1)

    def serve(d, r, letters, u):
        p = chosen[d * cap + r]
        pages = [pages_ref[i, p] for i in range(page_count)]
        length = lengths_ref[low + p]
        key_block = jnp.concatenate([keys[page] for page in pages], axis=0)
        value_block = jnp.concatenate([values[page] for page in pages], axis=0)
        mine = [letter[u * group : (u + 1) * group] for letter in letters]
        nothing = jnp.zeros((group, HD), jnp.float32)
        wide = jnp.concatenate(
            [
                jnp.concatenate([mine[h] if g == h else nothing for g in range(kvl)], axis=1)
                for h in range(kvl)
            ],
            axis=0,
        ).astype(jnp.bfloat16)
        scores = (
            lax.dot_general(
                wide, key_block, (((1,), (1,)), ((), ())), preferred_element_type=jnp.float32
            )
            * scale
        )
        scores = jnp.where(position < length, scores, -1e30)
        top = jnp.max(scores, axis=1, keepdims=True)
        w = jnp.exp(scores - top)
        den = jnp.sum(w, axis=1, keepdims=True)
        everything = jnp.dot(w.astype(jnp.bfloat16), value_block, preferred_element_type=jnp.float32)
        answers = []
        for h in range(kvl):
            rows = slice(h * group, (h + 1) * group)
            own_score = jnp.sum(mine[h] * mine[kvl][h : h + 1], axis=1, keepdims=True) * scale
            own = jnp.exp(own_score - top[rows])
            num = everything[rows, h * HD : (h + 1) * HD] + own * mine[kvl][kvl + h : kvl + h + 1]
            answers.append(num / (den[rows] + own))
        return answers

    def serve_block(i, carry):
        steps_of_turn(i)
        away = i // blocks
        d = lax.rem(z + away, nb)
        r0 = lax.rem(i, blocks) * step

        @pl.when((lax.rem(i, blocks) == 0) & (away > 0))
        def _():
            mail(nb - away).wait_recv()

        some = pl.ds(pl.multiple_of(r0 * group, step * group), step * group)
        letters = [mail_in[d, h, some].astype(jnp.float32) for h in range(kvl + 1)]
        results = [serve(d, r0 + u, letters, u) for u in range(step)]
        for h in range(kvl):
            served_out[d, h, some] = jnp.concatenate([answers[h] for answers in results], axis=0).astype(
                jnp.bfloat16
            )
        return carry

    lax.fori_loop(0, serve_turns, serve_block, 0)
    own_back = pltpu.make_async_copy(served_out.at[z], returned.at[z], local_sem.at[9])
    own_back.start()

    features = row_width * mp
    pieces_per_block = row_width // depth
    fine = min(16, per_chunk)

    def row_step(i):
        for d in range(1, mp):
            row_copy(d, i).wait_recv()

        def normalise(j, carry):
            start = pl.multiple_of(i * per_chunk + j * fine, fine)
            part = pl.ds(start, fine)
            power = jnp.zeros((fine, 1), jnp.float32)
            for b in range(mp):
                block = raw[b, part].astype(jnp.float32)
                power = power + jnp.sum(block * block, axis=1, keepdims=True)
            factor = lax.rsqrt(power / features + 1e-06)
            for b in range(mp):
                block = raw[b, part].astype(jnp.float32)
                gain = gain_ref[:, b * row_width : (b + 1) * row_width]
                result = (block * factor * gain).astype(jnp.bfloat16)
                for p in range(pieces_per_block):
                    normed[c, b * pieces_per_block + p, part] = result[:, p * depth : (p + 1) * depth]
            return carry

        lax.fori_loop(0, per_chunk // fine, normalise, 0)
        norm_copy(i).start()

    own_copies[5].wait()
    own_copies[7].wait()
    for i in range(row_chunks):
        steps_of_turn(serve_turns + i)
        row_step(i)
    for i in range(row_chunks):
        norm_copy(i).wait_recv()
    own_copies[6].wait()

    def multiply(piece, kind, n, fresh=False):
        here = slice(n * chunk, (n + 1) * chunk)
        for side in range(2):
            product = jnp.dot(
                normed[side, piece * ns + kind], weights[piece, kind, n], preferred_element_type=jnp.float32
            )
            if fresh:
                total[side, :, here] = bias_ref[:, columns(c, n)] + product
            else:
                total[side, :, here] += product

    def multiply_own(n):
        own_weights[n].wait()
        swap(n).wait_recv()
        multiply(z, 0, n, fresh=True)
        multiply(z, 1, n)

    def multiply_at(r, n):
        def both(piece):
            multiply(piece, cross, n)
            for j in range(cuts):
                twin_copy(piece, n * cuts + j, 1 - cross).wait_recv()
            multiply(piece, 1 - cross, n)

        def left():
            both(z - r)

        def right():
            both(z + r)

        pl.when(z - r >= 0)(left)
        pl.when(z + r < nb)(right)

    def near(n):
        multiply_own(n)

        def one(r, carry):
            multiply_at(r, n)
            return carry

        lax.fori_loop(1, nb - 1, one, 0)

    def last(n):
        multiply_at(nb - 1, n)
        class_part = class_ref[:, columns(c, n)]
        here = slice(n * chunk, (n + 1) * chunk)
        for side in range(2):
            hidden = jnp.maximum(total[side, :, here], 0.0).astype(jnp.bfloat16)
            sums = lax.dot_general(
                class_part, hidden, (((1,), (1,)), ((), ())), preferred_element_type=jnp.float32
            )
            if n == 0:
                partial[side, 0:2] = sums
            else:
                partial[side, 0:2] += sums

    partial[...] = jnp.zeros_like(partial)
    plan = [[] for _ in range(parts + 1)]
    for n in range(chunks):
        plan[n * (parts // 2) // chunks].append(functools.partial(near, n))
    for n in range(chunks):
        when = (n + 1) * cuts + cuts
        plan[when if parts // 2 <= when < parts else parts].append(functools.partial(last, n))
    for m in range(parts):
        line_step(early + m)
        for unit in plan[m]:
            unit()
        if m == parts - dims["late"]:
            for d in range(1, nb):
                back(d).start()
    for unit in plan[parts]:
        unit()

    pairs = [(d, e) for d in range(mp) for e in range(2) if d or e]
    for d, e in pairs:
        sum_copy(d, e).start()

    own_back.wait()
    for d in range(1, nb):
        back(d).wait_recv()
    for h in range(kvl):
        answers = returned[:, h].reshape(lines, HD)
        mine = jnp.dot(picker[...], answers, preferred_element_type=jnp.float32).astype(jnp.bfloat16)
        for g in range(group):
            at = (h * group + g) * HD
            attention_ref[:, at : at + HD] = mine[g * wide_slots : g * wide_slots + slots]
    attention_out = pltpu.make_async_copy(attention_ref, attention_hbm, small_sem.at[0])
    attention_out.start()

    logits = partial[c]
    for d, e in pairs:
        sum_copy(d, e).wait_recv()
        logits = logits + logits_in[d * 2 + e]
    odds_ref[...] = (logits[1:2] + class_bias_ref[1]) - (logits[0:1] + class_bias_ref[0])
    odds_out = pltpu.make_async_copy(odds_ref, odds_hbm, small_sem.at[1])
    odds_out.start()

    for d in range(1, nb):
        mail(d).wait_send()
        back(d).wait_send()
    for i in range(row_chunks):
        for d in range(1, mp):
            row_copy(d, i).wait_send()
        norm_copy(i).wait_send()
    for d, e in pairs:
        sum_copy(d, e).wait_send()
    for n in range(chunks):
        swap(n).wait_send()

    def drain_first(m, carry):
        @pl.when(z < nb - 1)
        def _():
            first_hop(0, m).wait_send()

        @pl.when(z > 0)
        def _():
            first_hop(1, m).wait_send()

        return carry

    lax.fori_loop(0, parts, drain_first, 0)

    def drain(k, carry):
        r, m = k // parts + 1, k % parts

        @pl.when(z - r >= 0)
        def _():
            @pl.when(z + 1 < nb)
            def _():
                later_hop(0, r, m, z - r).wait_send()

            twin_copy(z - r, m, cross).wait_send()

        @pl.when(z + r < nb)
        def _():
            @pl.when(z > 0)
            def _():
                later_hop(1, r, m, z + r).wait_send()

            twin_copy(z + r, m, cross).wait_send()

        return carry

    lax.fori_loop(0, (nb - 1) * parts, drain, 0)
    attention_out.wait()
    odds_out.wait()


def per_device(
    queries,
    new_keys,
    new_values,
    key_pages,
    value_pages,
    page_table,
    ancestry,
    lengths,
    step_rows,
    norm_gain,
    head_weight,
    head_bias,
    class_weight,
    class_bias,
):
    slot_count, page_count = page_table.shape
    kv_width = key_pages.shape[3]
    kvl = kv_width // HD
    group = queries.shape[2] // kv_width
    nb, ng = lax.axis_size("batch"), lax.axis_size("group")
    mp, ns = lax.axis_size("mp"), lax.axis_size("section")
    assert ng == 2 and ns == 2 and queries.shape[0] == 1 and 2 * kvl <= group
    cap = max(2, (2 * slot_count + nb - 1) // nb)
    wide_slots = (slot_count + 15) // 16 * 16

    row_count, row_width = step_rows.shape
    depth, width = head_weight.shape
    half = width // ns
    chunk = min(256, half)
    chunks = half // chunk
    cuts = 2
    parts = chunks * cuts
    row_chunks = 4
    dims = dict(
        nb=nb, mp=mp, ns=ns, cap=cap, page_count=page_count, kvl=kvl, group=group, slots=slot_count,
        wide_slots=wide_slots, half=half, chunk=chunk, chunks=chunks, depth=depth, row_chunks=row_chunks,
        cuts=cuts, first=2, late=1,
    )
    anywhere = pl.BlockSpec(memory_space=pl.ANY)
    bf16, f32, i32 = jnp.bfloat16, jnp.float32, jnp.int32
    sems = pltpu.SemaphoreType.DMA
    letters = (nb, kvl + 1, cap * group, HD)
    answers = (nb, kvl, cap * group, HD)
    attention, odds = pl.pallas_call(
        functools.partial(fused_kernel, dims),
        out_shape=(
            jax.ShapeDtypeStruct((slot_count, kvl * group * HD), bf16),
            jax.ShapeDtypeStruct((1, row_count), f32),
        ),
        in_specs=[anywhere] * 14,
        out_specs=(anywhere, anywhere),
        scratch_shapes=[
            pltpu.SMEM(ancestry.shape, i32),
            pltpu.SMEM(lengths.shape, i32),
            pltpu.SMEM((page_count, slot_count), i32),
            pltpu.SMEM(class_bias.shape, f32),
            pltpu.VMEM((2, width), bf16),
            pltpu.VMEM((slot_count, kvl * group * HD), bf16),
            pltpu.VMEM((1, row_count), f32),
            pltpu.SMEM((slot_count + 1,), i32),
            pltpu.SMEM((nb * cap,), i32),
            pltpu.VMEM(queries.shape[1:], bf16),
            pltpu.VMEM(new_keys.shape[1:], bf16),
            pltpu.VMEM(new_values.shape[1:], bf16),
            pltpu.VMEM((1, row_width * mp), f32),
            pltpu.VMEM((1, width), f32),
            pltpu.VMEM((group * wide_slots, nb * cap * group), bf16),
            pltpu.VMEM(letters, bf16),
            pltpu.VMEM(letters, bf16),
            pltpu.VMEM(answers, bf16),
            pltpu.VMEM(answers, bf16),
            pltpu.VMEM(key_pages.shape[1:], bf16),
            pltpu.VMEM(key_pages.shape[1:], bf16),
            pltpu.VMEM((mp, row_count, row_width), bf16),
            pltpu.VMEM((2, nb * ns, row_count, depth), bf16),
            pltpu.VMEM((nb, ns, chunks, depth, chunk), bf16),
            pltpu.VMEM((2, row_count, half), f32),
            pltpu.VMEM((2, 8, row_count), f32),
            pltpu.VMEM((2 * mp, 8, row_count), f32),
            pltpu.SemaphoreType.REGULAR((2,)),
            sems((5,)),
            sems((10,)),
            sems((chunks,)),
            sems((nb,)),
            sems((nb,)),
            sems((nb,)),
            sems((nb,)),
            sems((2, nb, parts)),
            sems((2, nb, parts)),
            sems((nb, parts)),
            sems((nb, parts)),
            sems((chunks,)),
            sems((chunks,)),
            sems((mp, row_chunks)),
            sems((mp, row_chunks)),
            sems((row_chunks,)),
            sems((row_chunks,)),
            sems((2 * mp,)),
            sems((2 * mp,)),
        ],
        compiler_params=pltpu.CompilerParams(
            collective_id=0, has_side_effects=True, vmem_limit_bytes=60 * 1024 * 1024
        ),
        name="filter_round",
    )(
        ancestry,
        lengths,
        page_table.T,
        class_bias,
        queries,
        new_keys,
        new_values,
        key_pages,
        value_pages,
        step_rows,
        norm_gain.reshape(1, -1),
        head_weight,
        head_bias.reshape(1, -1),
        class_weight.T,
    )
    return attention.reshape(1, slot_count, -1), odds.reshape(-1)


def solution(mesh):
    placed = (
        P("section", ("group", "batch"), "mp"),
        P("section", ("group", "batch"), "mp"),
        P("section", ("group", "batch"), "mp"),
        P("section", ("group", "batch"), None, "mp"),
        P("section", ("group", "batch"), None, "mp"),
        P(("group", "batch"), None),
        P("group"),
        P("group"),
        P(("group", "batch", "section"), "mp"),
        P(),
        P(("batch", "section"), "mp"),
        P("mp"),
        P("mp", None),
        P(),
    )
    return jax.shard_map(
        per_device,
        mesh=mesh,
        in_specs=placed,
        out_specs=(P("section", ("group", "batch"), "mp"), P(("group", "batch", "section"))),
        check_vma=False,
    )
```

```python
import functools

import jax
import jax.numpy as jnp
from jax import lax
from jax.experimental import pallas as pl
from jax.experimental.pallas import tpu as pltpu
from jax.sharding import PartitionSpec as P

HD = 128
MESH = pl.DeviceIdType.MESH


def fused_kernel(
    dims,
    ancestry_hbm,
    lengths_hbm,
    pages_hbm,
    class_bias_hbm,
    queries_hbm,
    new_keys_hbm,
    new_values_hbm,
    keys_hbm,
    values_hbm,
    rows_hbm,
    gain_hbm,
    weight_hbm,
    bias_hbm,
    class_hbm,
    attention_hbm,
    odds_hbm,
    ancestry_ref,
    lengths_ref,
    pages_ref,
    class_bias_ref,
    class_ref,
    attention_ref,
    odds_ref,
    follow,
    chosen,
    letter_rows,
    key_rows_in,
    value_rows_in,
    gain_ref,
    bias_ref,
    picker,
    row_picker,
    lane_key,
    own_scores,
    peaks_out,
    peaks_in,
    mail_out,
    mail_in,
    served_out,
    returned,
    keys,
    values,
    raw,
    normed,
    weights,
    total,
    partial,
    logits_in,
    relay,
    small_sem,
    local_sem,
    weight_sem,
    mail_send,
    mail_recv,
    back_send,
    back_recv,
    line_send,
    line_recv,
    twin_send,
    twin_recv,
    swap_send,
    swap_recv,
    row_send,
    row_recv,
    norm_send,
    norm_recv,
    sum_send,
    sum_recv,
    end_send,
    end_recv,
    end_twin_send,
    end_twin_recv,
    peak_send,
    peak_recv,
):
    nb, mp, ns = dims["nb"], dims["mp"], dims["ns"]
    cap, page_count, kvl, group = dims["cap"], dims["page_count"], dims["kvl"], dims["group"]
    half, chunk, chunks, depth = dims["half"], dims["chunk"], dims["chunks"], dims["depth"]
    row_chunks, cuts, first = dims["row_chunks"], dims["cuts"], dims["first"]
    slots, wide_slots = dims["slots"], dims["wide_slots"]
    heads = kvl * group
    sub = depth // cuts
    ends = dims["ends"]
    parts = chunks * cuts
    z, y = lax.axis_index("batch"), lax.axis_index("group")
    x, c = lax.axis_index("mp"), lax.axis_index("section")
    other = 1 - c
    twin = 1 - y
    cross = lax.rem(c + y, 2)
    row_count, row_width = rows_hbm.shape
    per_chunk = row_count // row_chunks

    def remote(src, dst, send, recv, device):
        return pltpu.make_async_remote_copy(
            src_ref=src, dst_ref=dst, send_sem=send, recv_sem=recv, device_id=device, device_id_type=MESH
        )

    def columns(owner, n):
        return pl.ds(pl.multiple_of(owner * half + n * chunk, chunk), chunk)

    barrier = pltpu.get_barrier_semaphore()

    def greet(device):
        pl.semaphore_signal(barrier, inc=1, device_id=device, device_id_type=MESH)

    @pl.when(z > 0)
    def _():
        greet({"batch": z - 1})
        greet({"batch": z - 1, "section": other})

    @pl.when(z < nb - 1)
    def _():
        greet({"batch": z + 1})
        greet({"batch": z + 1, "section": other})

    greet({"section": other})
    greet({"group": twin})
    for d in range(1, mp):
        peer = lax.rem(x + d, mp)
        greet({"mp": peer})
        greet({"mp": peer, "section": other})

    own_copies = [
        pltpu.make_async_copy(queries_hbm.at[0], letter_rows, local_sem.at[0]),
        pltpu.make_async_copy(new_keys_hbm.at[0], key_rows_in, local_sem.at[1]),
        pltpu.make_async_copy(new_values_hbm.at[0], value_rows_in, local_sem.at[2]),
        pltpu.make_async_copy(keys_hbm.at[0], keys, local_sem.at[3]),
        pltpu.make_async_copy(values_hbm.at[0], values, local_sem.at[4]),
        pltpu.make_async_copy(gain_hbm, gain_ref, local_sem.at[5]),
        pltpu.make_async_copy(bias_hbm, bias_ref, local_sem.at[6]),
        pltpu.make_async_copy(rows_hbm, raw.at[x], local_sem.at[7]),
    ]
    small_copies = [
        pltpu.make_async_copy(src, dst, small_sem.at[i])
        for i, (src, dst) in enumerate(
            [
                (ancestry_hbm, ancestry_ref),
                (lengths_hbm, lengths_ref),
                (pages_hbm, pages_ref),
                (class_bias_hbm, class_bias_ref),
                (class_hbm, class_ref),
            ]
        )
    ]
    for copy in small_copies + own_copies:
        copy.start()

    neighbours = jnp.where(z > 0, 1, 0) + jnp.where(z < nb - 1, 1, 0)
    pl.semaphore_wait(barrier, 2 + 2 * (mp - 1) + 2 * neighbours)

    def mail(d):
        target = lax.rem(z + d, nb)
        return remote(mail_out.at[target], mail_in.at[z], mail_send.at[d], mail_recv.at[d], {"batch": target})

    def back(d):
        target = lax.rem(z + d, nb)
        return remote(
            served_out.at[target], returned.at[z], back_send.at[d], back_recv.at[d], {"batch": target}
        )

    def peak_back(d):
        target = lax.rem(z + d, nb)
        return remote(
            peaks_out.at[target], peaks_in.at[z], peak_send.at[d], peak_recv.at[d], {"batch": target}
        )

    def row_copy(d, i):
        target = lax.rem(x + d, mp)
        part = pl.ds(i * per_chunk, per_chunk)
        return remote(
            rows_hbm.at[part], raw.at[x, part], row_send.at[d, i], row_recv.at[d, i], {"mp": target}
        )

    def swap(n):
        return remote(
            weight_hbm.at[:, columns(other, n)],
            weights.at[z, c, n],
            swap_send.at[n],
            swap_recv.at[n],
            {"section": other},
        )

    def piece_rows(m):
        return pl.ds(pl.multiple_of((m % cuts) * sub, sub), sub)

    def first_hop(direction, m):
        return remote(
            weight_hbm.at[piece_rows(m), columns(cross, m // cuts)],
            weights.at[z, c, m // cuts, piece_rows(m)],
            line_send.at[direction, 0, m],
            line_recv.at[direction, 0, m],
            {"batch": z + (1 if direction == 0 else -1), "section": cross},
        )

    def later_hop(direction, hop, m, piece):
        place = weights.at[piece, cross, m // cuts, piece_rows(m)]
        return remote(
            place,
            place,
            line_send.at[direction, hop, m],
            line_recv.at[direction, hop, m],
            {"batch": z + (1 if direction == 0 else -1)},
        )

    def twin_copy(piece, m, kind):
        place = weights.at[piece, kind, m // cuts, piece_rows(m)]
        return remote(place, place, twin_send.at[piece, m], twin_recv.at[piece, m], {"group": twin})

    def end_place(piece, kind, f):
        return weights.at[piece, kind, chunks - 1, pl.ds(depth - sub + f * (sub // ends), sub // ends)]

    def end_hop(direction, f):
        place = end_place(0 if direction == 0 else nb - 1, cross, f)
        return remote(
            place,
            place,
            end_send.at[direction, f],
            end_recv.at[direction, f],
            {"batch": z + (1 if direction == 0 else -1)},
        )

    def end_twin(piece, f, kind):
        place = end_place(piece, kind, f)
        return remote(place, place, end_twin_send.at[f], end_twin_recv.at[f], {"group": twin})

    def norm_copy(i):
        part = pl.ds(i * per_chunk, per_chunk)
        return remote(
            normed.at[c, :, part],
            normed.at[c, :, part],
            norm_send.at[i],
            norm_recv.at[i],
            {"section": other},
        )

    def sum_copy(d, e):
        peer, side = lax.rem(x + d, mp), lax.rem(c + e, 2)
        return remote(
            partial.at[side],
            logits_in.at[d * 2 + e],
            sum_send.at[d * 2 + e],
            sum_recv.at[d * 2 + e],
            {"mp": peer, "section": side},
        )

    own_weights = [
        pltpu.make_async_copy(weight_hbm.at[:, columns(c, n)], weights.at[z, c, n], weight_sem.at[n])
        for n in range(chunks)
    ]

    def send_first(m):
        @pl.when(z < nb - 1)
        def _():
            first_hop(0, m).start()

        @pl.when(z > 0)
        def _():
            first_hop(1, m).start()

    for m in range(first):
        send_first(m)
    for i in range(row_chunks):
        for d in range(1, mp):
            row_copy(d, i).start()

    def pass_on(side, has_before, has_after, after):
        @pl.when(has_before)
        def _():
            pl.semaphore_wait(relay.at[side], 1)

        @pl.when(has_after)
        def _():
            pl.semaphore_signal(
                relay.at[side], inc=1, device_id={"batch": after}, device_id_type=MESH
            )

    def pass_right():
        pass_on(0, z > 0, z < nb - 1, z + 1)

    def pass_left():
        pass_on(1, z < nb - 1, z > 0, z - 1)

    @pl.when(z < nb // 2)
    def _():
        pass_right()
        pass_left()

    @pl.when(z >= nb // 2)
    def _():
        pass_left()
        pass_right()

    for copy in small_copies:
        copy.wait()
    lane = lax.broadcasted_iota(jnp.int32, (1, group * wide_slots), 1)
    slot_of_lane = lane % wide_slots
    ancestor = jnp.full((1, group * wide_slots), -1, jnp.int32)
    for p in range(slots):
        ancestor = jnp.where(slot_of_lane == p, ancestry_ref[z * slots + p], ancestor)
    source = jnp.zeros_like(ancestor)
    for d in range(1, nb):
        source = source + jnp.where(ancestor >= d * slots, 1, 0)
    source = jnp.where(ancestor >= 0, source, -1)
    spread = jnp.broadcast_to(source, (wide_slots, group * wide_slots))
    row_at = lax.broadcasted_iota(jnp.int32, spread.shape, 0)
    lane_at = lax.broadcasted_iota(jnp.int32, spread.shape, 1)
    source_column = jnp.sum(jnp.where(row_at == lane_at, spread, 0), axis=1, keepdims=True)
    before = (source_column == spread) & (row_at < lane_at % wide_slots)
    rank = jnp.sum(jnp.where(before, 1, 0), axis=0, keepdims=True)
    code = jnp.where(source >= 0, (source * cap + rank) * group + lane // wide_slots, -1)
    lines = nb * cap * group
    wanted = lax.broadcasted_iota(jnp.int32, (lines, group * wide_slots), 0) == code
    requests = jnp.where(wanted, 1.0, 0.0).astype(jnp.bfloat16)

    own_copies[0].wait()

    def stack(blocks_of):
        filler = jnp.zeros((wide_slots - slots, HD), jnp.float32)
        tall = [part for g in blocks_of for part in ((g, filler) if wide_slots > slots else (g,))]
        return jnp.concatenate(tall, axis=0)

    def query_stack(h):
        start = h * group
        return stack(
            [letter_rows[:, (start + g) * HD : (start + g + 1) * HD].astype(jnp.float32) for g in range(group)]
        )

    def repeated(ref, h):
        return stack([ref[:, h * HD : (h + 1) * HD].astype(jnp.float32)] * group)

    for h in range(kvl):
        tall = query_stack(h).astype(jnp.bfloat16)
        packed = jnp.dot(requests, tall, preferred_element_type=jnp.float32).astype(jnp.bfloat16)
        for s in range(nb):
            mail_out[s, h] = packed[s * cap * group : (s + 1) * cap * group]
    for d in range(1, nb):
        mail(d).start()
    own_mail = pltpu.make_async_copy(mail_out.at[z], mail_in.at[z], local_sem.at[8])
    own_mail.start()
    for m in range(first, parts):
        send_first(m)
    for n in range(chunks):
        swap(n).start()
    for copy in own_weights:
        copy.start()

    squares = (group * wide_slots, group * wide_slots)
    diagonal = lax.broadcasted_iota(jnp.int32, squares, 0) == lax.broadcasted_iota(jnp.int32, squares, 1)
    code_column = jnp.sum(jnp.where(diagonal, jnp.broadcast_to(code, squares), 0), axis=1, keepdims=True)
    found = lax.broadcasted_iota(jnp.int32, (group * wide_slots, lines), 1) == code_column
    picker[...] = jnp.where(found, 1.0, 0.0).astype(jnp.bfloat16)

    step = 4 if cap % 4 == 0 else cap
    blocks = cap // step
    scale = 1.0 / HD**0.5
    turn = jnp.zeros_like(rank)
    for b in range(1, blocks):
        turn = turn + jnp.where(rank >= b * step, 1, 0)

    def as_column(row):
        return jnp.sum(jnp.where(diagonal, jnp.broadcast_to(row, squares), 0), axis=1, keepdims=True)

    row_column = as_column(jnp.where(source >= 0, source * 8 + turn, -1))
    found_row = lax.broadcasted_iota(jnp.int32, row_picker.shape, 1) == row_column
    row_picker[...] = jnp.where(found_row, 1.0, 0.0).astype(jnp.bfloat16)
    key_column = as_column((rank - turn * step) * heads + lane // wide_slots)
    lane_key[...] = jnp.broadcast_to(key_column, lane_key.shape)
    own_copies[1].wait()
    own_copies[2].wait()
    head_lane = lax.broadcasted_iota(jnp.int32, own_scores.shape, 1)
    mine_scores = jnp.zeros(own_scores.shape, jnp.float32)
    for h in range(kvl):
        products = query_stack(h) * repeated(key_rows_in, h)
        one_head = jnp.sum(products, axis=1, keepdims=True) * scale
        mine_scores = jnp.where(head_lane == h, one_head, mine_scores)
    own_scores[...] = mine_scores
    peaks_out[...] = jnp.zeros_like(peaks_out)

    low = z * slots

    def list_served(d, carry):
        upcoming = jnp.int32(slots)
        follow[slots] = upcoming
        for p in reversed(range(slots)):
            a = ancestry_ref[d * slots + p]
            upcoming = jnp.where((a >= low) & (a < low + slots), p, upcoming)
            follow[p] = upcoming
        at = follow[0]
        for r in range(cap):
            chosen[d * cap + r] = jnp.minimum(at, slots - 1)
            at = follow[jnp.minimum(at + 1, slots)]
        return carry

    lax.fori_loop(0, nb, list_served, 0)

    own_copies[3].wait()
    own_copies[4].wait()
    own_mail.wait()

    def line_step(k, split=False):
        r, m = k // parts + 1, k % parts

        def arrived(direction, has_next, piece):
            later_hop(direction, r - 1, m, piece).wait_recv()

            @pl.when(has_next)
            def _():
                if split:
                    for f in range(ends):
                        end_hop(direction, f).start()
                else:
                    later_hop(direction, r, m, piece).start()

            twin_copy(piece, m, cross).start()

        @pl.when(z - r >= 0)
        def _():
            arrived(0, z + 1 < nb, z - r)

        @pl.when(z + r < nb)
        def _():
            arrived(1, z > 0, z + r)

    def end_step():
        def arrived(direction, piece):
            for f in range(ends):
                end_hop(direction, f).wait_recv()
                end_twin(piece, f, cross).start()

        @pl.when(z == nb - 1)
        def _():
            arrived(0, 0)

        @pl.when(z == 0)
        def _():
            arrived(1, nb - 1)

    context = page_count * keys.shape[1]
    serve_turns = nb * blocks
    turns = serve_turns + row_chunks
    early = (nb - 2) * parts

    def steps_of_turn(i, final=False):
        spare = 1 if final else 0
        if early % turns == 0:
            for u in range(early // turns - spare):
                line_step(i * (early // turns) + u)
        else:

            def one(k, carry):
                line_step(k)
                return carry

            lax.fori_loop(i * early // turns, (i + 1) * early // turns - spare, one, 0)
        if final:
            line_step(early - 1, split=True)

    position = lax.broadcasted_iota(jnp.int32, (heads, context), 1)

    def serve(d, r, letters, u):
        p = chosen[d * cap + r]
        pages = [pages_ref[i, p] for i in range(page_count)]
        length = lengths_ref[low + p]
        key_block = jnp.concatenate([keys[page] for page in pages], axis=0)
        value_block = jnp.concatenate([values[page] for page in pages], axis=0)
        mine = [letter[u * group : (u + 1) * group] for letter in letters]
        nothing = jnp.zeros((group, HD), jnp.float32)
        wide = jnp.concatenate(
            [
                jnp.concatenate([mine[h] if g == h else nothing for g in range(kvl)], axis=1)
                for h in range(kvl)
            ],
            axis=0,
        ).astype(jnp.bfloat16)
        scores = (
            lax.dot_general(
                wide, key_block, (((1,), (1,)), ((), ())), preferred_element_type=jnp.float32
            )
            * scale
        )
        scores = jnp.where(position < length, scores, -1e30)
        top = jnp.max(scores, axis=1, keepdims=True)
        w = jnp.exp(scores - top)
        den = jnp.sum(w, axis=1, keepdims=True)
        everything = jnp.dot(w.astype(jnp.bfloat16), value_block, preferred_element_type=jnp.float32)
        answers = []
        for h in range(kvl):
            rows = slice(h * group, (h + 1) * group)
            answers.append(everything[rows, h * HD : (h + 1) * HD] / den[rows])
        return answers, top + jnp.log(den)

    peak_square = (step * heads, HD)
    peak_diagonal = lax.broadcasted_iota(jnp.int32, peak_square, 0) == lax.broadcasted_iota(
        jnp.int32, peak_square, 1
    )

    def serve_block(i, carry):
        steps_of_turn(i)
        away = i // blocks
        d = lax.rem(z + away, nb)
        r0 = lax.rem(i, blocks) * step

        @pl.when((lax.rem(i, blocks) == 0) & (away > 0))
        def _():
            mail(nb - away).wait_recv()

        some = pl.ds(pl.multiple_of(r0 * group, step * group), step * group)
        letters = [mail_in[d, h, some].astype(jnp.float32) for h in range(kvl)]
        results = [serve(d, r0 + u, letters, u) for u in range(step)]
        for h in range(kvl):
            served_out[d, h, some] = jnp.concatenate([result[0][h] for result in results], axis=0).astype(
                jnp.bfloat16
            )
        peak_column = jnp.concatenate([result[1] for result in results], axis=0)
        spread_peaks = jnp.where(peak_diagonal, jnp.broadcast_to(peak_column, peak_square), 0.0)
        peaks_out[d, pl.ds(lax.rem(i, blocks), 1)] = jnp.sum(spread_peaks, axis=0, keepdims=True)
        return carry

    lax.fori_loop(0, serve_turns, serve_block, 0)
    own_back = pltpu.make_async_copy(served_out.at[z], returned.at[z], local_sem.at[9])
    own_back.start()

    features = row_width * mp
    pieces_per_block = row_width // depth
    fine = min(16, per_chunk)

    def row_step(i):
        for d in range(1, mp):
            row_copy(d, i).wait_recv()

        def normalise(j, carry):
            start = pl.multiple_of(i * per_chunk + j * fine, fine)
            part = pl.ds(start, fine)
            power = jnp.zeros((fine, 1), jnp.float32)
            for b in range(mp):
                block = raw[b, part].astype(jnp.float32)
                power = power + jnp.sum(block * block, axis=1, keepdims=True)
            factor = lax.rsqrt(power / features + 1e-06)
            for b in range(mp):
                block = raw[b, part].astype(jnp.float32)
                gain = gain_ref[:, b * row_width : (b + 1) * row_width]
                result = (block * factor * gain).astype(jnp.bfloat16)
                for p in range(pieces_per_block):
                    normed[c, b * pieces_per_block + p, part] = result[:, p * depth : (p + 1) * depth]
            return carry

        lax.fori_loop(0, per_chunk // fine, normalise, 0)
        norm_copy(i).start()

    own_copies[5].wait()
    own_copies[7].wait()
    for i in range(row_chunks):
        steps_of_turn(serve_turns + i, final=i == row_chunks - 1)
        row_step(i)
    for i in range(row_chunks):
        norm_copy(i).wait_recv()
    own_copies[6].wait()

    def multiply(piece, kind, n, fresh=False):
        here = slice(n * chunk, (n + 1) * chunk)
        for side in range(2):
            product = jnp.dot(
                normed[side, piece * ns + kind], weights[piece, kind, n], preferred_element_type=jnp.float32
            )
            if fresh:
                total[side, :, here] = bias_ref[:, columns(c, n)] + product
            else:
                total[side, :, here] += product

    def multiply_own(n):
        own_weights[n].wait()
        swap(n).wait_recv()
        multiply(z, 0, n, fresh=True)
        multiply(z, 1, n)

    def multiply_at(r, n, ended=0):
        def both(piece):
            multiply(piece, cross, n)
            for j in range(cuts - ended):
                twin_copy(piece, n * cuts + j, 1 - cross).wait_recv()
            for f in range(ends * ended):
                end_twin(piece, f, 1 - cross).wait_recv()
            multiply(piece, 1 - cross, n)

        def left():
            both(z - r)

        def right():
            both(z + r)

        pl.when(z - r >= 0)(left)
        pl.when(z + r < nb)(right)

    def near(n):
        multiply_own(n)

        def one(r, carry):
            multiply_at(r, n)
            return carry

        lax.fori_loop(1, nb - 1, one, 0)

    def last(n):
        multiply_at(nb - 1, n, ended=1 if n == chunks - 1 else 0)
        class_part = class_ref[:, columns(c, n)]
        here = slice(n * chunk, (n + 1) * chunk)
        for side in range(2):
            hidden = jnp.maximum(total[side, :, here], 0.0).astype(jnp.bfloat16)
            sums = lax.dot_general(
                class_part, hidden, (((1,), (1,)), ((), ())), preferred_element_type=jnp.float32
            )
            if n == 0:
                partial[side, 0:2] = sums
            else:
                partial[side, 0:2] += sums

    partial[...] = jnp.zeros_like(partial)
    plan = [[] for _ in range(parts + 1)]
    for n in range(chunks):
        plan[n * (parts // 2) // chunks].append(functools.partial(near, n))
    for n in range(chunks):
        when = (n + 1) * cuts + cuts
        plan[when if parts // 2 <= when < parts else parts].append(functools.partial(last, n))
    for m in range(parts):
        if m < parts - 1:
            line_step(early + m)
        else:
            end_step()
        for unit in plan[m]:
            unit()
        if m == parts - dims["late"]:
            for d in range(1, nb):
                back(d).start()
                peak_back(d).start()
    for unit in plan[parts]:
        unit()

    pairs = [(d, e) for d in range(mp) for e in range(2) if d or e]
    for d, e in pairs:
        sum_copy(d, e).start()

    own_back.wait()
    for d in range(1, nb):
        back(d).wait_recv()
        peak_back(d).wait_recv()
    peaks_in[z] = peaks_out[z]
    rest = peaks_in[...].reshape(nb * 8, HD)
    picked = jnp.zeros((group * wide_slots, HD), jnp.float32)
    for _ in range(3):
        coarse = rest.astype(jnp.bfloat16)
        picked = picked + jnp.dot(row_picker[...], coarse, preferred_element_type=jnp.float32)
        rest = rest - coarse.astype(jnp.float32)
    for h in range(kvl):
        here = lax.broadcasted_iota(jnp.int32, picked.shape, 1) == lane_key[...] + h * group
        peak = jnp.sum(jnp.where(here, picked, 0.0), axis=1, keepdims=True)
        share = 1.0 / (1.0 + jnp.exp(own_scores[:, h : h + 1] - peak))
        answers = returned[:, h].reshape(lines, HD)
        mine = jnp.dot(picker[...], answers, preferred_element_type=jnp.float32)
        mine = (mine * share + repeated(value_rows_in, h) * (1.0 - share)).astype(jnp.bfloat16)
        for g in range(group):
            at = (h * group + g) * HD
            attention_ref[:, at : at + HD] = mine[g * wide_slots : g * wide_slots + slots]
    attention_out = pltpu.make_async_copy(attention_ref, attention_hbm, small_sem.at[0])
    attention_out.start()

    logits = partial[c]
    for d, e in pairs:
        sum_copy(d, e).wait_recv()
        logits = logits + logits_in[d * 2 + e]
    odds_ref[...] = (logits[1:2] + class_bias_ref[1]) - (logits[0:1] + class_bias_ref[0])
    odds_out = pltpu.make_async_copy(odds_ref, odds_hbm, small_sem.at[1])
    odds_out.start()

    for d in range(1, nb):
        mail(d).wait_send()
        back(d).wait_send()
        peak_back(d).wait_send()
    for i in range(row_chunks):
        for d in range(1, mp):
            row_copy(d, i).wait_send()
        norm_copy(i).wait_send()
    for d, e in pairs:
        sum_copy(d, e).wait_send()
    for n in range(chunks):
        swap(n).wait_send()

    def drain_first(m, carry):
        @pl.when(z < nb - 1)
        def _():
            first_hop(0, m).wait_send()

        @pl.when(z > 0)
        def _():
            first_hop(1, m).wait_send()

        return carry

    lax.fori_loop(0, parts, drain_first, 0)

    def drain(k, carry, split=False):
        r, m = k // parts + 1, k % parts

        def sent(direction, has_next, piece):
            @pl.when(has_next)
            def _():
                if split:
                    for f in range(ends):
                        end_hop(direction, f).wait_send()
                else:
                    later_hop(direction, r, m, piece).wait_send()

            twin_copy(piece, m, cross).wait_send()

        @pl.when(z - r >= 0)
        def _():
            sent(0, z + 1 < nb, z - r)

        @pl.when(z + r < nb)
        def _():
            sent(1, z > 0, z + r)

        return carry

    lax.fori_loop(0, early - 1, drain, 0)
    drain(early - 1, 0, split=True)
    lax.fori_loop(early, early + parts - 1, drain, 0)

    @pl.when(z == nb - 1)
    def _():
        for f in range(ends):
            end_twin(0, f, cross).wait_send()

    @pl.when(z == 0)
    def _():
        for f in range(ends):
            end_twin(nb - 1, f, cross).wait_send()

    attention_out.wait()
    odds_out.wait()


def per_device(
    queries,
    new_keys,
    new_values,
    key_pages,
    value_pages,
    page_table,
    ancestry,
    lengths,
    step_rows,
    norm_gain,
    head_weight,
    head_bias,
    class_weight,
    class_bias,
):
    slot_count, page_count = page_table.shape
    kv_width = key_pages.shape[3]
    kvl = kv_width // HD
    group = queries.shape[2] // kv_width
    nb, ng = lax.axis_size("batch"), lax.axis_size("group")
    mp, ns = lax.axis_size("mp"), lax.axis_size("section")
    assert ng == 2 and ns == 2 and queries.shape[0] == 1
    cap = max(2, (2 * slot_count + nb - 1) // nb)
    wide_slots = (slot_count + 15) // 16 * 16

    row_count, row_width = step_rows.shape
    depth, width = head_weight.shape
    half = width // ns
    chunk = min(256, half)
    chunks = half // chunk
    cuts = 2
    parts = chunks * cuts
    ends = max(1, min(4, depth // cuts // 16))
    row_chunks = 4
    dims = dict(
        nb=nb, mp=mp, ns=ns, cap=cap, page_count=page_count, kvl=kvl, group=group, slots=slot_count,
        wide_slots=wide_slots, half=half, chunk=chunk, chunks=chunks, depth=depth, row_chunks=row_chunks,
        cuts=cuts, ends=ends, first=2, late=2,
    )
    anywhere = pl.BlockSpec(memory_space=pl.ANY)
    bf16, f32, i32 = jnp.bfloat16, jnp.float32, jnp.int32
    sems = pltpu.SemaphoreType.DMA
    answers = (nb, kvl, cap * group, HD)
    attention, odds = pl.pallas_call(
        functools.partial(fused_kernel, dims),
        out_shape=(
            jax.ShapeDtypeStruct((slot_count, kvl * group * HD), bf16),
            jax.ShapeDtypeStruct((1, row_count), f32),
        ),
        in_specs=[anywhere] * 14,
        out_specs=(anywhere, anywhere),
        scratch_shapes=[
            pltpu.SMEM(ancestry.shape, i32),
            pltpu.SMEM(lengths.shape, i32),
            pltpu.SMEM((page_count, slot_count), i32),
            pltpu.SMEM(class_bias.shape, f32),
            pltpu.VMEM((2, width), bf16),
            pltpu.VMEM((slot_count, kvl * group * HD), bf16),
            pltpu.VMEM((1, row_count), f32),
            pltpu.SMEM((slot_count + 1,), i32),
            pltpu.SMEM((nb * cap,), i32),
            pltpu.VMEM(queries.shape[1:], bf16),
            pltpu.VMEM(new_keys.shape[1:], bf16),
            pltpu.VMEM(new_values.shape[1:], bf16),
            pltpu.VMEM((1, row_width * mp), f32),
            pltpu.VMEM((1, width), f32),
            pltpu.VMEM((group * wide_slots, nb * cap * group), bf16),
            pltpu.VMEM((group * wide_slots, nb * 8), bf16),
            pltpu.VMEM((group * wide_slots, HD), i32),
            pltpu.VMEM((group * wide_slots, HD), f32),
            pltpu.VMEM((nb, 8, HD), f32),
            pltpu.VMEM((nb, 8, HD), f32),
            pltpu.VMEM(answers, bf16),
            pltpu.VMEM(answers, bf16),
            pltpu.VMEM(answers, bf16),
            pltpu.VMEM(answers, bf16),
            pltpu.VMEM(key_pages.shape[1:], bf16),
            pltpu.VMEM(key_pages.shape[1:], bf16),
            pltpu.VMEM((mp, row_count, row_width), bf16),
            pltpu.VMEM((2, nb * ns, row_count, depth), bf16),
            pltpu.VMEM((nb, ns, chunks, depth, chunk), bf16),
            pltpu.VMEM((2, row_count, half), f32),
            pltpu.VMEM((2, 8, row_count), f32),
            pltpu.VMEM((2 * mp, 8, row_count), f32),
            pltpu.SemaphoreType.REGULAR((2,)),
            sems((5,)),
            sems((10,)),
            sems((chunks,)),
            sems((nb,)),
            sems((nb,)),
            sems((nb,)),
            sems((nb,)),
            sems((2, nb, parts)),
            sems((2, nb, parts)),
            sems((nb, parts)),
            sems((nb, parts)),
            sems((chunks,)),
            sems((chunks,)),
            sems((mp, row_chunks)),
            sems((mp, row_chunks)),
            sems((row_chunks,)),
            sems((row_chunks,)),
            sems((2 * mp,)),
            sems((2 * mp,)),
            sems((2, ends)),
            sems((2, ends)),
            sems((ends,)),
            sems((ends,)),
            sems((nb,)),
            sems((nb,)),
        ],
        compiler_params=pltpu.CompilerParams(
            collective_id=0, has_side_effects=True, vmem_limit_bytes=60 * 1024 * 1024
        ),
        name="filter_round",
    )(
        ancestry,
        lengths,
        page_table.T,
        class_bias,
        queries,
        new_keys,
        new_values,
        key_pages,
        value_pages,
        step_rows,
        norm_gain.reshape(1, -1),
        head_weight,
        head_bias.reshape(1, -1),
        class_weight.T,
    )
    return attention.reshape(1, slot_count, -1), odds.reshape(-1)


def solution(mesh):
    placed = (
        P("section", ("group", "batch"), "mp"),
        P("section", ("group", "batch"), "mp"),
        P("section", ("group", "batch"), "mp"),
        P("section", ("group", "batch"), None, "mp"),
        P("section", ("group", "batch"), None, "mp"),
        P(("group", "batch"), None),
        P("group"),
        P("group"),
        P(("group", "batch", "section"), "mp"),
        P(),
        P(("batch", "section"), "mp"),
        P("mp"),
        P("mp", None),
        P(),
    )
    return jax.shard_map(
        per_device,
        mesh=mesh,
        in_specs=placed,
        out_specs=(P("section", ("group", "batch"), "mp"), P(("group", "batch", "section"))),
        check_vma=False,
    )
```

```python
import functools

import jax
import jax.numpy as jnp
from jax import lax
from jax.experimental import pallas as pl
from jax.experimental.pallas import tpu as pltpu
from jax.sharding import PartitionSpec as P

HD = 128
MESH = pl.DeviceIdType.MESH


def fused_kernel(
    dims,
    ancestry_hbm,
    lengths_hbm,
    pages_hbm,
    class_bias_hbm,
    queries_hbm,
    new_keys_hbm,
    new_values_hbm,
    keys_hbm,
    values_hbm,
    rows_hbm,
    gain_hbm,
    weight_hbm,
    bias_hbm,
    class_hbm,
    attention_hbm,
    odds_hbm,
    ancestry_ref,
    lengths_ref,
    pages_ref,
    class_bias_ref,
    class_ref,
    attention_ref,
    odds_ref,
    follow,
    chosen,
    letter_rows,
    key_rows_in,
    value_rows_in,
    gain_ref,
    bias_ref,
    picker,
    row_picker,
    lane_key,
    own_scores,
    peaks_out,
    peaks_in,
    mail_out,
    mail_in,
    served_out,
    returned,
    keys,
    values,
    raw,
    normed,
    weights,
    total,
    partial,
    logits_in,
    relay,
    small_sem,
    local_sem,
    weight_sem,
    mail_send,
    mail_recv,
    back_send,
    back_recv,
    line_send,
    line_recv,
    twin_send,
    twin_recv,
    swap_send,
    swap_recv,
    row_send,
    row_recv,
    norm_send,
    norm_recv,
    sum_send,
    sum_recv,
    end_send,
    end_recv,
    end_twin_send,
    end_twin_recv,
    peak_send,
    peak_recv,
    hub_picker,
    hub_in,
    merged_out,
    merged_in,
    hub_send,
    hub_recv,
    merged_send,
    merged_recv,
    both_send,
    both_recv,
):
    nb, mp, ns = dims["nb"], dims["mp"], dims["ns"]
    cap, page_count, kvl, group = dims["cap"], dims["page_count"], dims["kvl"], dims["group"]
    half, chunk, chunks, depth = dims["half"], dims["chunk"], dims["chunks"], dims["depth"]
    row_chunks, cuts, first = dims["row_chunks"], dims["cuts"], dims["first"]
    slots, wide_slots = dims["slots"], dims["wide_slots"]
    heads = kvl * group
    sub = depth // cuts
    ends, swapped = dims["ends"], dims["ends"] - dims["doubled"]
    parts = chunks * cuts
    z, y = lax.axis_index("batch"), lax.axis_index("group")
    x, c = lax.axis_index("mp"), lax.axis_index("section")
    other = 1 - c
    twin = 1 - y
    cross = lax.rem(c + y, 2)
    row_count, row_width = rows_hbm.shape
    per_chunk = row_count // row_chunks

    def remote(src, dst, send, recv, device):
        return pltpu.make_async_remote_copy(
            src_ref=src, dst_ref=dst, send_sem=send, recv_sem=recv, device_id=device, device_id_type=MESH
        )

    def columns(owner, n):
        return pl.ds(pl.multiple_of(owner * half + n * chunk, chunk), chunk)

    barrier = pltpu.get_barrier_semaphore()

    def greet(device):
        pl.semaphore_signal(barrier, inc=1, device_id=device, device_id_type=MESH)

    @pl.when(z > 0)
    def _():
        greet({"batch": z - 1})
        greet({"batch": z - 1, "section": other})

    @pl.when(z < nb - 1)
    def _():
        greet({"batch": z + 1})
        greet({"batch": z + 1, "section": other})

    greet({"section": other})
    greet({"group": twin})
    for d in range(1, mp):
        peer = lax.rem(x + d, mp)
        greet({"mp": peer})
        greet({"mp": peer, "section": other})

    own_copies = [
        pltpu.make_async_copy(queries_hbm.at[0], letter_rows, local_sem.at[0]),
        pltpu.make_async_copy(new_keys_hbm.at[0], key_rows_in, local_sem.at[1]),
        pltpu.make_async_copy(new_values_hbm.at[0], value_rows_in, local_sem.at[2]),
        pltpu.make_async_copy(keys_hbm.at[0], keys, local_sem.at[3]),
        pltpu.make_async_copy(values_hbm.at[0], values, local_sem.at[4]),
        pltpu.make_async_copy(gain_hbm, gain_ref, local_sem.at[5]),
        pltpu.make_async_copy(bias_hbm, bias_ref, local_sem.at[6]),
        pltpu.make_async_copy(rows_hbm, raw.at[x], local_sem.at[7]),
    ]
    small_copies = [
        pltpu.make_async_copy(src, dst, small_sem.at[i])
        for i, (src, dst) in enumerate(
            [
                (ancestry_hbm, ancestry_ref),
                (lengths_hbm, lengths_ref),
                (pages_hbm, pages_ref),
                (class_bias_hbm, class_bias_ref),
                (class_hbm, class_ref),
            ]
        )
    ]
    for copy in small_copies + own_copies:
        copy.start()

    neighbours = jnp.where(z > 0, 1, 0) + jnp.where(z < nb - 1, 1, 0)
    pl.semaphore_wait(barrier, 2 + 2 * (mp - 1) + 2 * neighbours)

    def mail(d):
        target = lax.rem(z + d, nb)
        return remote(mail_out.at[target], mail_in.at[z], mail_send.at[d], mail_recv.at[d], {"batch": target})

    def back(d):
        target = lax.rem(z + d, nb)
        return remote(
            served_out.at[target], returned.at[z], back_send.at[d], back_recv.at[d], {"batch": target}
        )

    def inside(d):
        target = lax.rem(z + d, nb)
        return (target > 0) & (target < nb - 1)

    def to_hub(end):
        hub = nb - 2 if end else 1
        return remote(
            served_out.at[end],
            hub_in.at[z],
            hub_send.at[1 if end else 0],
            hub_recv.at[z],
            {"batch": hub},
        )

    def from_hub_source(origin):
        return remote(
            served_out.at[0], hub_in.at[origin], hub_send.at[0], hub_recv.at[origin], {"batch": z - 1}
        )

    def merged_copy(end):
        return remote(merged_out, merged_in, merged_send, merged_recv, {"batch": end})

    def merge(end):
        hub = nb - 2 if end else 1
        for f in range(swapped, ends):
            end_other(0 if end else 1, f).start()
        for origin in range(nb):
            if origin not in (end, hub):
                from_hub_source(origin).wait_recv()
        hub_in[end] = jnp.zeros(hub_in.shape[1:], hub_in.dtype)
        hub_in[hub] = served_out[end]
        for h in range(kvl):
            answers = hub_in[:, h].reshape(nb * cap * group, HD)
            mine = jnp.dot(hub_picker[...], answers, preferred_element_type=jnp.float32)
            merged_out[h] = jnp.concatenate(
                [mine[g * wide_slots : g * wide_slots + slots] for g in range(group)], axis=0
            ).astype(jnp.bfloat16)
        merged_copy(end).start()

    def peak_back(d):
        target = lax.rem(z + d, nb)
        return remote(
            peaks_out.at[target], peaks_in.at[z], peak_send.at[d], peak_recv.at[d], {"batch": target}
        )

    def row_copy(d, i):
        target = lax.rem(x + d, mp)
        part = pl.ds(i * per_chunk, per_chunk)
        return remote(
            rows_hbm.at[part], raw.at[x, part], row_send.at[d, i], row_recv.at[d, i], {"mp": target}
        )

    def swap(n):
        return remote(
            weight_hbm.at[:, columns(other, n)],
            weights.at[z, c, n],
            swap_send.at[n],
            swap_recv.at[n],
            {"section": other},
        )

    def piece_rows(m):
        return pl.ds(pl.multiple_of((m % cuts) * sub, sub), sub)

    def first_hop(direction, m):
        return remote(
            weight_hbm.at[piece_rows(m), columns(cross, m // cuts)],
            weights.at[z, c, m // cuts, piece_rows(m)],
            line_send.at[direction, 0, m],
            line_recv.at[direction, 0, m],
            {"batch": z + (1 if direction == 0 else -1), "section": cross},
        )

    def later_hop(direction, hop, m, piece):
        place = weights.at[piece, cross, m // cuts, piece_rows(m)]
        return remote(
            place,
            place,
            line_send.at[direction, hop, m],
            line_recv.at[direction, hop, m],
            {"batch": z + (1 if direction == 0 else -1)},
        )

    def twin_copy(piece, m, kind):
        place = weights.at[piece, kind, m // cuts, piece_rows(m)]
        return remote(place, place, twin_send.at[piece, m], twin_recv.at[piece, m], {"group": twin})

    def end_place(piece, kind, f):
        return weights.at[piece, kind, chunks - 1, pl.ds(depth - sub + f * (sub // ends), sub // ends)]

    def end_hop(direction, f):
        place = end_place(0 if direction == 0 else nb - 1, cross, f)
        return remote(
            place,
            place,
            end_send.at[direction, f],
            end_recv.at[direction, f],
            {"batch": z + (1 if direction == 0 else -1)},
        )

    def end_twin(piece, f, kind):
        place = end_place(piece, kind, f)
        return remote(place, place, end_twin_send.at[f], end_twin_recv.at[f], {"group": twin})

    def end_other(direction, f):
        place = end_place(0 if direction == 0 else nb - 1, 1 - cross, f)
        return remote(
            place, place, both_send.at[f], both_recv.at[f], {"batch": z + (1 if direction == 0 else -1)}
        )

    def norm_copy(i):
        part = pl.ds(i * per_chunk, per_chunk)
        return remote(
            normed.at[c, :, part],
            normed.at[c, :, part],
            norm_send.at[i],
            norm_recv.at[i],
            {"section": other},
        )

    def sum_copy(d, e):
        peer, side = lax.rem(x + d, mp), lax.rem(c + e, 2)
        return remote(
            partial.at[side],
            logits_in.at[d * 2 + e],
            sum_send.at[d * 2 + e],
            sum_recv.at[d * 2 + e],
            {"mp": peer, "section": side},
        )

    own_weights = [
        pltpu.make_async_copy(weight_hbm.at[:, columns(c, n)], weights.at[z, c, n], weight_sem.at[n])
        for n in range(chunks)
    ]

    def send_first(m):
        @pl.when(z < nb - 1)
        def _():
            first_hop(0, m).start()

        @pl.when(z > 0)
        def _():
            first_hop(1, m).start()

    for m in range(first):
        send_first(m)
    for i in range(row_chunks):
        for d in range(1, mp):
            row_copy(d, i).start()

    def pass_on(side, has_before, has_after, after):
        @pl.when(has_before)
        def _():
            pl.semaphore_wait(relay.at[side], 1)

        @pl.when(has_after)
        def _():
            pl.semaphore_signal(
                relay.at[side], inc=1, device_id={"batch": after}, device_id_type=MESH
            )

    def pass_right():
        pass_on(0, z > 0, z < nb - 1, z + 1)

    def pass_left():
        pass_on(1, z < nb - 1, z > 0, z - 1)

    @pl.when(z < nb // 2)
    def _():
        pass_right()
        pass_left()

    @pl.when(z >= nb // 2)
    def _():
        pass_left()
        pass_right()

    for copy in small_copies:
        copy.wait()
    lane = lax.broadcasted_iota(jnp.int32, (1, group * wide_slots), 1)
    slot_of_lane = lane % wide_slots


    def slot_codes(owner):
        ancestor = jnp.full((1, group * wide_slots), -1, jnp.int32)
        for p in range(slots):
            ancestor = jnp.where(slot_of_lane == p, ancestry_ref[owner * slots + p], ancestor)
        source = jnp.zeros_like(ancestor)
        for d in range(1, nb):
            source = source + jnp.where(ancestor >= d * slots, 1, 0)
        source = jnp.where(ancestor >= 0, source, -1)
        spread = jnp.broadcast_to(source, (wide_slots, group * wide_slots))
        row_at = lax.broadcasted_iota(jnp.int32, spread.shape, 0)
        lane_at = lax.broadcasted_iota(jnp.int32, spread.shape, 1)
        source_column = jnp.sum(jnp.where(row_at == lane_at, spread, 0), axis=1, keepdims=True)
        before = (source_column == spread) & (row_at < lane_at % wide_slots)
        rank = jnp.sum(jnp.where(before, 1, 0), axis=0, keepdims=True)
        code = jnp.where(source >= 0, (source * cap + rank) * group + lane // wide_slots, -1)
        return source, rank, code

    source, rank, code = slot_codes(z)
    lines = nb * cap * group
    wanted = lax.broadcasted_iota(jnp.int32, (lines, group * wide_slots), 0) == code
    requests = jnp.where(wanted, 1.0, 0.0).astype(jnp.bfloat16)

    own_copies[0].wait()

    def stack(blocks_of):
        filler = jnp.zeros((wide_slots - slots, HD), jnp.float32)
        tall = [part for g in blocks_of for part in ((g, filler) if wide_slots > slots else (g,))]
        return jnp.concatenate(tall, axis=0)

    def query_stack(h):
        start = h * group
        return stack(
            [letter_rows[:, (start + g) * HD : (start + g + 1) * HD].astype(jnp.float32) for g in range(group)]
        )

    def repeated(ref, h):
        return stack([ref[:, h * HD : (h + 1) * HD].astype(jnp.float32)] * group)

    for h in range(kvl):
        tall = query_stack(h).astype(jnp.bfloat16)
        packed = jnp.dot(requests, tall, preferred_element_type=jnp.float32).astype(jnp.bfloat16)
        for s in range(nb):
            mail_out[s, h] = packed[s * cap * group : (s + 1) * cap * group]
    for d in range(1, nb):
        mail(d).start()
    own_mail = pltpu.make_async_copy(mail_out.at[z], mail_in.at[z], local_sem.at[8])
    own_mail.start()
    for m in range(first, parts):
        send_first(m)
    for n in range(chunks):
        swap(n).start()
    for copy in own_weights:
        copy.start()

    squares = (group * wide_slots, group * wide_slots)
    diagonal = lax.broadcasted_iota(jnp.int32, squares, 0) == lax.broadcasted_iota(jnp.int32, squares, 1)

    def as_column(row):
        return jnp.sum(jnp.where(diagonal, jnp.broadcast_to(row, squares), 0), axis=1, keepdims=True)

    code_column = as_column(code)
    found = lax.broadcasted_iota(jnp.int32, (group * wide_slots, lines), 1) == code_column
    picker[...] = jnp.where(found, 1.0, 0.0).astype(jnp.bfloat16)

    step = 4 if cap % 4 == 0 else cap
    blocks = cap // step
    scale = 1.0 / HD**0.5
    turn = jnp.zeros_like(rank)
    for b in range(1, blocks):
        turn = turn + jnp.where(rank >= b * step, 1, 0)

    end_code = as_column(slot_codes(jnp.where(z == nb - 2, nb - 1, 0))[2])
    found_end = lax.broadcasted_iota(jnp.int32, hub_picker.shape, 1) == end_code
    hub_picker[...] = jnp.where(found_end, 1.0, 0.0).astype(jnp.bfloat16)
    at_end = (z == 0) | (z == nb - 1)

    @pl.when(at_end)
    def _():
        returned[...] = jnp.zeros_like(returned)

    @pl.when(jnp.logical_not(at_end))
    def _():
        merged_in[...] = jnp.zeros_like(merged_in)

    row_column = as_column(jnp.where(source >= 0, source * 8 + turn, -1))
    found_row = lax.broadcasted_iota(jnp.int32, row_picker.shape, 1) == row_column
    row_picker[...] = jnp.where(found_row, 1.0, 0.0).astype(jnp.bfloat16)
    key_column = as_column((rank - turn * step) * heads + lane // wide_slots)
    lane_key[...] = jnp.broadcast_to(key_column, lane_key.shape)
    own_copies[1].wait()
    own_copies[2].wait()
    head_lane = lax.broadcasted_iota(jnp.int32, own_scores.shape, 1)
    mine_scores = jnp.zeros(own_scores.shape, jnp.float32)
    for h in range(kvl):
        products = query_stack(h) * repeated(key_rows_in, h)
        one_head = jnp.sum(products, axis=1, keepdims=True) * scale
        mine_scores = jnp.where(head_lane == h, one_head, mine_scores)
    own_scores[...] = mine_scores
    peaks_out[...] = jnp.zeros_like(peaks_out)

    low = z * slots

    def list_served(d, carry):
        upcoming = jnp.int32(slots)
        follow[slots] = upcoming
        for p in reversed(range(slots)):
            a = ancestry_ref[d * slots + p]
            upcoming = jnp.where((a >= low) & (a < low + slots), p, upcoming)
            follow[p] = upcoming
        at = follow[0]
        for r in range(cap):
            chosen[d * cap + r] = jnp.minimum(at, slots - 1)
            at = follow[jnp.minimum(at + 1, slots)]
        return carry

    lax.fori_loop(0, nb, list_served, 0)

    own_copies[3].wait()
    own_copies[4].wait()
    own_mail.wait()

    def line_step(k, split=False):
        r, m = k // parts + 1, k % parts

        def arrived(direction, has_next, piece):
            later_hop(direction, r - 1, m, piece).wait_recv()

            @pl.when(has_next)
            def _():
                if split:
                    for f in range(ends):
                        end_hop(direction, f).start()
                else:
                    later_hop(direction, r, m, piece).start()

            twin_copy(piece, m, cross).start()

        @pl.when(z - r >= 0)
        def _():
            arrived(0, z + 1 < nb, z - r)

        @pl.when(z + r < nb)
        def _():
            arrived(1, z > 0, z + r)

    def end_step():
        def arrived(direction, piece):
            for f in range(ends):
                end_hop(direction, f).wait_recv()
                if f < swapped:
                    end_twin(piece, f, cross).start()

        @pl.when(z == nb - 1)
        def _():
            arrived(0, 0)

        @pl.when(z == 0)
        def _():
            arrived(1, nb - 1)

    context = page_count * keys.shape[1]
    serve_turns = nb * blocks
    turns = serve_turns + row_chunks
    early = (nb - 2) * parts

    def steps_of_turn(i, final=False):
        spare = 1 if final else 0
        if early % turns == 0:
            for u in range(early // turns - spare):
                line_step(i * (early // turns) + u)
        else:

            def one(k, carry):
                line_step(k)
                return carry

            lax.fori_loop(i * early // turns, (i + 1) * early // turns - spare, one, 0)
        if final:
            line_step(early - 1, split=True)

    position = lax.broadcasted_iota(jnp.int32, (heads, context), 1)

    def serve(d, r, letters, u):
        p = chosen[d * cap + r]
        pages = [pages_ref[i, p] for i in range(page_count)]
        length = lengths_ref[low + p]
        key_block = jnp.concatenate([keys[page] for page in pages], axis=0)
        value_block = jnp.concatenate([values[page] for page in pages], axis=0)
        mine = [letter[u * group : (u + 1) * group] for letter in letters]
        nothing = jnp.zeros((group, HD), jnp.float32)
        wide = jnp.concatenate(
            [
                jnp.concatenate([mine[h] if g == h else nothing for g in range(kvl)], axis=1)
                for h in range(kvl)
            ],
            axis=0,
        ).astype(jnp.bfloat16)
        scores = (
            lax.dot_general(
                wide, key_block, (((1,), (1,)), ((), ())), preferred_element_type=jnp.float32
            )
            * scale
        )
        scores = jnp.where(position < length, scores, -1e30)
        top = jnp.max(scores, axis=1, keepdims=True)
        w = jnp.exp(scores - top)
        den = jnp.sum(w, axis=1, keepdims=True)
        everything = jnp.dot(w.astype(jnp.bfloat16), value_block, preferred_element_type=jnp.float32)
        answers = []
        for h in range(kvl):
            rows = slice(h * group, (h + 1) * group)
            answers.append(everything[rows, h * HD : (h + 1) * HD] / den[rows])
        return answers, top + jnp.log(den)

    peak_square = (step * heads, HD)
    peak_diagonal = lax.broadcasted_iota(jnp.int32, peak_square, 0) == lax.broadcasted_iota(
        jnp.int32, peak_square, 1
    )

    def serve_block(i, carry):
        steps_of_turn(i)
        away = i // blocks
        d = lax.rem(z + away, nb)
        r0 = lax.rem(i, blocks) * step

        @pl.when((lax.rem(i, blocks) == 0) & (away > 0))
        def _():
            mail(nb - away).wait_recv()

        some = pl.ds(pl.multiple_of(r0 * group, step * group), step * group)
        letters = [mail_in[d, h, some].astype(jnp.float32) for h in range(kvl)]
        results = [serve(d, r0 + u, letters, u) for u in range(step)]
        for h in range(kvl):
            served_out[d, h, some] = jnp.concatenate([result[0][h] for result in results], axis=0).astype(
                jnp.bfloat16
            )
        peak_column = jnp.concatenate([result[1] for result in results], axis=0)
        spread_peaks = jnp.where(peak_diagonal, jnp.broadcast_to(peak_column, peak_square), 0.0)
        peaks_out[d, pl.ds(lax.rem(i, blocks), 1)] = jnp.sum(spread_peaks, axis=0, keepdims=True)
        return carry

    lax.fori_loop(0, serve_turns, serve_block, 0)
    own_back = pltpu.make_async_copy(served_out.at[z], returned.at[z], local_sem.at[9])
    own_back.start()
    for d in range(1, nb):
        pl.when(inside(d))(lambda d=d: back(d).start())
    pl.when(z < nb - 2)(lambda: to_hub(nb - 1).start())
    pl.when(z > 1)(lambda: to_hub(0).start())

    features = row_width * mp
    pieces_per_block = row_width // depth
    fine = min(16, per_chunk)

    def row_step(i):
        for d in range(1, mp):
            row_copy(d, i).wait_recv()

        def normalise(j, carry):
            start = pl.multiple_of(i * per_chunk + j * fine, fine)
            part = pl.ds(start, fine)
            power = jnp.zeros((fine, 1), jnp.float32)
            for b in range(mp):
                block = raw[b, part].astype(jnp.float32)
                power = power + jnp.sum(block * block, axis=1, keepdims=True)
            factor = lax.rsqrt(power / features + 1e-06)
            for b in range(mp):
                block = raw[b, part].astype(jnp.float32)
                gain = gain_ref[:, b * row_width : (b + 1) * row_width]
                result = (block * factor * gain).astype(jnp.bfloat16)
                for p in range(pieces_per_block):
                    normed[c, b * pieces_per_block + p, part] = result[:, p * depth : (p + 1) * depth]
            return carry

        lax.fori_loop(0, per_chunk // fine, normalise, 0)
        norm_copy(i).start()

    own_copies[5].wait()
    own_copies[7].wait()
    for i in range(row_chunks):
        steps_of_turn(serve_turns + i, final=i == row_chunks - 1)
        row_step(i)
    for i in range(row_chunks):
        norm_copy(i).wait_recv()
    own_copies[6].wait()

    def multiply(piece, kind, n, fresh=False):
        here = slice(n * chunk, (n + 1) * chunk)
        for side in range(2):
            product = jnp.dot(
                normed[side, piece * ns + kind], weights[piece, kind, n], preferred_element_type=jnp.float32
            )
            if fresh:
                total[side, :, here] = bias_ref[:, columns(c, n)] + product
            else:
                total[side, :, here] += product

    def multiply_own(n):
        own_weights[n].wait()
        swap(n).wait_recv()
        multiply(z, 0, n, fresh=True)
        multiply(z, 1, n)

    def multiply_at(r, n, ended=0):
        def both(piece, direction):
            multiply(piece, cross, n)
            for j in range(cuts - ended):
                twin_copy(piece, n * cuts + j, 1 - cross).wait_recv()
            for f in range(swapped * ended):
                end_twin(piece, f, 1 - cross).wait_recv()
            if ended:
                for f in range(swapped, ends):
                    end_other(direction, f).wait_recv()
            multiply(piece, 1 - cross, n)

        def left():
            both(z - r, 0)

        def right():
            both(z + r, 1)

        pl.when(z - r >= 0)(left)
        pl.when(z + r < nb)(right)

    def near(n):
        multiply_own(n)

        def one(r, carry):
            multiply_at(r, n)
            return carry

        lax.fori_loop(1, nb - 1, one, 0)

    def last(n):
        multiply_at(nb - 1, n, ended=1 if n == chunks - 1 else 0)
        class_part = class_ref[:, columns(c, n)]
        here = slice(n * chunk, (n + 1) * chunk)
        for side in range(2):
            hidden = jnp.maximum(total[side, :, here], 0.0).astype(jnp.bfloat16)
            sums = lax.dot_general(
                class_part, hidden, (((1,), (1,)), ((), ())), preferred_element_type=jnp.float32
            )
            if n == 0:
                partial[side, 0:2] = sums
            else:
                partial[side, 0:2] += sums

    partial[...] = jnp.zeros_like(partial)
    plan = [[] for _ in range(parts + 1)]
    for n in range(chunks):
        plan[n * (parts // 2) // chunks].append(functools.partial(near, n))
    for n in range(chunks):
        when = (n + 1) * cuts + cuts
        plan[when if parts // 2 <= when < parts else parts].append(functools.partial(last, n))
    for m in range(parts):
        if m < parts - 1:
            line_step(early + m)
        else:
            end_step()
        for unit in plan[m]:
            unit()
        if m == parts - dims["late"]:
            for d in range(1, nb):
                peak_back(d).start()
            pl.when(z == nb - 2)(lambda: merge(nb - 1))
            pl.when(z == 1)(lambda: merge(0))
    for unit in plan[parts]:
        unit()

    pairs = [(d, e) for d in range(mp) for e in range(2) if d or e]
    for d, e in pairs:
        sum_copy(d, e).start()

    own_back.wait()
    for d in range(1, nb):
        peak_back(d).wait_recv()

    @pl.when(jnp.logical_not(at_end))
    def _():
        for d in range(1, nb):
            back(d).wait_recv()

    pl.when(at_end)(lambda: merged_copy(nb - 2).wait_recv())
    peaks_in[z] = peaks_out[z]
    rest = peaks_in[...].reshape(nb * 8, HD)
    picked = jnp.zeros((group * wide_slots, HD), jnp.float32)
    for _ in range(3):
        coarse = rest.astype(jnp.bfloat16)
        picked = picked + jnp.dot(row_picker[...], coarse, preferred_element_type=jnp.float32)
        rest = rest - coarse.astype(jnp.float32)
    for h in range(kvl):
        here = lax.broadcasted_iota(jnp.int32, picked.shape, 1) == lane_key[...] + h * group
        peak = jnp.sum(jnp.where(here, picked, 0.0), axis=1, keepdims=True)
        share = 1.0 / (1.0 + jnp.exp(own_scores[:, h : h + 1] - peak))
        answers = returned[:, h].reshape(lines, HD)
        mine = jnp.dot(picker[...], answers, preferred_element_type=jnp.float32)
        merged = merged_in[h].astype(jnp.float32)
        mine = mine + stack([merged[g * slots : (g + 1) * slots] for g in range(group)])
        mine = (mine * share + repeated(value_rows_in, h) * (1.0 - share)).astype(jnp.bfloat16)
        for g in range(group):
            at = (h * group + g) * HD
            attention_ref[:, at : at + HD] = mine[g * wide_slots : g * wide_slots + slots]
    attention_out = pltpu.make_async_copy(attention_ref, attention_hbm, small_sem.at[0])
    attention_out.start()

    logits = partial[c]
    for d, e in pairs:
        sum_copy(d, e).wait_recv()
        logits = logits + logits_in[d * 2 + e]
    odds_ref[...] = (logits[1:2] + class_bias_ref[1]) - (logits[0:1] + class_bias_ref[0])
    odds_out = pltpu.make_async_copy(odds_ref, odds_hbm, small_sem.at[1])
    odds_out.start()

    for d in range(1, nb):
        mail(d).wait_send()
        pl.when(inside(d))(lambda d=d: back(d).wait_send())
        peak_back(d).wait_send()
    pl.when(z < nb - 2)(lambda: to_hub(nb - 1).wait_send())
    pl.when(z > 1)(lambda: to_hub(0).wait_send())
    def drain_hub(end):
        merged_copy(end).wait_send()
        for f in range(swapped, ends):
            end_other(0 if end else 1, f).wait_send()

    pl.when(z == nb - 2)(lambda: drain_hub(nb - 1))
    pl.when(z == 1)(lambda: drain_hub(0))
    for i in range(row_chunks):
        for d in range(1, mp):
            row_copy(d, i).wait_send()
        norm_copy(i).wait_send()
    for d, e in pairs:
        sum_copy(d, e).wait_send()
    for n in range(chunks):
        swap(n).wait_send()

    def drain_first(m, carry):
        @pl.when(z < nb - 1)
        def _():
            first_hop(0, m).wait_send()

        @pl.when(z > 0)
        def _():
            first_hop(1, m).wait_send()

        return carry

    lax.fori_loop(0, parts, drain_first, 0)

    def drain(k, carry, split=False):
        r, m = k // parts + 1, k % parts

        def sent(direction, has_next, piece):
            @pl.when(has_next)
            def _():
                if split:
                    for f in range(ends):
                        end_hop(direction, f).wait_send()
                else:
                    later_hop(direction, r, m, piece).wait_send()

            twin_copy(piece, m, cross).wait_send()

        @pl.when(z - r >= 0)
        def _():
            sent(0, z + 1 < nb, z - r)

        @pl.when(z + r < nb)
        def _():
            sent(1, z > 0, z + r)

        return carry

    lax.fori_loop(0, early - 1, drain, 0)
    drain(early - 1, 0, split=True)
    lax.fori_loop(early, early + parts - 1, drain, 0)

    @pl.when(z == nb - 1)
    def _():
        for f in range(swapped):
            end_twin(0, f, cross).wait_send()

    @pl.when(z == 0)
    def _():
        for f in range(swapped):
            end_twin(nb - 1, f, cross).wait_send()

    attention_out.wait()
    odds_out.wait()


def per_device(
    queries,
    new_keys,
    new_values,
    key_pages,
    value_pages,
    page_table,
    ancestry,
    lengths,
    step_rows,
    norm_gain,
    head_weight,
    head_bias,
    class_weight,
    class_bias,
):
    slot_count, page_count = page_table.shape
    kv_width = key_pages.shape[3]
    kvl = kv_width // HD
    group = queries.shape[2] // kv_width
    nb, ng = lax.axis_size("batch"), lax.axis_size("group")
    mp, ns = lax.axis_size("mp"), lax.axis_size("section")
    assert ng == 2 and ns == 2 and nb >= 4 and queries.shape[0] == 1
    cap = max(2, (2 * slot_count + nb - 1) // nb)
    wide_slots = (slot_count + 15) // 16 * 16

    row_count, row_width = step_rows.shape
    depth, width = head_weight.shape
    half = width // ns
    chunk = min(256, half)
    chunks = half // chunk
    cuts = 2
    parts = chunks * cuts
    ends = max(1, min(4, depth // cuts // 16))
    row_chunks = 4
    dims = dict(
        nb=nb, mp=mp, ns=ns, cap=cap, page_count=page_count, kvl=kvl, group=group, slots=slot_count,
        wide_slots=wide_slots, half=half, chunk=chunk, chunks=chunks, depth=depth, row_chunks=row_chunks,
        cuts=cuts, ends=ends, doubled=min(2, ends - 1), first=2, late=3,
    )
    anywhere = pl.BlockSpec(memory_space=pl.ANY)
    bf16, f32, i32 = jnp.bfloat16, jnp.float32, jnp.int32
    sems = pltpu.SemaphoreType.DMA
    answers = (nb, kvl, cap * group, HD)
    attention, odds = pl.pallas_call(
        functools.partial(fused_kernel, dims),
        out_shape=(
            jax.ShapeDtypeStruct((slot_count, kvl * group * HD), bf16),
            jax.ShapeDtypeStruct((1, row_count), f32),
        ),
        in_specs=[anywhere] * 14,
        out_specs=(anywhere, anywhere),
        scratch_shapes=[
            pltpu.SMEM(ancestry.shape, i32),
            pltpu.SMEM(lengths.shape, i32),
            pltpu.SMEM((page_count, slot_count), i32),
            pltpu.SMEM(class_bias.shape, f32),
            pltpu.VMEM((2, width), bf16),
            pltpu.VMEM((slot_count, kvl * group * HD), bf16),
            pltpu.VMEM((1, row_count), f32),
            pltpu.SMEM((slot_count + 1,), i32),
            pltpu.SMEM((nb * cap,), i32),
            pltpu.VMEM(queries.shape[1:], bf16),
            pltpu.VMEM(new_keys.shape[1:], bf16),
            pltpu.VMEM(new_values.shape[1:], bf16),
            pltpu.VMEM((1, row_width * mp), f32),
            pltpu.VMEM((1, width), f32),
            pltpu.VMEM((group * wide_slots, nb * cap * group), bf16),
            pltpu.VMEM((group * wide_slots, nb * 8), bf16),
            pltpu.VMEM((group * wide_slots, HD), i32),
            pltpu.VMEM((group * wide_slots, HD), f32),
            pltpu.VMEM((nb, 8, HD), f32),
            pltpu.VMEM((nb, 8, HD), f32),
            pltpu.VMEM(answers, bf16),
            pltpu.VMEM(answers, bf16),
            pltpu.VMEM(answers, bf16),
            pltpu.VMEM(answers, bf16),
            pltpu.VMEM(key_pages.shape[1:], bf16),
            pltpu.VMEM(key_pages.shape[1:], bf16),
            pltpu.VMEM((mp, row_count, row_width), bf16),
            pltpu.VMEM((2, nb * ns, row_count, depth), bf16),
            pltpu.VMEM((nb, ns, chunks, depth, chunk), bf16),
            pltpu.VMEM((2, row_count, half), f32),
            pltpu.VMEM((2, 8, row_count), f32),
            pltpu.VMEM((2 * mp, 8, row_count), f32),
            pltpu.SemaphoreType.REGULAR((2,)),
            sems((5,)),
            sems((10,)),
            sems((chunks,)),
            sems((nb,)),
            sems((nb,)),
            sems((nb,)),
            sems((nb,)),
            sems((2, nb, parts)),
            sems((2, nb, parts)),
            sems((nb, parts)),
            sems((nb, parts)),
            sems((chunks,)),
            sems((chunks,)),
            sems((mp, row_chunks)),
            sems((mp, row_chunks)),
            sems((row_chunks,)),
            sems((row_chunks,)),
            sems((2 * mp,)),
            sems((2 * mp,)),
            sems((2, ends)),
            sems((2, ends)),
            sems((ends,)),
            sems((ends,)),
            sems((nb,)),
            sems((nb,)),
            pltpu.VMEM((group * wide_slots, nb * cap * group), bf16),
            pltpu.VMEM(answers, bf16),
            pltpu.VMEM((kvl, group * slot_count, HD), bf16),
            pltpu.VMEM((kvl, group * slot_count, HD), bf16),
            sems((2,)),
            sems((nb,)),
            sems,
            sems,
            sems((ends,)),
            sems((ends,)),
        ],
        compiler_params=pltpu.CompilerParams(
            collective_id=0, has_side_effects=True, vmem_limit_bytes=60 * 1024 * 1024
        ),
        name="filter_round",
    )(
        ancestry,
        lengths,
        page_table.T,
        class_bias,
        queries,
        new_keys,
        new_values,
        key_pages,
        value_pages,
        step_rows,
        norm_gain.reshape(1, -1),
        head_weight,
        head_bias.reshape(1, -1),
        class_weight.T,
    )
    return attention.reshape(1, slot_count, -1), odds.reshape(-1)


def solution(mesh):
    placed = (
        P("section", ("group", "batch"), "mp"),
        P("section", ("group", "batch"), "mp"),
        P("section", ("group", "batch"), "mp"),
        P("section", ("group", "batch"), None, "mp"),
        P("section", ("group", "batch"), None, "mp"),
        P(("group", "batch"), None),
        P("group"),
        P("group"),
        P(("group", "batch", "section"), "mp"),
        P(),
        P(("batch", "section"), "mp"),
        P("mp"),
        P("mp", None),
        P(),
    )
    return jax.shard_map(
        per_device,
        mesh=mesh,
        in_specs=placed,
        out_specs=(P("section", ("group", "batch"), "mp"), P(("group", "batch", "section"))),
        check_vma=False,
    )
```

```python
import functools

import jax
import jax.numpy as jnp
from jax import lax
from jax.experimental import pallas as pl
from jax.experimental.pallas import tpu as pltpu
from jax.sharding import PartitionSpec as P

HD = 128
MESH = pl.DeviceIdType.MESH


def fused_kernel(
    dims,
    ancestry_hbm,
    lengths_hbm,
    pages_hbm,
    class_bias_hbm,
    queries_hbm,
    new_keys_hbm,
    new_values_hbm,
    keys_hbm,
    values_hbm,
    rows_hbm,
    gain_hbm,
    weight_hbm,
    bias_hbm,
    class_hbm,
    attention_hbm,
    odds_hbm,
    ancestry_ref,
    lengths_ref,
    pages_ref,
    class_bias_ref,
    class_ref,
    attention_ref,
    odds_ref,
    follow,
    chosen,
    letter_rows,
    key_rows_in,
    value_rows_in,
    gain_ref,
    bias_ref,
    picker,
    row_picker,
    lane_key,
    own_scores,
    peaks_out,
    peaks_in,
    mail_out,
    mail_in,
    served_out,
    returned,
    keys,
    values,
    raw,
    normed,
    weights,
    total,
    partial,
    logits_in,
    relay,
    small_sem,
    local_sem,
    weight_sem,
    mail_send,
    mail_recv,
    back_send,
    back_recv,
    line_send,
    line_recv,
    twin_send,
    twin_recv,
    swap_send,
    swap_recv,
    row_send,
    row_recv,
    norm_send,
    norm_recv,
    sum_send,
    sum_recv,
    end_send,
    end_recv,
    end_twin_send,
    end_twin_recv,
    peak_send,
    peak_recv,
    hub_picker,
    hub_in,
    merged_out,
    merged_in,
    hub_send,
    hub_recv,
    merged_send,
    merged_recv,
    both_send,
    both_recv,
    staged,
    stage_sem,
):
    nb, mp, ns = dims["nb"], dims["mp"], dims["ns"]
    cap, page_count, kvl, group = dims["cap"], dims["page_count"], dims["kvl"], dims["group"]
    half, chunk, chunks, depth = dims["half"], dims["chunk"], dims["chunks"], dims["depth"]
    row_chunks, cuts, first = dims["row_chunks"], dims["cuts"], dims["first"]
    slots, wide_slots = dims["slots"], dims["wide_slots"]
    heads = kvl * group
    sub = depth // cuts
    ends, swapped = dims["ends"], dims["ends"] - dims["doubled"]
    parts = chunks * cuts
    z, y = lax.axis_index("batch"), lax.axis_index("group")
    x, c = lax.axis_index("mp"), lax.axis_index("section")
    other = 1 - c
    twin = 1 - y
    cross = lax.rem(c + y, 2)
    row_count, row_width = rows_hbm.shape
    per_chunk = row_count // row_chunks

    def remote(src, dst, send, recv, device):
        return pltpu.make_async_remote_copy(
            src_ref=src, dst_ref=dst, send_sem=send, recv_sem=recv, device_id=device, device_id_type=MESH
        )

    def columns(owner, n):
        return pl.ds(pl.multiple_of(owner * half + n * chunk, chunk), chunk)

    barrier = pltpu.get_barrier_semaphore()

    def greet(device):
        pl.semaphore_signal(barrier, inc=1, device_id=device, device_id_type=MESH)

    @pl.when(z > 0)
    def _():
        greet({"batch": z - 1})
        greet({"batch": z - 1, "section": other})

    @pl.when(z < nb - 1)
    def _():
        greet({"batch": z + 1})
        greet({"batch": z + 1, "section": other})

    greet({"section": other})
    greet({"group": twin})
    for d in range(1, mp):
        peer = lax.rem(x + d, mp)
        greet({"mp": peer})
        greet({"mp": peer, "section": other})

    own_copies = [
        pltpu.make_async_copy(queries_hbm.at[0], letter_rows, local_sem.at[0]),
        pltpu.make_async_copy(new_keys_hbm.at[0], key_rows_in, local_sem.at[1]),
        pltpu.make_async_copy(new_values_hbm.at[0], value_rows_in, local_sem.at[2]),
        pltpu.make_async_copy(keys_hbm.at[0], keys, local_sem.at[3]),
        pltpu.make_async_copy(values_hbm.at[0], values, local_sem.at[4]),
        pltpu.make_async_copy(gain_hbm, gain_ref, local_sem.at[5]),
        pltpu.make_async_copy(bias_hbm, bias_ref, local_sem.at[6]),
        pltpu.make_async_copy(rows_hbm, raw.at[x], local_sem.at[7]),
    ]
    small_copies = [
        pltpu.make_async_copy(src, dst, small_sem.at[i])
        for i, (src, dst) in enumerate(
            [
                (ancestry_hbm, ancestry_ref),
                (lengths_hbm, lengths_ref),
                (pages_hbm, pages_ref),
                (class_bias_hbm, class_bias_ref),
                (class_hbm, class_ref),
            ]
        )
    ]
    staging = [
        pltpu.make_async_copy(weight_hbm.at[:, columns(cross, n)], staged.at[n], stage_sem.at[n])
        for n in range(chunks)
    ]
    for copy in staging + small_copies + own_copies:
        copy.start()

    neighbours = jnp.where(z > 0, 1, 0) + jnp.where(z < nb - 1, 1, 0)
    pl.semaphore_wait(barrier, 2 + 2 * (mp - 1) + 2 * neighbours)

    def mail(d):
        target = lax.rem(z + d, nb)
        return remote(mail_out.at[target], mail_in.at[z], mail_send.at[d], mail_recv.at[d], {"batch": target})

    def back(d):
        target = lax.rem(z + d, nb)
        return remote(
            served_out.at[target], returned.at[z], back_send.at[d], back_recv.at[d], {"batch": target}
        )

    def inside(d):
        target = lax.rem(z + d, nb)
        return (target > 0) & (target < nb - 1)

    def to_hub(end):
        hub = nb - 2 if end else 1
        return remote(
            served_out.at[end],
            hub_in.at[z],
            hub_send.at[1 if end else 0],
            hub_recv.at[z],
            {"batch": hub},
        )

    def from_hub_source(origin):
        return remote(
            served_out.at[0], hub_in.at[origin], hub_send.at[0], hub_recv.at[origin], {"batch": z - 1}
        )

    def merged_copy(end):
        return remote(merged_out, merged_in, merged_send, merged_recv, {"batch": end})

    def merge(end):
        hub = nb - 2 if end else 1
        for f in range(swapped, ends):
            end_other(0 if end else 1, f).start()
        for origin in range(nb):
            if origin not in (end, hub):
                from_hub_source(origin).wait_recv()
        hub_in[end] = jnp.zeros(hub_in.shape[1:], hub_in.dtype)
        hub_in[hub] = served_out[end]
        for h in range(kvl):
            answers = hub_in[:, h].reshape(nb * cap * group, HD)
            mine = jnp.dot(hub_picker[...], answers, preferred_element_type=jnp.float32)
            merged_out[h] = jnp.concatenate(
                [mine[g * wide_slots : g * wide_slots + slots] for g in range(group)], axis=0
            ).astype(jnp.bfloat16)
        merged_copy(end).start()

    def peak_back(d):
        target = lax.rem(z + d, nb)
        return remote(
            peaks_out.at[target], peaks_in.at[z], peak_send.at[d], peak_recv.at[d], {"batch": target}
        )

    def row_copy(d, i):
        target = lax.rem(x + d, mp)
        part = pl.ds(i * per_chunk, per_chunk)
        return remote(
            rows_hbm.at[part], raw.at[x, part], row_send.at[d, i], row_recv.at[d, i], {"mp": target}
        )

    def swap(n):
        return remote(
            weight_hbm.at[:, columns(other, n)],
            weights.at[z, c, n],
            swap_send.at[n],
            swap_recv.at[n],
            {"section": other},
        )

    def piece_rows(m):
        return pl.ds(pl.multiple_of((m % cuts) * sub, sub), sub)

    def first_hop(direction, m):
        return remote(
            staged.at[m // cuts, piece_rows(m)],
            weights.at[z, c, m // cuts, piece_rows(m)],
            line_send.at[direction, 0, m],
            line_recv.at[direction, 0, m],
            {"batch": z + (1 if direction == 0 else -1), "section": cross},
        )

    def later_hop(direction, hop, m, piece):
        place = weights.at[piece, cross, m // cuts, piece_rows(m)]
        return remote(
            place,
            place,
            line_send.at[direction, hop, m],
            line_recv.at[direction, hop, m],
            {"batch": z + (1 if direction == 0 else -1)},
        )

    def twin_copy(piece, m, kind):
        place = weights.at[piece, kind, m // cuts, piece_rows(m)]
        return remote(place, place, twin_send.at[piece, m], twin_recv.at[piece, m], {"group": twin})

    def end_place(piece, kind, f):
        return weights.at[piece, kind, chunks - 1, pl.ds(depth - sub + f * (sub // ends), sub // ends)]

    def end_hop(direction, f):
        place = end_place(0 if direction == 0 else nb - 1, cross, f)
        return remote(
            place,
            place,
            end_send.at[direction, f],
            end_recv.at[direction, f],
            {"batch": z + (1 if direction == 0 else -1)},
        )

    def end_twin(piece, f, kind):
        place = end_place(piece, kind, f)
        return remote(place, place, end_twin_send.at[f], end_twin_recv.at[f], {"group": twin})

    def end_other(direction, f):
        place = end_place(0 if direction == 0 else nb - 1, 1 - cross, f)
        return remote(
            place, place, both_send.at[f], both_recv.at[f], {"batch": z + (1 if direction == 0 else -1)}
        )

    def norm_copy(i):
        part = pl.ds(i * per_chunk, per_chunk)
        return remote(
            normed.at[c, :, part],
            normed.at[c, :, part],
            norm_send.at[i],
            norm_recv.at[i],
            {"section": other},
        )

    def sum_copy(d, e):
        peer, side = lax.rem(x + d, mp), lax.rem(c + e, 2)
        return remote(
            partial.at[side],
            logits_in.at[d * 2 + e],
            sum_send.at[d * 2 + e],
            sum_recv.at[d * 2 + e],
            {"mp": peer, "section": side},
        )

    own_weights = [
        pltpu.make_async_copy(weight_hbm.at[:, columns(c, n)], weights.at[z, c, n], weight_sem.at[n])
        for n in range(chunks)
    ]

    def send_first(m):
        @pl.when(z < nb - 1)
        def _():
            first_hop(0, m).start()

        @pl.when(z > 0)
        def _():
            first_hop(1, m).start()

    for copy in staging[: (first + cuts - 1) // cuts]:
        copy.wait()
    for m in range(first):
        send_first(m)
    for i in range(row_chunks):
        for d in range(1, mp):
            row_copy(d, i).start()

    def pass_on(side, has_before, has_after, after):
        @pl.when(has_before)
        def _():
            pl.semaphore_wait(relay.at[side], 1)

        @pl.when(has_after)
        def _():
            pl.semaphore_signal(
                relay.at[side], inc=1, device_id={"batch": after}, device_id_type=MESH
            )

    def pass_right():
        pass_on(0, z > 0, z < nb - 1, z + 1)

    def pass_left():
        pass_on(1, z < nb - 1, z > 0, z - 1)

    @pl.when(z < nb // 2)
    def _():
        pass_right()
        pass_left()

    @pl.when(z >= nb // 2)
    def _():
        pass_left()
        pass_right()

    for copy in small_copies:
        copy.wait()
    lane = lax.broadcasted_iota(jnp.int32, (1, group * wide_slots), 1)
    slot_of_lane = lane % wide_slots


    def slot_codes(owner):
        ancestor = jnp.full((1, group * wide_slots), -1, jnp.int32)
        for p in range(slots):
            ancestor = jnp.where(slot_of_lane == p, ancestry_ref[owner * slots + p], ancestor)
        source = jnp.zeros_like(ancestor)
        for d in range(1, nb):
            source = source + jnp.where(ancestor >= d * slots, 1, 0)
        source = jnp.where(ancestor >= 0, source, -1)
        spread = jnp.broadcast_to(source, (wide_slots, group * wide_slots))
        row_at = lax.broadcasted_iota(jnp.int32, spread.shape, 0)
        lane_at = lax.broadcasted_iota(jnp.int32, spread.shape, 1)
        source_column = jnp.sum(jnp.where(row_at == lane_at, spread, 0), axis=1, keepdims=True)
        before = (source_column == spread) & (row_at < lane_at % wide_slots)
        rank = jnp.sum(jnp.where(before, 1, 0), axis=0, keepdims=True)
        code = jnp.where(source >= 0, (source * cap + rank) * group + lane // wide_slots, -1)
        return source, rank, code

    source, rank, code = slot_codes(z)
    lines = nb * cap * group
    wanted = lax.broadcasted_iota(jnp.int32, (lines, group * wide_slots), 0) == code
    requests = jnp.where(wanted, 1.0, 0.0).astype(jnp.bfloat16)

    own_copies[0].wait()

    def stack(blocks_of):
        filler = jnp.zeros((wide_slots - slots, HD), jnp.float32)
        tall = [part for g in blocks_of for part in ((g, filler) if wide_slots > slots else (g,))]
        return jnp.concatenate(tall, axis=0)

    def query_stack(h):
        start = h * group
        return stack(
            [letter_rows[:, (start + g) * HD : (start + g + 1) * HD].astype(jnp.float32) for g in range(group)]
        )

    def repeated(ref, h):
        return stack([ref[:, h * HD : (h + 1) * HD].astype(jnp.float32)] * group)

    for h in range(kvl):
        tall = query_stack(h).astype(jnp.bfloat16)
        packed = jnp.dot(requests, tall, preferred_element_type=jnp.float32).astype(jnp.bfloat16)
        for s in range(nb):
            mail_out[s, h] = packed[s * cap * group : (s + 1) * cap * group]
    for d in range(1, nb):
        mail(d).start()
    own_mail = pltpu.make_async_copy(mail_out.at[z], mail_in.at[z], local_sem.at[8])
    own_mail.start()
    for copy in staging[(first + cuts - 1) // cuts :]:
        copy.wait()
    for m in range(first, parts):
        send_first(m)
    for n in range(chunks):
        swap(n).start()
    for copy in own_weights:
        copy.start()

    squares = (group * wide_slots, group * wide_slots)
    diagonal = lax.broadcasted_iota(jnp.int32, squares, 0) == lax.broadcasted_iota(jnp.int32, squares, 1)

    def as_column(row):
        return jnp.sum(jnp.where(diagonal, jnp.broadcast_to(row, squares), 0), axis=1, keepdims=True)

    code_column = as_column(code)
    found = lax.broadcasted_iota(jnp.int32, (group * wide_slots, lines), 1) == code_column
    picker[...] = jnp.where(found, 1.0, 0.0).astype(jnp.bfloat16)

    step = 4 if cap % 4 == 0 else cap
    blocks = cap // step
    scale = 1.0 / HD**0.5
    turn = jnp.zeros_like(rank)
    for b in range(1, blocks):
        turn = turn + jnp.where(rank >= b * step, 1, 0)

    end_code = as_column(slot_codes(jnp.where(z == nb - 2, nb - 1, 0))[2])
    found_end = lax.broadcasted_iota(jnp.int32, hub_picker.shape, 1) == end_code
    hub_picker[...] = jnp.where(found_end, 1.0, 0.0).astype(jnp.bfloat16)
    at_end = (z == 0) | (z == nb - 1)

    @pl.when(at_end)
    def _():
        returned[...] = jnp.zeros_like(returned)

    @pl.when(jnp.logical_not(at_end))
    def _():
        merged_in[...] = jnp.zeros_like(merged_in)

    row_column = as_column(jnp.where(source >= 0, source * 8 + turn, -1))
    found_row = lax.broadcasted_iota(jnp.int32, row_picker.shape, 1) == row_column
    row_picker[...] = jnp.where(found_row, 1.0, 0.0).astype(jnp.bfloat16)
    key_column = as_column((rank - turn * step) * heads + lane // wide_slots)
    lane_key[...] = jnp.broadcast_to(key_column, lane_key.shape)
    own_copies[1].wait()
    own_copies[2].wait()
    head_lane = lax.broadcasted_iota(jnp.int32, own_scores.shape, 1)
    mine_scores = jnp.zeros(own_scores.shape, jnp.float32)
    for h in range(kvl):
        products = query_stack(h) * repeated(key_rows_in, h)
        one_head = jnp.sum(products, axis=1, keepdims=True) * scale
        mine_scores = jnp.where(head_lane == h, one_head, mine_scores)
    own_scores[...] = mine_scores
    peaks_out[...] = jnp.zeros_like(peaks_out)

    low = z * slots

    def list_served(d, carry):
        upcoming = jnp.int32(slots)
        follow[slots] = upcoming
        for p in reversed(range(slots)):
            a = ancestry_ref[d * slots + p]
            upcoming = jnp.where((a >= low) & (a < low + slots), p, upcoming)
            follow[p] = upcoming
        at = follow[0]
        for r in range(cap):
            chosen[d * cap + r] = jnp.minimum(at, slots - 1)
            at = follow[jnp.minimum(at + 1, slots)]
        return carry

    lax.fori_loop(0, nb, list_served, 0)

    own_copies[3].wait()
    own_copies[4].wait()
    own_mail.wait()

    def line_step(k, split=False):
        r, m = k // parts + 1, k % parts

        def arrived(direction, has_next, piece):
            later_hop(direction, r - 1, m, piece).wait_recv()

            @pl.when(has_next)
            def _():
                if split:
                    for f in range(ends):
                        end_hop(direction, f).start()
                else:
                    later_hop(direction, r, m, piece).start()

            twin_copy(piece, m, cross).start()

        @pl.when(z - r >= 0)
        def _():
            arrived(0, z + 1 < nb, z - r)

        @pl.when(z + r < nb)
        def _():
            arrived(1, z > 0, z + r)

    def end_step():
        def arrived(direction, piece):
            for f in range(ends):
                end_hop(direction, f).wait_recv()
                if f < swapped:
                    end_twin(piece, f, cross).start()

        @pl.when(z == nb - 1)
        def _():
            arrived(0, 0)

        @pl.when(z == 0)
        def _():
            arrived(1, nb - 1)

    context = page_count * keys.shape[1]
    serve_turns = nb * blocks
    turns = serve_turns + row_chunks
    early = (nb - 2) * parts

    def steps_of_turn(i, final=False):
        spare = 1 if final else 0
        if early % turns == 0:
            for u in range(early // turns - spare):
                line_step(i * (early // turns) + u)
        else:

            def one(k, carry):
                line_step(k)
                return carry

            lax.fori_loop(i * early // turns, (i + 1) * early // turns - spare, one, 0)
        if final:
            line_step(early - 1, split=True)

    position = lax.broadcasted_iota(jnp.int32, (heads, context), 1)

    def serve(d, r, letters, u):
        p = chosen[d * cap + r]
        pages = [pages_ref[i, p] for i in range(page_count)]
        length = lengths_ref[low + p]
        key_block = jnp.concatenate([keys[page] for page in pages], axis=0)
        value_block = jnp.concatenate([values[page] for page in pages], axis=0)
        mine = [letter[u * group : (u + 1) * group] for letter in letters]
        nothing = jnp.zeros((group, HD), jnp.float32)
        wide = jnp.concatenate(
            [
                jnp.concatenate([mine[h] if g == h else nothing for g in range(kvl)], axis=1)
                for h in range(kvl)
            ],
            axis=0,
        ).astype(jnp.bfloat16)
        scores = (
            lax.dot_general(
                wide, key_block, (((1,), (1,)), ((), ())), preferred_element_type=jnp.float32
            )
            * scale
        )
        scores = jnp.where(position < length, scores, -1e30)
        top = jnp.max(scores, axis=1, keepdims=True)
        w = jnp.exp(scores - top)
        den = jnp.sum(w, axis=1, keepdims=True)
        everything = jnp.dot(w.astype(jnp.bfloat16), value_block, preferred_element_type=jnp.float32)
        answers = []
        for h in range(kvl):
            rows = slice(h * group, (h + 1) * group)
            answers.append(everything[rows, h * HD : (h + 1) * HD] / den[rows])
        return answers, top + jnp.log(den)

    peak_square = (step * heads, HD)
    peak_diagonal = lax.broadcasted_iota(jnp.int32, peak_square, 0) == lax.broadcasted_iota(
        jnp.int32, peak_square, 1
    )

    def serve_block(i, carry):
        steps_of_turn(i)
        away = i // blocks
        d = lax.rem(z + away, nb)
        r0 = lax.rem(i, blocks) * step

        @pl.when((lax.rem(i, blocks) == 0) & (away > 0))
        def _():
            mail(nb - away).wait_recv()

        some = pl.ds(pl.multiple_of(r0 * group, step * group), step * group)
        letters = [mail_in[d, h, some].astype(jnp.float32) for h in range(kvl)]
        results = [serve(d, r0 + u, letters, u) for u in range(step)]
        for h in range(kvl):
            served_out[d, h, some] = jnp.concatenate([result[0][h] for result in results], axis=0).astype(
                jnp.bfloat16
            )
        peak_column = jnp.concatenate([result[1] for result in results], axis=0)
        spread_peaks = jnp.where(peak_diagonal, jnp.broadcast_to(peak_column, peak_square), 0.0)
        peaks_out[d, pl.ds(lax.rem(i, blocks), 1)] = jnp.sum(spread_peaks, axis=0, keepdims=True)
        return carry

    lax.fori_loop(0, serve_turns, serve_block, 0)
    own_back = pltpu.make_async_copy(served_out.at[z], returned.at[z], local_sem.at[9])
    own_back.start()
    for d in range(1, nb):
        pl.when(inside(d))(lambda d=d: back(d).start())
    pl.when(z < nb - 2)(lambda: to_hub(nb - 1).start())
    pl.when(z > 1)(lambda: to_hub(0).start())

    features = row_width * mp
    pieces_per_block = row_width // depth
    fine = min(16, per_chunk)

    def row_step(i):
        for d in range(1, mp):
            row_copy(d, i).wait_recv()

        def normalise(j, carry):
            start = pl.multiple_of(i * per_chunk + j * fine, fine)
            part = pl.ds(start, fine)
            power = jnp.zeros((fine, 1), jnp.float32)
            for b in range(mp):
                block = raw[b, part].astype(jnp.float32)
                power = power + jnp.sum(block * block, axis=1, keepdims=True)
            factor = lax.rsqrt(power / features + 1e-06)
            for b in range(mp):
                block = raw[b, part].astype(jnp.float32)
                gain = gain_ref[:, b * row_width : (b + 1) * row_width]
                result = (block * factor * gain).astype(jnp.bfloat16)
                for p in range(pieces_per_block):
                    normed[c, b * pieces_per_block + p, part] = result[:, p * depth : (p + 1) * depth]
            return carry

        lax.fori_loop(0, per_chunk // fine, normalise, 0)
        norm_copy(i).start()

    own_copies[5].wait()
    own_copies[7].wait()
    for i in range(row_chunks):
        steps_of_turn(serve_turns + i, final=i == row_chunks - 1)
        row_step(i)
    for i in range(row_chunks):
        norm_copy(i).wait_recv()
    own_copies[6].wait()

    def multiply(piece, kind, n, fresh=False):
        here = slice(n * chunk, (n + 1) * chunk)
        for side in range(2):
            product = jnp.dot(
                normed[side, piece * ns + kind], weights[piece, kind, n], preferred_element_type=jnp.float32
            )
            if fresh:
                total[side, :, here] = bias_ref[:, columns(c, n)] + product
            else:
                total[side, :, here] += product

    def multiply_own(n):
        own_weights[n].wait()
        swap(n).wait_recv()
        multiply(z, 0, n, fresh=True)
        multiply(z, 1, n)

    def multiply_at(r, n, ended=0):
        def both(piece, direction):
            multiply(piece, cross, n)
            for j in range(cuts - ended):
                twin_copy(piece, n * cuts + j, 1 - cross).wait_recv()
            for f in range(swapped * ended):
                end_twin(piece, f, 1 - cross).wait_recv()
            if ended:
                for f in range(swapped, ends):
                    end_other(direction, f).wait_recv()
            multiply(piece, 1 - cross, n)

        def left():
            both(z - r, 0)

        def right():
            both(z + r, 1)

        pl.when(z - r >= 0)(left)
        pl.when(z + r < nb)(right)

    def near(n):
        multiply_own(n)

        def one(r, carry):
            multiply_at(r, n)
            return carry

        lax.fori_loop(1, nb - 1, one, 0)

    def last(n):
        multiply_at(nb - 1, n, ended=1 if n == chunks - 1 else 0)
        class_part = class_ref[:, columns(c, n)]
        here = slice(n * chunk, (n + 1) * chunk)
        for side in range(2):
            hidden = jnp.maximum(total[side, :, here], 0.0).astype(jnp.bfloat16)
            sums = lax.dot_general(
                class_part, hidden, (((1,), (1,)), ((), ())), preferred_element_type=jnp.float32
            )
            if n == 0:
                partial[side, 0:2] = sums
            else:
                partial[side, 0:2] += sums

    partial[...] = jnp.zeros_like(partial)
    plan = [[] for _ in range(parts + 1)]
    for n in range(chunks):
        plan[n * (parts // 2) // chunks].append(functools.partial(near, n))
    for n in range(chunks):
        when = (n + 1) * cuts + cuts
        plan[when if parts // 2 <= when < parts else parts].append(functools.partial(last, n))
    for m in range(parts):
        if m < parts - 1:
            line_step(early + m)
        else:
            end_step()
        for unit in plan[m]:
            unit()
        if m == parts - dims["late"]:
            for d in range(1, nb):
                peak_back(d).start()
            pl.when(z == nb - 2)(lambda: merge(nb - 1))
            pl.when(z == 1)(lambda: merge(0))
    for unit in plan[parts]:
        unit()

    pairs = [(d, e) for d in range(mp) for e in range(2) if d or e]
    for d, e in pairs:
        sum_copy(d, e).start()

    own_back.wait()
    for d in range(1, nb):
        peak_back(d).wait_recv()

    @pl.when(jnp.logical_not(at_end))
    def _():
        for d in range(1, nb):
            back(d).wait_recv()

    pl.when(at_end)(lambda: merged_copy(nb - 2).wait_recv())
    peaks_in[z] = peaks_out[z]
    rest = peaks_in[...].reshape(nb * 8, HD)
    picked = jnp.zeros((group * wide_slots, HD), jnp.float32)
    for _ in range(3):
        coarse = rest.astype(jnp.bfloat16)
        picked = picked + jnp.dot(row_picker[...], coarse, preferred_element_type=jnp.float32)
        rest = rest - coarse.astype(jnp.float32)
    for h in range(kvl):
        here = lax.broadcasted_iota(jnp.int32, picked.shape, 1) == lane_key[...] + h * group
        peak = jnp.sum(jnp.where(here, picked, 0.0), axis=1, keepdims=True)
        share = 1.0 / (1.0 + jnp.exp(own_scores[:, h : h + 1] - peak))
        answers = returned[:, h].reshape(lines, HD)
        mine = jnp.dot(picker[...], answers, preferred_element_type=jnp.float32)
        merged = merged_in[h].astype(jnp.float32)
        mine = mine + stack([merged[g * slots : (g + 1) * slots] for g in range(group)])
        mine = (mine * share + repeated(value_rows_in, h) * (1.0 - share)).astype(jnp.bfloat16)
        for g in range(group):
            at = (h * group + g) * HD
            attention_ref[:, at : at + HD] = mine[g * wide_slots : g * wide_slots + slots]
    attention_out = pltpu.make_async_copy(attention_ref, attention_hbm, small_sem.at[0])
    attention_out.start()

    logits = partial[c]
    for d, e in pairs:
        sum_copy(d, e).wait_recv()
        logits = logits + logits_in[d * 2 + e]
    odds_ref[...] = (logits[1:2] + class_bias_ref[1]) - (logits[0:1] + class_bias_ref[0])
    odds_out = pltpu.make_async_copy(odds_ref, odds_hbm, small_sem.at[1])
    odds_out.start()

    for d in range(1, nb):
        mail(d).wait_send()
        pl.when(inside(d))(lambda d=d: back(d).wait_send())
        peak_back(d).wait_send()
    pl.when(z < nb - 2)(lambda: to_hub(nb - 1).wait_send())
    pl.when(z > 1)(lambda: to_hub(0).wait_send())
    def drain_hub(end):
        merged_copy(end).wait_send()
        for f in range(swapped, ends):
            end_other(0 if end else 1, f).wait_send()

    pl.when(z == nb - 2)(lambda: drain_hub(nb - 1))
    pl.when(z == 1)(lambda: drain_hub(0))
    for i in range(row_chunks):
        for d in range(1, mp):
            row_copy(d, i).wait_send()
        norm_copy(i).wait_send()
    for d, e in pairs:
        sum_copy(d, e).wait_send()
    for n in range(chunks):
        swap(n).wait_send()

    def drain_first(m, carry):
        @pl.when(z < nb - 1)
        def _():
            first_hop(0, m).wait_send()

        @pl.when(z > 0)
        def _():
            first_hop(1, m).wait_send()

        return carry

    lax.fori_loop(0, parts, drain_first, 0)

    def drain(k, carry, split=False):
        r, m = k // parts + 1, k % parts

        def sent(direction, has_next, piece):
            @pl.when(has_next)
            def _():
                if split:
                    for f in range(ends):
                        end_hop(direction, f).wait_send()
                else:
                    later_hop(direction, r, m, piece).wait_send()

            twin_copy(piece, m, cross).wait_send()

        @pl.when(z - r >= 0)
        def _():
            sent(0, z + 1 < nb, z - r)

        @pl.when(z + r < nb)
        def _():
            sent(1, z > 0, z + r)

        return carry

    lax.fori_loop(0, early - 1, drain, 0)
    drain(early - 1, 0, split=True)
    lax.fori_loop(early, early + parts - 1, drain, 0)

    @pl.when(z == nb - 1)
    def _():
        for f in range(swapped):
            end_twin(0, f, cross).wait_send()

    @pl.when(z == 0)
    def _():
        for f in range(swapped):
            end_twin(nb - 1, f, cross).wait_send()

    attention_out.wait()
    odds_out.wait()


def per_device(
    queries,
    new_keys,
    new_values,
    key_pages,
    value_pages,
    page_table,
    ancestry,
    lengths,
    step_rows,
    norm_gain,
    head_weight,
    head_bias,
    class_weight,
    class_bias,
):
    slot_count, page_count = page_table.shape
    kv_width = key_pages.shape[3]
    kvl = kv_width // HD
    group = queries.shape[2] // kv_width
    nb, ng = lax.axis_size("batch"), lax.axis_size("group")
    mp, ns = lax.axis_size("mp"), lax.axis_size("section")
    assert ng == 2 and ns == 2 and nb >= 4 and queries.shape[0] == 1
    cap = max(2, (2 * slot_count + nb - 1) // nb)
    wide_slots = (slot_count + 15) // 16 * 16

    row_count, row_width = step_rows.shape
    depth, width = head_weight.shape
    half = width // ns
    chunk = min(256, half)
    chunks = half // chunk
    cuts = 2
    parts = chunks * cuts
    ends = max(1, min(4, depth // cuts // 16))
    row_chunks = 4
    dims = dict(
        nb=nb, mp=mp, ns=ns, cap=cap, page_count=page_count, kvl=kvl, group=group, slots=slot_count,
        wide_slots=wide_slots, half=half, chunk=chunk, chunks=chunks, depth=depth, row_chunks=row_chunks,
        cuts=cuts, ends=ends, doubled=min(2, ends - 1), first=2, late=3,
    )
    anywhere = pl.BlockSpec(memory_space=pl.ANY)
    bf16, f32, i32 = jnp.bfloat16, jnp.float32, jnp.int32
    sems = pltpu.SemaphoreType.DMA
    answers = (nb, kvl, cap * group, HD)
    attention, odds = pl.pallas_call(
        functools.partial(fused_kernel, dims),
        out_shape=(
            jax.ShapeDtypeStruct((slot_count, kvl * group * HD), bf16),
            jax.ShapeDtypeStruct((1, row_count), f32),
        ),
        in_specs=[anywhere] * 14,
        out_specs=(anywhere, anywhere),
        scratch_shapes=[
            pltpu.SMEM(ancestry.shape, i32),
            pltpu.SMEM(lengths.shape, i32),
            pltpu.SMEM((page_count, slot_count), i32),
            pltpu.SMEM(class_bias.shape, f32),
            pltpu.VMEM((2, width), bf16),
            pltpu.VMEM((slot_count, kvl * group * HD), bf16),
            pltpu.VMEM((1, row_count), f32),
            pltpu.SMEM((slot_count + 1,), i32),
            pltpu.SMEM((nb * cap,), i32),
            pltpu.VMEM(queries.shape[1:], bf16),
            pltpu.VMEM(new_keys.shape[1:], bf16),
            pltpu.VMEM(new_values.shape[1:], bf16),
            pltpu.VMEM((1, row_width * mp), f32),
            pltpu.VMEM((1, width), f32),
            pltpu.VMEM((group * wide_slots, nb * cap * group), bf16),
            pltpu.VMEM((group * wide_slots, nb * 8), bf16),
            pltpu.VMEM((group * wide_slots, HD), i32),
            pltpu.VMEM((group * wide_slots, HD), f32),
            pltpu.VMEM((nb, 8, HD), f32),
            pltpu.VMEM((nb, 8, HD), f32),
            pltpu.VMEM(answers, bf16),
            pltpu.VMEM(answers, bf16),
            pltpu.VMEM(answers, bf16),
            pltpu.VMEM(answers, bf16),
            pltpu.VMEM(key_pages.shape[1:], bf16),
            pltpu.VMEM(key_pages.shape[1:], bf16),
            pltpu.VMEM((mp, row_count, row_width), bf16),
            pltpu.VMEM((2, nb * ns, row_count, depth), bf16),
            pltpu.VMEM((nb, ns, chunks, depth, chunk), bf16),
            pltpu.VMEM((2, row_count, half), f32),
            pltpu.VMEM((2, 8, row_count), f32),
            pltpu.VMEM((2 * mp, 8, row_count), f32),
            pltpu.SemaphoreType.REGULAR((2,)),
            sems((5,)),
            sems((10,)),
            sems((chunks,)),
            sems((nb,)),
            sems((nb,)),
            sems((nb,)),
            sems((nb,)),
            sems((2, nb, parts)),
            sems((2, nb, parts)),
            sems((nb, parts)),
            sems((nb, parts)),
            sems((chunks,)),
            sems((chunks,)),
            sems((mp, row_chunks)),
            sems((mp, row_chunks)),
            sems((row_chunks,)),
            sems((row_chunks,)),
            sems((2 * mp,)),
            sems((2 * mp,)),
            sems((2, ends)),
            sems((2, ends)),
            sems((ends,)),
            sems((ends,)),
            sems((nb,)),
            sems((nb,)),
            pltpu.VMEM((group * wide_slots, nb * cap * group), bf16),
            pltpu.VMEM(answers, bf16),
            pltpu.VMEM((kvl, group * slot_count, HD), bf16),
            pltpu.VMEM((kvl, group * slot_count, HD), bf16),
            sems((2,)),
            sems((nb,)),
            sems,
            sems,
            sems((ends,)),
            sems((ends,)),
            pltpu.VMEM((chunks, depth, chunk), bf16),
            sems((chunks,)),
        ],
        compiler_params=pltpu.CompilerParams(
            collective_id=0, has_side_effects=True, vmem_limit_bytes=60 * 1024 * 1024
        ),
        name="filter_round",
    )(
        ancestry,
        lengths,
        page_table.T,
        class_bias,
        queries,
        new_keys,
        new_values,
        key_pages,
        value_pages,
        step_rows,
        norm_gain.reshape(1, -1),
        head_weight,
        head_bias.reshape(1, -1),
        class_weight.T,
    )
    return attention.reshape(1, slot_count, -1), odds.reshape(-1)


def solution(mesh):
    placed = (
        P("section", ("group", "batch"), "mp"),
        P("section", ("group", "batch"), "mp"),
        P("section", ("group", "batch"), "mp"),
        P("section", ("group", "batch"), None, "mp"),
        P("section", ("group", "batch"), None, "mp"),
        P(("group", "batch"), None),
        P("group"),
        P("group"),
        P(("group", "batch", "section"), "mp"),
        P(),
        P(("batch", "section"), "mp"),
        P("mp"),
        P("mp", None),
        P(),
    )
    return jax.shard_map(
        per_device,
        mesh=mesh,
        in_specs=placed,
        out_specs=(P("section", ("group", "batch"), "mp"), P(("group", "batch", "section"))),
        check_vma=False,
    )
```

```python
import functools

import jax
import jax.numpy as jnp
from jax import lax
from jax.experimental import pallas as pl
from jax.experimental.pallas import tpu as pltpu
from jax.sharding import PartitionSpec as P

HD = 128
MESH = pl.DeviceIdType.MESH


def fused_kernel(
    dims,
    ancestry_hbm,
    lengths_hbm,
    pages_hbm,
    class_bias_hbm,
    queries_hbm,
    new_keys_hbm,
    new_values_hbm,
    keys_hbm,
    values_hbm,
    rows_hbm,
    gain_hbm,
    weight_hbm,
    bias_hbm,
    class_hbm,
    attention_hbm,
    odds_hbm,
    ancestry_ref,
    lengths_ref,
    pages_ref,
    class_bias_ref,
    class_ref,
    attention_ref,
    odds_ref,
    follow,
    chosen,
    letter_rows,
    key_rows_in,
    value_rows_in,
    gain_ref,
    bias_ref,
    picker,
    row_picker,
    lane_key,
    own_scores,
    peaks_out,
    peaks_in,
    mail_out,
    mail_in,
    served_out,
    returned,
    keys,
    values,
    raw,
    normed,
    weights,
    total,
    partial,
    logits_in,
    relay,
    small_sem,
    local_sem,
    weight_sem,
    mail_send,
    mail_recv,
    back_send,
    back_recv,
    line_send,
    line_recv,
    twin_send,
    twin_recv,
    swap_send,
    swap_recv,
    row_send,
    row_recv,
    norm_send,
    norm_recv,
    sum_send,
    sum_recv,
    end_send,
    end_recv,
    end_twin_send,
    end_twin_recv,
    peak_send,
    peak_recv,
    hub_picker,
    hub_in,
    merged_out,
    merged_in,
    hub_send,
    hub_recv,
    merged_send,
    merged_recv,
    both_send,
    both_recv,
    staged,
    stage_sem,
):
    nb, mp, ns = dims["nb"], dims["mp"], dims["ns"]
    cap, page_count, kvl, group = dims["cap"], dims["page_count"], dims["kvl"], dims["group"]
    half, chunk, chunks, depth = dims["half"], dims["chunk"], dims["chunks"], dims["depth"]
    row_chunks, cuts, first = dims["row_chunks"], dims["cuts"], dims["first"]
    slots, wide_slots = dims["slots"], dims["wide_slots"]
    heads = kvl * group
    sub = depth // cuts
    ends, swapped = dims["ends"], dims["ends"] - dims["doubled"]
    parts = chunks * cuts
    z, y = lax.axis_index("batch"), lax.axis_index("group")
    x, c = lax.axis_index("mp"), lax.axis_index("section")
    other = 1 - c
    twin = 1 - y
    cross = lax.rem(c + y, 2)
    row_count, row_width = rows_hbm.shape
    per_chunk = row_count // row_chunks

    def remote(src, dst, send, recv, device):
        return pltpu.make_async_remote_copy(
            src_ref=src, dst_ref=dst, send_sem=send, recv_sem=recv, device_id=device, device_id_type=MESH
        )

    def columns(owner, n):
        return pl.ds(pl.multiple_of(owner * half + n * chunk, chunk), chunk)

    barrier = pltpu.get_barrier_semaphore()

    def greet(device):
        pl.semaphore_signal(barrier, inc=1, device_id=device, device_id_type=MESH)

    @pl.when(z > 0)
    def _():
        greet({"batch": z - 1})
        greet({"batch": z - 1, "section": other})

    @pl.when(z < nb - 1)
    def _():
        greet({"batch": z + 1})
        greet({"batch": z + 1, "section": other})

    greet({"section": other})
    greet({"group": twin})
    for d in range(1, mp):
        peer = lax.rem(x + d, mp)
        greet({"mp": peer})
        greet({"mp": peer, "section": other})

    own_copies = [
        pltpu.make_async_copy(queries_hbm.at[0], letter_rows, local_sem.at[0]),
        pltpu.make_async_copy(new_keys_hbm.at[0], key_rows_in, local_sem.at[1]),
        pltpu.make_async_copy(new_values_hbm.at[0], value_rows_in, local_sem.at[2]),
        pltpu.make_async_copy(keys_hbm.at[0], keys, local_sem.at[3]),
        pltpu.make_async_copy(values_hbm.at[0], values, local_sem.at[4]),
        pltpu.make_async_copy(gain_hbm, gain_ref, local_sem.at[5]),
        pltpu.make_async_copy(bias_hbm, bias_ref, local_sem.at[6]),
        pltpu.make_async_copy(rows_hbm, raw.at[x], local_sem.at[7]),
    ]
    small_copies = [
        pltpu.make_async_copy(src, dst, small_sem.at[i])
        for i, (src, dst) in enumerate(
            [
                (ancestry_hbm, ancestry_ref),
                (lengths_hbm, lengths_ref),
                (pages_hbm, pages_ref),
                (class_bias_hbm, class_bias_ref),
                (class_hbm, class_ref),
            ]
        )
    ]
    staging = [
        pltpu.make_async_copy(weight_hbm.at[:, columns(cross, n)], staged.at[n], stage_sem.at[n])
        for n in range(chunks)
    ]
    for copy in staging + small_copies + own_copies:
        copy.start()

    neighbours = jnp.where(z > 0, 1, 0) + jnp.where(z < nb - 1, 1, 0)
    pl.semaphore_wait(barrier, 2 + 2 * (mp - 1) + 2 * neighbours)

    def mail(d):
        target = lax.rem(z + d, nb)
        return remote(mail_out.at[target], mail_in.at[z], mail_send.at[d], mail_recv.at[d], {"batch": target})

    def back(d):
        target = lax.rem(z + d, nb)
        return remote(
            served_out.at[target], returned.at[z], back_send.at[d], back_recv.at[d], {"batch": target}
        )

    def inside(d):
        target = lax.rem(z + d, nb)
        return (target > 0) & (target < nb - 1)

    def to_hub(end):
        hub = nb - 2 if end else 1
        return remote(
            served_out.at[end],
            hub_in.at[z],
            hub_send.at[1 if end else 0],
            hub_recv.at[z],
            {"batch": hub},
        )

    def from_hub_source(origin):
        return remote(
            served_out.at[0], hub_in.at[origin], hub_send.at[0], hub_recv.at[origin], {"batch": z - 1}
        )

    def merged_copy(end):
        return remote(merged_out, merged_in, merged_send, merged_recv, {"batch": end})

    def merge(end):
        hub = nb - 2 if end else 1
        for f in range(swapped, ends):
            end_other(0 if end else 1, f).start()
        for origin in range(nb):
            if origin not in (end, hub):
                from_hub_source(origin).wait_recv()
        hub_in[end] = jnp.zeros(hub_in.shape[1:], hub_in.dtype)
        hub_in[hub] = served_out[end]
        for h in range(kvl):
            answers = hub_in[:, h].reshape(nb * cap * group, HD)
            mine = jnp.dot(hub_picker[...], answers, preferred_element_type=jnp.float32)
            merged_out[h] = jnp.concatenate(
                [mine[g * wide_slots : g * wide_slots + slots] for g in range(group)], axis=0
            ).astype(jnp.bfloat16)
        merged_copy(end).start()

    def peak_back(d):
        target = lax.rem(z + d, nb)
        return remote(
            peaks_out.at[target], peaks_in.at[z], peak_send.at[d], peak_recv.at[d], {"batch": target}
        )

    def row_copy(d, i):
        target = lax.rem(x + d, mp)
        part = pl.ds(i * per_chunk, per_chunk)
        return remote(
            rows_hbm.at[part], raw.at[x, part], row_send.at[d, i], row_recv.at[d, i], {"mp": target}
        )

    def swap(n):
        return remote(
            weight_hbm.at[:, columns(other, n)],
            weights.at[z, c, n],
            swap_send.at[n],
            swap_recv.at[n],
            {"section": other},
        )

    def piece_rows(m):
        return pl.ds(pl.multiple_of((m % cuts) * sub, sub), sub)

    def first_hop(direction, m):
        return remote(
            staged.at[m // cuts, piece_rows(m)],
            weights.at[z, c, m // cuts, piece_rows(m)],
            line_send.at[direction, 0, m],
            line_recv.at[direction, 0, m],
            {"batch": z + (1 if direction == 0 else -1), "section": cross},
        )

    def later_hop(direction, hop, m, piece):
        place = weights.at[piece, cross, m // cuts, piece_rows(m)]
        return remote(
            place,
            place,
            line_send.at[direction, hop, m],
            line_recv.at[direction, hop, m],
            {"batch": z + (1 if direction == 0 else -1)},
        )

    def twin_copy(piece, m, kind):
        place = weights.at[piece, kind, m // cuts, piece_rows(m)]
        return remote(place, place, twin_send.at[piece, m], twin_recv.at[piece, m], {"group": twin})

    def end_place(piece, kind, f):
        return weights.at[piece, kind, chunks - 1, pl.ds(depth - sub + f * (sub // ends), sub // ends)]

    def end_hop(direction, f):
        place = end_place(0 if direction == 0 else nb - 1, cross, f)
        return remote(
            place,
            place,
            end_send.at[direction, f],
            end_recv.at[direction, f],
            {"batch": z + (1 if direction == 0 else -1)},
        )

    def end_twin(piece, f, kind):
        place = end_place(piece, kind, f)
        return remote(place, place, end_twin_send.at[f], end_twin_recv.at[f], {"group": twin})

    def end_other(direction, f):
        place = end_place(0 if direction == 0 else nb - 1, 1 - cross, f)
        return remote(
            place, place, both_send.at[f], both_recv.at[f], {"batch": z + (1 if direction == 0 else -1)}
        )

    def norm_copy(i):
        part = pl.ds(i * per_chunk, per_chunk)
        return remote(
            normed.at[c, :, part],
            normed.at[c, :, part],
            norm_send.at[i],
            norm_recv.at[i],
            {"section": other},
        )

    def sum_copy(d, e):
        peer, side = lax.rem(x + d, mp), lax.rem(c + e, 2)
        return remote(
            partial.at[side],
            logits_in.at[d * 2 + e],
            sum_send.at[d * 2 + e],
            sum_recv.at[d * 2 + e],
            {"mp": peer, "section": side},
        )

    own_weights = [
        pltpu.make_async_copy(weight_hbm.at[:, columns(c, n)], weights.at[z, c, n], weight_sem.at[n])
        for n in range(chunks)
    ]

    def send_first(m):
        @pl.when(z < nb - 1)
        def _():
            first_hop(0, m).start()

        @pl.when(z > 0)
        def _():
            first_hop(1, m).start()

    for copy in staging[: (first + cuts - 1) // cuts]:
        copy.wait()
    for m in range(first):
        send_first(m)
    for i in range(row_chunks):
        for d in range(1, mp):
            row_copy(d, i).start()

    def pass_on(side, has_before, has_after, after):
        @pl.when(has_before)
        def _():
            pl.semaphore_wait(relay.at[side], 1)

        @pl.when(has_after)
        def _():
            pl.semaphore_signal(
                relay.at[side], inc=1, device_id={"batch": after}, device_id_type=MESH
            )

    def pass_right():
        pass_on(0, z > 0, z < nb - 1, z + 1)

    def pass_left():
        pass_on(1, z < nb - 1, z > 0, z - 1)

    @pl.when(z < nb // 2)
    def _():
        pass_right()
        pass_left()

    @pl.when(z >= nb // 2)
    def _():
        pass_left()
        pass_right()

    for copy in small_copies:
        copy.wait()
    lane = lax.broadcasted_iota(jnp.int32, (1, group * wide_slots), 1)
    slot_of_lane = lane % wide_slots


    def slot_codes(owner):
        ancestor = jnp.full((1, group * wide_slots), -1, jnp.int32)
        for p in range(slots):
            ancestor = jnp.where(slot_of_lane == p, ancestry_ref[owner * slots + p], ancestor)
        source = jnp.zeros_like(ancestor)
        for d in range(1, nb):
            source = source + jnp.where(ancestor >= d * slots, 1, 0)
        source = jnp.where(ancestor >= 0, source, -1)
        spread = jnp.broadcast_to(source, (wide_slots, group * wide_slots))
        row_at = lax.broadcasted_iota(jnp.int32, spread.shape, 0)
        lane_at = lax.broadcasted_iota(jnp.int32, spread.shape, 1)
        source_column = jnp.sum(jnp.where(row_at == lane_at, spread, 0), axis=1, keepdims=True)
        before = (source_column == spread) & (row_at < lane_at % wide_slots)
        rank = jnp.sum(jnp.where(before, 1, 0), axis=0, keepdims=True)
        code = jnp.where(source >= 0, (source * cap + rank) * group + lane // wide_slots, -1)
        return source, rank, code

    source, rank, code = slot_codes(z)
    lines = nb * cap * group
    wanted = lax.broadcasted_iota(jnp.int32, (lines, group * wide_slots), 0) == code
    requests = jnp.where(wanted, 1.0, 0.0).astype(jnp.bfloat16)

    own_copies[0].wait()

    def stack(blocks_of):
        filler = jnp.zeros((wide_slots - slots, HD), jnp.float32)
        tall = [part for g in blocks_of for part in ((g, filler) if wide_slots > slots else (g,))]
        return jnp.concatenate(tall, axis=0)

    def query_stack(h):
        start = h * group
        return stack(
            [letter_rows[:, (start + g) * HD : (start + g + 1) * HD].astype(jnp.float32) for g in range(group)]
        )

    def repeated(ref, h):
        return stack([ref[:, h * HD : (h + 1) * HD].astype(jnp.float32)] * group)

    for h in range(kvl):
        tall = query_stack(h).astype(jnp.bfloat16)
        packed = jnp.dot(requests, tall, preferred_element_type=jnp.float32).astype(jnp.bfloat16)
        for s in range(nb):
            mail_out[s, h] = packed[s * cap * group : (s + 1) * cap * group]
    for d in range(1, nb):
        mail(d).start()
    own_mail = pltpu.make_async_copy(mail_out.at[z], mail_in.at[z], local_sem.at[8])
    own_mail.start()
    for copy in staging[(first + cuts - 1) // cuts :]:
        copy.wait()
    for m in range(first, parts):
        send_first(m)
    for n in range(chunks):
        swap(n).start()
    for copy in own_weights:
        copy.start()

    squares = (group * wide_slots, group * wide_slots)
    diagonal = lax.broadcasted_iota(jnp.int32, squares, 0) == lax.broadcasted_iota(jnp.int32, squares, 1)

    def as_column(row):
        return jnp.sum(jnp.where(diagonal, jnp.broadcast_to(row, squares), 0), axis=1, keepdims=True)

    code_column = as_column(code)
    found = lax.broadcasted_iota(jnp.int32, (group * wide_slots, lines), 1) == code_column
    picker[...] = jnp.where(found, 1.0, 0.0).astype(jnp.bfloat16)

    step = 4 if cap % 4 == 0 else cap
    blocks = cap // step
    scale = 1.0 / HD**0.5
    turn = jnp.zeros_like(rank)
    for b in range(1, blocks):
        turn = turn + jnp.where(rank >= b * step, 1, 0)

    end_code = as_column(slot_codes(jnp.where(z == nb - 2, nb - 1, 0))[2])
    found_end = lax.broadcasted_iota(jnp.int32, hub_picker.shape, 1) == end_code
    hub_picker[...] = jnp.where(found_end, 1.0, 0.0).astype(jnp.bfloat16)
    at_end = (z == 0) | (z == nb - 1)

    @pl.when(at_end)
    def _():
        returned[...] = jnp.zeros_like(returned)

    @pl.when(jnp.logical_not(at_end))
    def _():
        merged_in[...] = jnp.zeros_like(merged_in)

    row_column = as_column(jnp.where(source >= 0, source * 8 + turn, -1))
    found_row = lax.broadcasted_iota(jnp.int32, row_picker.shape, 1) == row_column
    row_picker[...] = jnp.where(found_row, 1.0, 0.0).astype(jnp.bfloat16)
    key_column = as_column((rank - turn * step) * heads + lane // wide_slots)
    lane_key[...] = jnp.broadcast_to(key_column, lane_key.shape)
    own_copies[1].wait()
    own_copies[2].wait()
    head_lane = lax.broadcasted_iota(jnp.int32, own_scores.shape, 1)
    mine_scores = jnp.zeros(own_scores.shape, jnp.float32)
    for h in range(kvl):
        products = query_stack(h) * repeated(key_rows_in, h)
        one_head = jnp.sum(products, axis=1, keepdims=True) * scale
        mine_scores = jnp.where(head_lane == h, one_head, mine_scores)
    own_scores[...] = mine_scores
    peaks_out[...] = jnp.zeros_like(peaks_out)

    low = z * slots

    def list_served(d, carry):
        upcoming = jnp.int32(slots)
        follow[slots] = upcoming
        for p in reversed(range(slots)):
            a = ancestry_ref[d * slots + p]
            upcoming = jnp.where((a >= low) & (a < low + slots), p, upcoming)
            follow[p] = upcoming
        at = follow[0]
        for r in range(cap):
            chosen[d * cap + r] = jnp.minimum(at, slots - 1)
            at = follow[jnp.minimum(at + 1, slots)]
        return carry

    lax.fori_loop(0, nb, list_served, 0)

    own_copies[3].wait()
    own_copies[4].wait()
    own_mail.wait()

    def line_step(k, split=False):
        r, m = k // parts + 1, k % parts

        def arrived(direction, has_next, piece):
            later_hop(direction, r - 1, m, piece).wait_recv()

            @pl.when(has_next)
            def _():
                if split:
                    for f in range(ends):
                        end_hop(direction, f).start()
                else:
                    later_hop(direction, r, m, piece).start()

            twin_copy(piece, m, cross).start()

        @pl.when(z - r >= 0)
        def _():
            arrived(0, z + 1 < nb, z - r)

        @pl.when(z + r < nb)
        def _():
            arrived(1, z > 0, z + r)

    def end_step():
        def arrived(direction, piece):
            for f in range(ends):
                end_hop(direction, f).wait_recv()
                if f < swapped:
                    end_twin(piece, f, cross).start()

        @pl.when(z == nb - 1)
        def _():
            arrived(0, 0)

        @pl.when(z == 0)
        def _():
            arrived(1, nb - 1)

    context = page_count * keys.shape[1]
    serve_turns = nb * blocks
    turns = serve_turns + row_chunks
    early = (nb - 2) * parts

    def steps_of_turn(i, final=False):
        spare = 1 if final else 0
        if early % turns == 0:
            for u in range(early // turns - spare):
                line_step(i * (early // turns) + u)
        else:

            def one(k, carry):
                line_step(k)
                return carry

            lax.fori_loop(i * early // turns, (i + 1) * early // turns - spare, one, 0)
        if final:
            line_step(early - 1, split=True)

    position = lax.broadcasted_iota(jnp.int32, (heads, context), 1)

    def serve(d, r, letters, u):
        p = chosen[d * cap + r]
        pages = [pages_ref[i, p] for i in range(page_count)]
        length = lengths_ref[low + p]
        key_block = jnp.concatenate([keys[page] for page in pages], axis=0)
        value_block = jnp.concatenate([values[page] for page in pages], axis=0)
        mine = [letter[u * group : (u + 1) * group] for letter in letters]
        nothing = jnp.zeros((group, HD), jnp.float32)
        wide = jnp.concatenate(
            [
                jnp.concatenate([mine[h] if g == h else nothing for g in range(kvl)], axis=1)
                for h in range(kvl)
            ],
            axis=0,
        ).astype(jnp.bfloat16)
        scores = (
            lax.dot_general(
                wide, key_block, (((1,), (1,)), ((), ())), preferred_element_type=jnp.float32
            )
            * scale
        )
        scores = jnp.where(position < length, scores, -1e30)
        top = jnp.max(scores, axis=1, keepdims=True)
        w = jnp.exp(scores - top)
        den = jnp.sum(w, axis=1, keepdims=True)
        everything = jnp.dot(w.astype(jnp.bfloat16), value_block, preferred_element_type=jnp.float32)
        answers = []
        for h in range(kvl):
            rows = slice(h * group, (h + 1) * group)
            answers.append(everything[rows, h * HD : (h + 1) * HD] / den[rows])
        return answers, top + jnp.log(den)

    peak_square = (step * heads, HD)
    peak_diagonal = lax.broadcasted_iota(jnp.int32, peak_square, 0) == lax.broadcasted_iota(
        jnp.int32, peak_square, 1
    )

    def serve_block(i, carry):
        steps_of_turn(i)
        away = i // blocks
        d = lax.rem(z + away, nb)
        r0 = lax.rem(i, blocks) * step

        @pl.when((lax.rem(i, blocks) == 0) & (away > 0))
        def _():
            mail(nb - away).wait_recv()

        some = pl.ds(pl.multiple_of(r0 * group, step * group), step * group)
        letters = [mail_in[d, h, some].astype(jnp.float32) for h in range(kvl)]
        results = [serve(d, r0 + u, letters, u) for u in range(step)]
        for h in range(kvl):
            served_out[d, h, some] = jnp.concatenate([result[0][h] for result in results], axis=0).astype(
                jnp.bfloat16
            )
        peak_column = jnp.concatenate([result[1] for result in results], axis=0)
        spread_peaks = jnp.where(peak_diagonal, jnp.broadcast_to(peak_column, peak_square), 0.0)
        peaks_out[d, pl.ds(lax.rem(i, blocks), 1)] = jnp.sum(spread_peaks, axis=0, keepdims=True)
        return carry

    lax.fori_loop(0, serve_turns, serve_block, 0)
    own_back = pltpu.make_async_copy(served_out.at[z], returned.at[z], local_sem.at[9])
    own_back.start()
    for d in range(1, nb):
        pl.when(inside(d))(lambda d=d: back(d).start())
    pl.when(z < nb - 2)(lambda: to_hub(nb - 1).start())
    pl.when(z > 1)(lambda: to_hub(0).start())

    features = row_width * mp
    pieces_per_block = row_width // depth
    fine = min(16, per_chunk)

    def row_step(i):
        for d in range(1, mp):
            row_copy(d, i).wait_recv()

        def normalise(j, carry):
            start = pl.multiple_of(i * per_chunk + j * fine, fine)
            part = pl.ds(start, fine)
            power = jnp.zeros((fine, 1), jnp.float32)
            for b in range(mp):
                block = raw[b, part].astype(jnp.float32)
                power = power + jnp.sum(block * block, axis=1, keepdims=True)
            factor = lax.rsqrt(power / features + 1e-06)
            for b in range(mp):
                block = raw[b, part].astype(jnp.float32)
                gain = gain_ref[:, b * row_width : (b + 1) * row_width]
                result = (block * factor * gain).astype(jnp.bfloat16)
                for p in range(pieces_per_block):
                    normed[c, b * pieces_per_block + p, part] = result[:, p * depth : (p + 1) * depth]
            return carry

        lax.fori_loop(0, per_chunk // fine, normalise, 0)
        norm_copy(i).start()

    own_copies[5].wait()
    own_copies[7].wait()
    for i in range(row_chunks):
        steps_of_turn(serve_turns + i, final=i == row_chunks - 1)
        row_step(i)
    for i in range(row_chunks):
        norm_copy(i).wait_recv()
    own_copies[6].wait()

    def multiply(piece, kind, n, fresh=False):
        here = slice(n * chunk, (n + 1) * chunk)
        for side in range(2):
            product = jnp.dot(
                normed[side, piece * ns + kind], weights[piece, kind, n], preferred_element_type=jnp.float32
            )
            if fresh:
                total[side, :, here] = bias_ref[:, columns(c, n)] + product
            else:
                total[side, :, here] += product

    def multiply_own(n):
        own_weights[n].wait()
        swap(n).wait_recv()
        multiply(z, 0, n, fresh=True)
        multiply(z, 1, n)

    def multiply_at(r, n, ended=0):
        def both(piece, direction):
            multiply(piece, cross, n)
            for j in range(cuts - ended):
                twin_copy(piece, n * cuts + j, 1 - cross).wait_recv()
            for f in range(swapped * ended):
                end_twin(piece, f, 1 - cross).wait_recv()
            if ended:
                for f in range(swapped, ends):
                    end_other(direction, f).wait_recv()
            multiply(piece, 1 - cross, n)

        def left():
            both(z - r, 0)

        def right():
            both(z + r, 1)

        pl.when(z - r >= 0)(left)
        pl.when(z + r < nb)(right)

    def near(n):
        multiply_own(n)

        def one(r, carry):
            multiply_at(r, n)
            return carry

        lax.fori_loop(1, nb - 1, one, 0)

    def last(n):
        multiply_at(nb - 1, n, ended=1 if n == chunks - 1 else 0)
        class_part = class_ref[:, columns(c, n)]
        here = slice(n * chunk, (n + 1) * chunk)
        for side in range(2):
            hidden = jnp.maximum(total[side, :, here], 0.0).astype(jnp.bfloat16)
            sums = lax.dot_general(
                class_part, hidden, (((1,), (1,)), ((), ())), preferred_element_type=jnp.float32
            )
            if n == 0:
                partial[side, 0:2] = sums
            else:
                partial[side, 0:2] += sums

    partial[...] = jnp.zeros_like(partial)
    plan = [[] for _ in range(parts + 1)]
    for n in range(chunks):
        plan[n * (parts // 2) // chunks].append(functools.partial(near, n))
    for n in range(chunks):
        when = (n + 1) * cuts + cuts
        plan[when if parts // 2 <= when < parts else parts].append(functools.partial(last, n))
    for m in range(parts):
        if m < parts - 1:
            line_step(early + m)
        else:
            end_step()
        for unit in plan[m]:
            unit()
        if m == parts - dims["late"]:
            for d in range(1, nb):
                peak_back(d).start()
            pl.when(z == nb - 2)(lambda: merge(nb - 1))
            pl.when(z == 1)(lambda: merge(0))
    for unit in plan[parts]:
        unit()

    pairs = [(d, e) for d in range(mp) for e in range(2) if d or e]
    for d, e in pairs:
        sum_copy(d, e).start()

    own_back.wait()
    for d in range(1, nb):
        peak_back(d).wait_recv()

    @pl.when(jnp.logical_not(at_end))
    def _():
        for d in range(1, nb):
            back(d).wait_recv()

    pl.when(at_end)(lambda: merged_copy(nb - 2).wait_recv())
    peaks_in[z] = peaks_out[z]
    rest = peaks_in[...].reshape(nb * 8, HD)
    picked = jnp.zeros((group * wide_slots, HD), jnp.float32)
    for _ in range(3):
        coarse = rest.astype(jnp.bfloat16)
        picked = picked + jnp.dot(row_picker[...], coarse, preferred_element_type=jnp.float32)
        rest = rest - coarse.astype(jnp.float32)
    for h in range(kvl):
        here = lax.broadcasted_iota(jnp.int32, picked.shape, 1) == lane_key[...] + h * group
        peak = jnp.sum(jnp.where(here, picked, 0.0), axis=1, keepdims=True)
        share = 1.0 / (1.0 + jnp.exp(own_scores[:, h : h + 1] - peak))
        answers = returned[:, h].reshape(lines, HD)
        mine = jnp.dot(picker[...], answers, preferred_element_type=jnp.float32)
        merged = merged_in[h].astype(jnp.float32)
        mine = mine + stack([merged[g * slots : (g + 1) * slots] for g in range(group)])
        mine = (mine * share + repeated(value_rows_in, h) * (1.0 - share)).astype(jnp.bfloat16)
        for g in range(group):
            at = (h * group + g) * HD
            attention_ref[:, at : at + HD] = mine[g * wide_slots : g * wide_slots + slots]
    attention_out = pltpu.make_async_copy(attention_ref, attention_hbm, small_sem.at[0])
    attention_out.start()

    logits = partial[c]
    for d, e in pairs:
        sum_copy(d, e).wait_recv()
        logits = logits + logits_in[d * 2 + e]
    odds_ref[...] = (logits[1:2] + class_bias_ref[1]) - (logits[0:1] + class_bias_ref[0])
    odds_out = pltpu.make_async_copy(odds_ref, odds_hbm, small_sem.at[1])
    odds_out.start()

    for d in range(1, nb):
        mail(d).wait_send()
        pl.when(inside(d))(lambda d=d: back(d).wait_send())
        peak_back(d).wait_send()
    pl.when(z < nb - 2)(lambda: to_hub(nb - 1).wait_send())
    pl.when(z > 1)(lambda: to_hub(0).wait_send())
    def drain_hub(end):
        merged_copy(end).wait_send()
        for f in range(swapped, ends):
            end_other(0 if end else 1, f).wait_send()

    pl.when(z == nb - 2)(lambda: drain_hub(nb - 1))
    pl.when(z == 1)(lambda: drain_hub(0))
    for i in range(row_chunks):
        for d in range(1, mp):
            row_copy(d, i).wait_send()
        norm_copy(i).wait_send()
    for d, e in pairs:
        sum_copy(d, e).wait_send()
    for n in range(chunks):
        swap(n).wait_send()

    def drain_first(m, carry):
        @pl.when(z < nb - 1)
        def _():
            first_hop(0, m).wait_send()

        @pl.when(z > 0)
        def _():
            first_hop(1, m).wait_send()

        return carry

    lax.fori_loop(0, parts, drain_first, 0)

    def drain(k, carry, split=False):
        r, m = k // parts + 1, k % parts

        def sent(direction, has_next, piece):
            @pl.when(has_next)
            def _():
                if split:
                    for f in range(ends):
                        end_hop(direction, f).wait_send()
                else:
                    later_hop(direction, r, m, piece).wait_send()

            twin_copy(piece, m, cross).wait_send()

        @pl.when(z - r >= 0)
        def _():
            sent(0, z + 1 < nb, z - r)

        @pl.when(z + r < nb)
        def _():
            sent(1, z > 0, z + r)

        return carry

    lax.fori_loop(0, early - 1, drain, 0)
    drain(early - 1, 0, split=True)
    lax.fori_loop(early, early + parts - 1, drain, 0)

    @pl.when(z == nb - 1)
    def _():
        for f in range(swapped):
            end_twin(0, f, cross).wait_send()

    @pl.when(z == 0)
    def _():
        for f in range(swapped):
            end_twin(nb - 1, f, cross).wait_send()

    attention_out.wait()
    odds_out.wait()


def per_device(
    queries,
    new_keys,
    new_values,
    key_pages,
    value_pages,
    page_table,
    ancestry,
    lengths,
    step_rows,
    norm_gain,
    head_weight,
    head_bias,
    class_weight,
    class_bias,
):
    slot_count, page_count = page_table.shape
    kv_width = key_pages.shape[3]
    kvl = kv_width // HD
    group = queries.shape[2] // kv_width
    nb, ng = lax.axis_size("batch"), lax.axis_size("group")
    mp, ns = lax.axis_size("mp"), lax.axis_size("section")
    assert ng == 2 and ns == 2 and nb >= 4 and queries.shape[0] == 1
    cap = max(2, (2 * slot_count + nb - 1) // nb)
    wide_slots = (slot_count + 15) // 16 * 16

    row_count, row_width = step_rows.shape
    depth, width = head_weight.shape
    half = width // ns
    chunk = min(256, half)
    chunks = half // chunk
    cuts = 2
    parts = chunks * cuts
    ends = max(1, min(4, depth // cuts // 16))
    row_chunks = 4
    dims = dict(
        nb=nb, mp=mp, ns=ns, cap=cap, page_count=page_count, kvl=kvl, group=group, slots=slot_count,
        wide_slots=wide_slots, half=half, chunk=chunk, chunks=chunks, depth=depth, row_chunks=row_chunks,
        cuts=cuts, ends=ends, doubled=min(2, ends - 1), first=2, late=4,
    )
    anywhere = pl.BlockSpec(memory_space=pl.ANY)
    bf16, f32, i32 = jnp.bfloat16, jnp.float32, jnp.int32
    sems = pltpu.SemaphoreType.DMA
    answers = (nb, kvl, cap * group, HD)
    attention, odds = pl.pallas_call(
        functools.partial(fused_kernel, dims),
        out_shape=(
            jax.ShapeDtypeStruct((slot_count, kvl * group * HD), bf16),
            jax.ShapeDtypeStruct((1, row_count), f32),
        ),
        in_specs=[anywhere] * 14,
        out_specs=(anywhere, anywhere),
        scratch_shapes=[
            pltpu.SMEM(ancestry.shape, i32),
            pltpu.SMEM(lengths.shape, i32),
            pltpu.SMEM((page_count, slot_count), i32),
            pltpu.SMEM(class_bias.shape, f32),
            pltpu.VMEM((2, width), bf16),
            pltpu.VMEM((slot_count, kvl * group * HD), bf16),
            pltpu.VMEM((1, row_count), f32),
            pltpu.SMEM((slot_count + 1,), i32),
            pltpu.SMEM((nb * cap,), i32),
            pltpu.VMEM(queries.shape[1:], bf16),
            pltpu.VMEM(new_keys.shape[1:], bf16),
            pltpu.VMEM(new_values.shape[1:], bf16),
            pltpu.VMEM((1, row_width * mp), f32),
            pltpu.VMEM((1, width), f32),
            pltpu.VMEM((group * wide_slots, nb * cap * group), bf16),
            pltpu.VMEM((group * wide_slots, nb * 8), bf16),
            pltpu.VMEM((group * wide_slots, HD), i32),
            pltpu.VMEM((group * wide_slots, HD), f32),
            pltpu.VMEM((nb, 8, HD), f32),
            pltpu.VMEM((nb, 8, HD), f32),
            pltpu.VMEM(answers, bf16),
            pltpu.VMEM(answers, bf16),
            pltpu.VMEM(answers, bf16),
            pltpu.VMEM(answers, bf16),
            pltpu.VMEM(key_pages.shape[1:], bf16),
            pltpu.VMEM(key_pages.shape[1:], bf16),
            pltpu.VMEM((mp, row_count, row_width), bf16),
            pltpu.VMEM((2, nb * ns, row_count, depth), bf16),
            pltpu.VMEM((nb, ns, chunks, depth, chunk), bf16),
            pltpu.VMEM((2, row_count, half), f32),
            pltpu.VMEM((2, 8, row_count), f32),
            pltpu.VMEM((2 * mp, 8, row_count), f32),
            pltpu.SemaphoreType.REGULAR((2,)),
            sems((5,)),
            sems((10,)),
            sems((chunks,)),
            sems((nb,)),
            sems((nb,)),
            sems((nb,)),
            sems((nb,)),
            sems((2, nb, parts)),
            sems((2, nb, parts)),
            sems((nb, parts)),
            sems((nb, parts)),
            sems((chunks,)),
            sems((chunks,)),
            sems((mp, row_chunks)),
            sems((mp, row_chunks)),
            sems((row_chunks,)),
            sems((row_chunks,)),
            sems((2 * mp,)),
            sems((2 * mp,)),
            sems((2, ends)),
            sems((2, ends)),
            sems((ends,)),
            sems((ends,)),
            sems((nb,)),
            sems((nb,)),
            pltpu.VMEM((group * wide_slots, nb * cap * group), bf16),
            pltpu.VMEM(answers, bf16),
            pltpu.VMEM((kvl, group * slot_count, HD), bf16),
            pltpu.VMEM((kvl, group * slot_count, HD), bf16),
            sems((2,)),
            sems((nb,)),
            sems,
            sems,
            sems((ends,)),
            sems((ends,)),
            pltpu.VMEM((chunks, depth, chunk), bf16),
            sems((chunks,)),
        ],
        compiler_params=pltpu.CompilerParams(
            collective_id=0, has_side_effects=True, vmem_limit_bytes=60 * 1024 * 1024
        ),
        name="filter_round",
    )(
        ancestry,
        lengths,
        page_table.T,
        class_bias,
        queries,
        new_keys,
        new_values,
        key_pages,
        value_pages,
        step_rows,
        norm_gain.reshape(1, -1),
        head_weight,
        head_bias.reshape(1, -1),
        class_weight.T,
    )
    return attention.reshape(1, slot_count, -1), odds.reshape(-1)


def solution(mesh):
    placed = (
        P("section", ("group", "batch"), "mp"),
        P("section", ("group", "batch"), "mp"),
        P("section", ("group", "batch"), "mp"),
        P("section", ("group", "batch"), None, "mp"),
        P("section", ("group", "batch"), None, "mp"),
        P(("group", "batch"), None),
        P("group"),
        P("group"),
        P(("group", "batch", "section"), "mp"),
        P(),
        P(("batch", "section"), "mp"),
        P("mp"),
        P("mp", None),
        P(),
    )
    return jax.shard_map(
        per_device,
        mesh=mesh,
        in_specs=placed,
        out_specs=(P("section", ("group", "batch"), "mp"), P(("group", "batch", "section"))),
        check_vma=False,
    )
```
